32 devices in a mesh: dp: 2 (over x), ctx: 4 (over z), tp: 4 (over y, core).
Axes of the slice: x: 2, y: 2, z: 4, core: 2. Of those that a mesh axis runs over, the one named last changes fastest.
Arguments:
- tokens: bfloat16 [6144, 2048], P(('dp', 'ctx')), may hold values from -6 to 6
- attn_gain: bfloat16 [2048], replicated, may hold values from 0.5 to 1.5
- query_weight: bfloat16 [2048, 2048], P(('dp', 'ctx'), 'tp'), may hold values from -0.125 to 0.125
- key_weight: bfloat16 [2048, 2048], P(('dp', 'ctx'), 'tp'), may hold values from -0.125 to 0.125
- value_weight: bfloat16 [2048, 2048], P(('dp', 'ctx'), 'tp'), may hold values from -0.125 to 0.125
- out_weight: bfloat16 [2048, 2048], P(('dp', 'ctx'), 'tp'), may hold values from -1 to 1
- ffn_gain: bfloat16 [2048], replicated, may hold values from 0.5 to 1.5
- gate_weight: bfloat16 [2048, 8192], P(('dp', 'ctx'), 'tp'), may hold values from -0.125 to 0.125
- up_weight: bfloat16 [2048, 8192], P(('dp', 'ctx'), 'tp'), may hold values from -0.125 to 0.125
- down_weight: bfloat16 [2048, 8192], P(('dp', 'ctx'), 'tp'), may hold values from -0.0625 to 0.0625
- seq_ids: int32 [2, 3072], P('dp'), may hold values from 0 to 8, as said below
- positions: int32 [2, 3072], P('dp'), may hold values from 0 to 1279, as said below
- out_grad: bfloat16 [6144, 2048], P(('dp', 'ctx')), may hold values from -6 to 6
Outputs:
- block_out: bfloat16 [6144, 2048], P(('dp', 'ctx'), 'tp')
- in_grad: bfloat16 [6144, 2048], P(('dp', 'ctx'), 'tp')
- attn_gain_grad: float32 [2048], P(('dp', 'ctx'))
- query_grad: float32 [2048, 2048], P(('dp', 'ctx'), 'tp')
- key_grad: float32 [2048, 2048], P(('dp', 'ctx'), 'tp')
- value_grad: float32 [2048, 2048], P(('dp', 'ctx'), 'tp')
- out_weight_grad: float32 [2048, 2048], P(('dp', 'ctx'), 'tp')
- ffn_gain_grad: float32 [2048], P(('dp', 'ctx'))
- gate_grad: float32 [2048, 8192], P(('dp', 'ctx'), 'tp')
- up_grad: float32 [2048, 8192], P(('dp', 'ctx'), 'tp')
- down_grad: float32 [2048, 8192], P(('dp', 'ctx'), 'tp')
The draws below stay inside these ranges and needn't reach their ends.
Inputs may be any that keep to these rules, and one draw needn't show every extreme that they name: `seq_ids`: A group's slots form aligned blocks of 256; each block is one piece of the prompt (value 0) or one whole continuation (its number); every continuation has one block, and each aligned block of 768 slots holds exactly one prompt piece. A prompt piece b holds positions b * 256 to b * 256 + 255 in order, each piece once in a group; a continuation's block holds 1024 to 1279 in order.
All inputs are finite; a program needn't handle non-finite values.
Results may differ from the reference program's by a relative error of at most 0.024.
Values may be sent and summed in bfloat16 or wider, within the bound.
No kernel may reach another device: no remote copies, remote signals or barrier semaphores. Data moves between devices by JAX's collectives and lax.ppermute only.
A program may use at most 320 MiB of HBM per device.

```python
import jax
import jax.numpy as jnp
from jax import lax

D = 2048
HEADS = 32
HEAD_DIM = 64
FF = 8192
CLEN = 256
PROMPT = 1024
TOK_DEV = 768
GTOK = 3072
GROUPS = 2
TOKENS = 6144


def layout(key):
    pieces = PROMPT // CLEN
    per_device = TOK_DEV // CLEN
    total = pieces * per_device

    def one_group(group_key):
        pick_key, order_key, rest_key = jax.random.split(group_key, 3)
        chosen = jax.random.randint(pick_key, (pieces,), 0, per_device)
        prompt_order = jax.random.permutation(order_key, pieces)
        others = jax.random.permutation(rest_key, total) + pieces
        slot = jnp.arange(total) % per_device
        owner = jnp.arange(total) // per_device
        is_prompt = slot == chosen[owner]
        ranks = jnp.where(is_prompt, prompt_order[owner], others)
        block = jnp.argsort(jnp.argsort(ranks))
        seqs = jnp.where(block < pieces, 0, block - pieces + 1)
        base = jnp.where(block < pieces, block * CLEN, PROMPT)
        offsets = jnp.arange(CLEN)
        seq_slots = jnp.repeat(seqs, CLEN)
        pos_slots = (base[:, None] + offsets[None, :]).reshape(-1)
        return (seq_slots.astype(jnp.int32), pos_slots.astype(jnp.int32))
    group_keys = jax.random.split(jax.random.fold_in(key, 11), GROUPS)
    return jax.vmap(one_group)(group_keys)


def draw_seq_ids(key, part):
    return layout(key)[0]


def draw_positions(key, part):
    return layout(key)[1]


def levels(stream_key, shape, cuts, least, high):
    def one(axis_at, parts):
        steps = jax.random.uniform(jax.random.fold_in(jax.random.fold_in(stream_key, 6), axis_at), (parts,), jnp.float32, least / len(cuts), high / len(cuts))
        return jnp.repeat(jnp.exp(steps), shape[axis_at] // parts).reshape((-1,) + (1,) * (len(shape) - axis_at - 1))

    factor_of = one(*cuts[0])
    for cut in cuts[1:]:
        factor_of = factor_of * one(*cut)
    return factor_of


def noise(own_key, extent, deviation, limit, cuts=(), kind=jnp.bfloat16):
    result = deviation * jax.random.normal(own_key, extent, jnp.float32)
    if cuts:
        result = result * levels(own_key, extent, cuts, -0.22, 0.18)
    return jnp.clip(result, -limit, limit).astype(kind)


def setup_inputs(seed: int = 0) -> dict:
    key_list = jax.random.split(jax.random.key(seed), 14)
    return {
        "tokens": noise(key_list[0], (TOKENS, D), 1.0, 6.0, ((0, 8),)),
        "attn_gain": jnp.clip(1.0 + 0.1 * jax.random.normal(key_list[1], (D,), jnp.float32), 0.5, 1.5).astype(jnp.bfloat16),
        "query_weight": noise(key_list[2], (D, D), D ** -0.5, 0.125, ((0, 8), (1, 4))),
        "key_weight": noise(key_list[3], (D, D), D ** -0.5, 0.125, ((0, 8), (1, 4))),
        "value_weight": noise(key_list[4], (D, D), D ** -0.5, 0.125, ((0, 8), (1, 4))),
        "out_weight": noise(key_list[5], (D, D), (max(D // 64, 8)) ** -0.5, 1.0, ((0, 8), (1, 4))),
        "ffn_gain": jnp.clip(1.0 + 0.1 * jax.random.normal(key_list[6], (D,), jnp.float32), 0.5, 1.5).astype(jnp.bfloat16),
        "gate_weight": noise(key_list[7], (D, FF), D ** -0.5, 0.125, ((0, 8), (1, 4))),
        "up_weight": noise(key_list[8], (D, FF), D ** -0.5, 0.125, ((0, 8), (1, 4))),
        "down_weight": noise(key_list[9], (D, FF), FF ** -0.5, 0.0625, ((0, 8), (1, 4))),
        "seq_ids": draw_seq_ids(jax.random.fold_in(key_list[13], 71), 0),
        "positions": draw_positions(jax.random.fold_in(key_list[13], 71), 0),
        "out_grad": noise(key_list[12], (TOKENS, D), 1.0, 6.0, ((0, 8),)),
    }


EPS = 1e-05
ROPE_BASE = 130000.0
MASKED = -1e+30

@jax.custom_vjp
def low(v):
    return lax.optimization_barrier(v.astype(jnp.bfloat16)).astype(jnp.float32)

@jax.custom_vjp
def low_back(v):
    return v

def low_keep(v):
    return (low(v), None)

def low_pass(kept, grad):
    return (grad,)

def back_keep(v):
    return (v, None)

def back_low(kept, grad):
    return (low(grad),)
low.defvjp(low_keep, low_pass)
low_back.defvjp(back_keep, back_low)

def matmul(left, right):
    return jnp.dot(left, right, precision=lax.Precision.HIGHEST)

def rope_angles(where):
    half = HEAD_DIM // 2
    freqs = ROPE_BASE ** (-(jnp.arange(half).astype(jnp.float32) * 2.0) / HEAD_DIM)
    angles = where.astype(jnp.float32)[:, None] * freqs[None, :]
    return (jnp.cos(angles), jnp.sin(angles))

def rotate(values, cosine, sine):
    half = HEAD_DIM // 2
    first_half = values[..., :half]
    second_half = values[..., half:]
    cosine = cosine[:, None, :]
    sine = sine[:, None, :]
    return jnp.concatenate([first_half * cosine - second_half * sine, second_half * cosine + first_half * sine], axis=-1)

def normalize(values):
    return values * lax.rsqrt(lax.optimization_barrier(jnp.mean(values * values, axis=-1, keepdims=True)) + EPS)

def layer(params, inputs, seqs, where):
    attn_gain, query_weight, key_weight, value_weight, out_weight, ffn_gain, gate_weight, up_weight, down_weight = params
    count = inputs.shape[0]
    cosine, sine = rope_angles(where)
    first = low(normalize(inputs) * attn_gain)
    query = low(rotate(low_back(matmul(first, query_weight)).reshape(count, HEADS, HEAD_DIM), cosine, sine))
    keys = low(rotate(low_back(matmul(first, key_weight)).reshape(count, HEADS, HEAD_DIM), cosine, sine))
    values = low(low_back(matmul(first, value_weight))).reshape(count, HEADS, HEAD_DIM)
    visible = (where[None, :] <= where[:, None]) & ((seqs[None, :] == 0) | (seqs[None, :] == seqs[:, None]))
    scale = HEAD_DIM ** (-0.5)

    def one_head(operands):
        query_head, key_head, value_head = operands
        scores = low_back(matmul(query_head, key_head.T) * scale)
        scores = jnp.where(visible, scores, MASKED)
        shifted = jnp.exp(scores - lax.optimization_barrier(jnp.max(scores, axis=-1, keepdims=True)))
        probs = shifted / lax.optimization_barrier(jnp.sum(shifted, axis=-1, keepdims=True))
        return matmul(low(probs), value_head)
    heads = lax.map(jax.checkpoint(one_head), (query.transpose(1, 0, 2), keys.transpose(1, 0, 2), values.transpose(1, 0, 2)))
    mixed = low_back(low(heads.transpose(1, 0, 2).reshape(count, D)))
    middle = inputs + low_back(matmul(mixed, out_weight.T))
    second = low(normalize(middle) * ffn_gain)
    gate = low_back(matmul(second, gate_weight))
    upward = low_back(matmul(second, up_weight))
    hidden = low(jax.nn.silu(gate) * upward)
    return middle + low_back(matmul(hidden, down_weight.T))

def reference(tokens, attn_gain, query_weight, key_weight, value_weight, out_weight, ffn_gain, gate_weight, up_weight, down_weight, seq_ids, positions, out_grad):
    params = tuple((weight.astype(jnp.float32) for weight in (attn_gain, query_weight, key_weight, value_weight, out_weight, ffn_gain, gate_weight, up_weight, down_weight)))
    inputs = tokens.astype(jnp.float32).reshape(GROUPS, GTOK, D)
    cotangents = out_grad.astype(jnp.float32).reshape(GROUPS, GTOK, D)

    def step(totals, group):
        rows, seqs, where, cotangent = group
        outputs, pullback = jax.vjp(lambda weights, acts: layer(weights, acts, seqs, where), params, rows)
        weight_grads, row_grads = pullback(cotangent)
        totals = tuple((total + extra for total, extra in zip(totals, weight_grads)))
        return (totals, (outputs, row_grads))
    initial = tuple((jnp.zeros_like(weight) for weight in params))
    totals, (outputs, row_grads) = lax.scan(step, initial, (inputs, seq_ids, positions, cotangents))
    block_out = outputs.reshape(TOKENS, D).astype(jnp.bfloat16)
    in_grad = row_grads.reshape(TOKENS, D).astype(jnp.bfloat16)
    return (block_out, in_grad, totals[0], totals[1], totals[2], totals[3], totals[4], totals[5], totals[6], totals[7], totals[8])
```

```python
import functools
import math

import jax
import jax.numpy as jnp
from jax import lax
from jax.experimental import pallas as pl
from jax.experimental.pallas import tpu as pltpu
from jax.sharding import PartitionSpec as P

HEAD_DIM = 64
CLEN = 256
LANES = 128
EPS = 1e-05
ROPE_BASE = 130000.0
MASKED = -1e30
FFN_CHUNKS = 4
BF16 = jnp.bfloat16
F32 = jnp.float32
VMEM_LIMIT = 56 * 1024 * 1024


def swap(values, axis, mask):
    count = lax.axis_size(axis)
    return lax.ppermute(values, axis, [(i, i ^ mask) for i in range(count)])


def fetch(values, axis, shift):
    count = lax.axis_size(axis)
    return lax.ppermute(values, axis, [(i, (i - shift) % count) for i in range(count)])


def send(values, axis, shift):
    count = lax.axis_size(axis)
    return lax.ppermute(values, axis, [(i, (i + shift) % count) for i in range(count)])


def add_low(left, right):
    return (left.astype(F32) + right.astype(F32)).astype(BF16)


def sum_over_tp(part):
    count = lax.axis_size("tp")
    rows = part.shape[0]
    half = rows // 2
    bit = lax.axis_index("tp") & 1
    keep = lax.dynamic_slice_in_dim(part, bit * half, half)
    give = lax.dynamic_slice_in_dim(part, (1 - bit) * half, half)
    total = add_low(keep, swap(give, "tp", 1))
    mask = 2
    while mask < count:
        total = add_low(total, swap(total, "tp", mask))
        mask *= 2
    back = swap(total, "tp", 1)
    first = jnp.where(bit == 0, total, back)
    last = jnp.where(bit == 0, back, total)
    return jnp.concatenate([first, last], axis=0)


def scatter_over_tp(part, shift):
    count = lax.axis_size("tp")
    width = part.shape[1] // count
    me = lax.axis_index("tp")

    def block(owner):
        start = lax.rem(owner * width - shift + part.shape[1], part.shape[1])
        return lax.dynamic_slice_in_dim(part, start, width, 1)

    held = {other: None for other in range(0, count, 2)}
    for other in held:
        held[other] = add_low(block(me ^ other), swap(block(me ^ other ^ 1), "tp", 1))
    mask = count // 2
    while mask >= 2:
        for other in [o for o in held if o & mask]:
            held[other ^ mask] = add_low(held[other ^ mask], swap(held.pop(other), "tp", mask))
        mask //= 2
    return held[0]


def sum_everywhere(values):
    for axis in ("tp", "ctx", "dp"):
        mask = 1
        while mask < lax.axis_size(axis):
            values = values + swap(values, axis, mask)
            mask *= 2
    return values


def gather_rows(weight):
    own = lax.all_gather(weight, "ctx", axis=0, tiled=True)
    return [own] + [fetch(own, "dp", s) for s in range(1, lax.axis_size("dp"))]


def scatter_rows(blocks):
    total = blocks[0]
    extra = [send(block, "dp", s) for s, block in enumerate(blocks) if s]
    if extra:
        total = total.astype(F32)
        for term in extra:
            total = total + term.astype(F32)
        total = total.astype(BF16)
    return lax.psum_scatter(total, "ctx", scatter_dimension=0, tiled=True)


def dot(left, right, dims):
    return lax.dot_general(left, right, (dims, ((), ())), preferred_element_type=F32)


NN = ((1,), (0,))
NT = ((1,), (1,))
TN = ((0,), (0,))


def half_swap(values):
    lane = lax.broadcasted_iota(jnp.int32, values.shape, 1)
    ahead = pltpu.roll(values, LANES - 32, 1)
    behind = pltpu.roll(values, 32, 1)
    return jnp.where((lane & 63) < 32, ahead, behind)


def project_kernel(count, rope, x_ref, *refs):
    w_refs = refs[:count]
    cos_ref, sin_ref, out_ref = refs[count:]
    depth = w_refs[0].shape[0]
    total = None
    for piece in range(count):
        term = dot(x_ref[:, piece * depth : (piece + 1) * depth], w_refs[piece][...], NN)
        total = term if total is None else total + term
    if rope:
        cosine, sine = cos_ref[...], sin_ref[...]
        for at in range(0, total.shape[1], LANES):
            part = total[:, at : at + LANES]
            out_ref[:, at : at + LANES] = (part * cosine + half_swap(part) * sine).astype(BF16)
    else:
        out_ref[...] = total.astype(BF16)


def project(x, pieces, cosine, sine, rope):
    rows, width = x.shape[0], pieces[0].shape[1]
    count = len(pieces)
    full = lambda i: (0, 0)
    row = lambda i: (i, 0)
    return pl.pallas_call(
        functools.partial(project_kernel, count, rope),
        grid=(rows // CLEN,),
        in_specs=[pl.BlockSpec((CLEN, x.shape[1]), row)]
        + [pl.BlockSpec(p.shape, full) for p in pieces]
        + [pl.BlockSpec((CLEN, LANES), row)] * 2,
        out_specs=pl.BlockSpec((CLEN, width), row),
        out_shape=jax.ShapeDtypeStruct((rows, width), BF16),
        compiler_params=pltpu.CompilerParams(vmem_limit_bytes=VMEM_LIMIT),
        cost_estimate=pl.CostEstimate(
            flops=2 * rows * x.shape[1] * width,
            bytes_accessed=2 * (x.size + x.shape[1] * width + rows * width),
            transcendentals=0,
        ),
        name="project",
    )(x, *pieces, cosine, sine)


SCALE = HEAD_DIM**-0.5
SCALE_LOG2 = SCALE * math.log2(math.e)


def forward_kernel(pieces, order_ref, rank_ref, q_ref, ks_ref, vs_ref, *refs):
    kp_refs, vp_refs = refs[:pieces], refs[pieces : 2 * pieces]
    o_ref, lse_ref = refs[2 * pieces :]
    q = q_ref[...]
    size = q.shape[0]
    prompt = pl.program_id(1) == 0
    low_lane = lax.broadcasted_iota(jnp.int32, q.shape, 1) < HEAD_DIM
    causal = lax.broadcasted_iota(jnp.int32, (size, size), 0) >= lax.broadcasted_iota(
        jnp.int32, (size, size), 1
    )
    outs = []
    for head in range(2):
        own = low_lane if head == 0 else jnp.logical_not(low_lane)
        qh = jnp.where(own, q, jnp.zeros_like(q))
        raw = [jnp.where(causal, dot(qh, ks_ref[...], NT), MASKED)]
        for s in range(pieces):
            hidden = jnp.logical_and(prompt, rank_ref[s] >= rank_ref[0])
            raw.append(dot(qh, kp_refs[s][...], NT) + jnp.where(hidden, MASKED, 0.0))
        top = raw[0]
        for r in raw[1:]:
            top = jnp.maximum(top, r)
        top = jnp.max(top, axis=-1, keepdims=True) * SCALE_LOG2
        sums, acc = None, None
        for s, r in enumerate(raw):
            e = jnp.exp2(r * SCALE_LOG2 - top)
            v = vs_ref if s == 0 else vp_refs[s - 1]
            term = dot(e.astype(BF16), v[...], NN)
            sums = e if sums is None else sums + e
            acc = term if acc is None else acc + term
        total = jnp.sum(sums, axis=-1, keepdims=True)
        outs.append((acc / total, top + jnp.log2(total)))
    o_ref[...] = jnp.where(low_lane, outs[0][0], outs[1][0]).astype(BF16)
    lse_ref[...] = jnp.where(low_lane, outs[0][1], outs[1][1])


def backward_kernel(
    pieces, order_ref, rank_ref, q_ref, ks_ref, vs_ref, o_ref, lse_ref, do_ref, cos_ref, sin_ref, *refs
):
    kp_refs, vp_refs = refs[:pieces], refs[pieces : 2 * pieces]
    dq_ref, dks_ref, dvs_ref, dkp_ref, dvp_ref = refs[2 * pieces :]
    step = pl.program_id(1)
    prompt = step == 0
    q, do = q_ref[...], do_ref[...]
    size = q.shape[0]
    low_lane = lax.broadcasted_iota(jnp.int32, q.shape, 1) < HEAD_DIM
    causal = lax.broadcasted_iota(jnp.int32, (size, size), 0) >= lax.broadcasted_iota(
        jnp.int32, (size, size), 1
    )
    product = do.astype(F32) * o_ref[...].astype(F32)
    lse = lse_ref[...]
    dq_heads = []
    dk_all = [None] * (pieces + 1)
    dv_all = [None] * (pieces + 1)
    for head in range(2):
        own = low_lane if head == 0 else jnp.logical_not(low_lane)
        qh = jnp.where(own, q, jnp.zeros_like(q))
        doh = jnp.where(own, do, jnp.zeros_like(do))
        delta = jnp.sum(jnp.where(own, product, 0.0), axis=-1, keepdims=True)
        log_sum = lse[:, head * HEAD_DIM : head * HEAD_DIM + 1]
        dq = None
        for s in range(pieces + 1):
            k = (ks_ref if s == 0 else kp_refs[s - 1])[...]
            v = (vs_ref if s == 0 else vp_refs[s - 1])[...]
            raw = dot(qh, k, NT)
            if s == 0:
                raw = jnp.where(causal, raw, MASKED)
            else:
                hidden = jnp.logical_and(prompt, rank_ref[s - 1] >= rank_ref[0])
                raw = raw + jnp.where(hidden, MASKED, 0.0)
            prob = jnp.exp2(raw * SCALE_LOG2 - log_sum)
            ds = (prob * (dot(doh, v, NT) - delta)).astype(BF16)
            term = dot(ds, k, NN)
            dq = term if dq is None else dq + term
            dk = dot(ds, qh, TN)
            dv = dot(prob.astype(BF16), doh, TN)
            dk_all[s] = dk if dk_all[s] is None else dk_all[s] + dk
            dv_all[s] = dv if dv_all[s] is None else dv_all[s] + dv
        dq_heads.append(dq)
    dq = jnp.where(low_lane, dq_heads[0], dq_heads[1]) * SCALE
    cosine, sine = cos_ref[...], sin_ref[...]
    dq_ref[...] = (dq * cosine - half_swap(dq) * sine).astype(BF16)
    dks_ref[...] = dk_all[0] * SCALE
    dvs_ref[...] = dv_all[0]
    for s in range(pieces):
        at = slice(s * size, (s + 1) * size)

        @pl.when(prompt)
        def _():
            dkp_ref[at, :] = dk_all[s + 1] * SCALE
            dvp_ref[at, :] = dv_all[s + 1]

        @pl.when(jnp.logical_not(prompt))
        def _():
            dkp_ref[at, :] += dk_all[s + 1] * SCALE
            dvp_ref[at, :] += dv_all[s + 1]


def attention_specs(pieces, key_pairs):
    own = pl.BlockSpec((CLEN, LANES), lambda h, j, order, rank: (order[j], h))
    key = pl.BlockSpec((CLEN, LANES), lambda h, j, order, rank: (0, h))
    value = pl.BlockSpec((CLEN, LANES), lambda h, j, order, rank: (0, key_pairs + h))
    trig = pl.BlockSpec((CLEN, LANES), lambda h, j, order, rank: (order[j], 0))
    prompt = pl.BlockSpec((pieces * CLEN, LANES), lambda h, j, order, rank: (0, h))
    return own, key, value, trig, prompt


def attention_forward(order, rank, query, keys, values, prompts):
    rows, width = query.shape
    pieces, pairs = len(prompts), width // LANES
    own, key, value, _, _ = attention_specs(pieces, pairs)
    scores = rows * (pieces + 1) * CLEN * (width // HEAD_DIM)
    return pl.pallas_call(
        functools.partial(forward_kernel, pieces),
        grid_spec=pltpu.PrefetchScalarGridSpec(
            num_scalar_prefetch=2,
            grid=(pairs, rows // CLEN),
            in_specs=[own] * 3 + [key] * pieces + [value] * pieces,
            out_specs=[own, own],
        ),
        out_shape=[jax.ShapeDtypeStruct((rows, width), BF16), jax.ShapeDtypeStruct((rows, width), F32)],
        compiler_params=pltpu.CompilerParams(vmem_limit_bytes=VMEM_LIMIT),
        cost_estimate=pl.CostEstimate(
            flops=16 * scores * HEAD_DIM, bytes_accessed=16 * rows * width, transcendentals=scores
        ),
        name="attend",
    )(order, rank, query, keys, values, *prompts, *prompts)


def attention_backward(order, rank, query, keys, values, mixed, lse, dmixed, cosine, sine, prompts):
    rows, width = query.shape
    pieces, pairs = len(prompts), width // LANES
    own, key, value, trig, prompt = attention_specs(pieces, pairs)
    scores = rows * (pieces + 1) * CLEN * (width // HEAD_DIM)
    return pl.pallas_call(
        functools.partial(backward_kernel, pieces),
        grid_spec=pltpu.PrefetchScalarGridSpec(
            num_scalar_prefetch=2,
            grid=(pairs, rows // CLEN),
            in_specs=[own] * 6 + [trig] * 2 + [key] * pieces + [value] * pieces,
            out_specs=[own, own, own, prompt, prompt],
        ),
        out_shape=[
            jax.ShapeDtypeStruct((rows, width), BF16),
            jax.ShapeDtypeStruct((rows, width), F32),
            jax.ShapeDtypeStruct((rows, width), F32),
            jax.ShapeDtypeStruct((pieces * CLEN, width), F32),
            jax.ShapeDtypeStruct((pieces * CLEN, width), F32),
        ],
        compiler_params=pltpu.CompilerParams(vmem_limit_bytes=VMEM_LIMIT),
        cost_estimate=pl.CostEstimate(
            flops=40 * scores * HEAD_DIM, bytes_accessed=32 * rows * width, transcendentals=scores
        ),
        name="attend_back",
    )(order, rank, query, keys, values, mixed, lse, dmixed, cosine, sine, *prompts, *prompts)


def normalize(values):
    factor = lax.rsqrt(jnp.mean(values * values, axis=-1, keepdims=True) + EPS)
    return (values * factor, factor)


def rope_tables(where):
    half = HEAD_DIM // 2
    freqs = ROPE_BASE ** (-(jnp.arange(half).astype(F32) * 2.0) / HEAD_DIM)
    angles = where.astype(F32)[:, None] * freqs[None, :]
    cosine, sine = jnp.cos(angles), jnp.sin(angles)
    return (
        jnp.concatenate([cosine] * 4, axis=1),
        jnp.concatenate([-sine, sine, -sine, sine], axis=1),
    )


def matmul_pieces(left, pieces):
    depth = pieces[0].shape[0]
    total = None
    for s, piece in enumerate(pieces):
        term = jnp.dot(left[:, s * depth : (s + 1) * depth], piece, preferred_element_type=F32)
        total = term if total is None else total + term
    return total


def matmul_back(left, pieces):
    return jnp.concatenate(
        [jnp.einsum("qf,df->qd", left, p, preferred_element_type=F32) for p in pieces], axis=1
    )


def row_grads(left, right, blocks):
    depth = left.shape[1] // blocks
    return [
        jnp.einsum(
            "tc,tf->cf", left[:, s * depth : (s + 1) * depth], right, preferred_element_type=F32
        ).astype(BF16)
        for s in range(blocks)
    ]


def body(
    tokens,
    attn_gain,
    query_weight,
    key_weight,
    value_weight,
    out_weight,
    ffn_gain,
    gate_weight,
    up_weight,
    down_weight,
    seq_ids,
    positions,
    out_grad,
):
    rows, width = tokens.shape
    head_width = query_weight.shape[1]
    ffn_width = gate_weight.shape[1]
    chunk = ffn_width // FFN_CHUNKS
    dp_count = lax.axis_size("dp")
    ctx_count = lax.axis_size("ctx")
    tp_count = lax.axis_size("tp")
    dp_index = lax.axis_index("dp")
    ctx_index = lax.axis_index("ctx")
    tp_index = lax.axis_index("tp")
    shift = dp_index * (width // dp_count)

    def turned(values):
        doubled = jnp.concatenate([values, values], axis=-1)
        return lax.dynamic_slice_in_dim(doubled, shift, width, values.ndim - 1)

    q_pieces = gather_rows(query_weight)
    k_pieces = gather_rows(key_weight)
    v_pieces = gather_rows(value_weight)
    o_pieces = gather_rows(out_weight)
    ffn_pieces = []
    for f in range(FFN_CHUNKS):
        at = slice(f * chunk, (f + 1) * chunk)
        ffn_pieces.append(
            gather_rows(
                jnp.concatenate([gate_weight[:, at], up_weight[:, at], down_weight[:, at]], axis=1)
            )
        )

    group_seq = seq_ids[0].reshape(ctx_count, rows // CLEN, CLEN)[:, :, 0]
    group_pos = positions[0].reshape(ctx_count, rows // CLEN, CLEN)[:, :, 0]
    prompt_at = jnp.argmax(group_seq == 0, axis=1).astype(jnp.int32)
    prompt_rank = jnp.sum(jnp.where(group_seq == 0, group_pos, 0), axis=1).astype(jnp.int32)
    rank = jnp.roll(prompt_rank, -ctx_index)
    mine = prompt_at[ctx_index]
    blocks = jnp.arange(rows // CLEN, dtype=jnp.int32)
    order = jnp.concatenate([mine[None], jnp.sort(jnp.where(blocks == mine, -1, blocks))[1:]])
    own_pos = lax.dynamic_slice_in_dim(positions[0], ctx_index * rows, rows)
    cosine, sine = rope_tables(own_pos)

    inputs = turned(tokens).astype(F32)
    cotangent_low = turned(out_grad)
    gain_one = turned(attn_gain).astype(F32)
    gain_two = turned(ffn_gain).astype(F32)
    first_norm, first_scale = normalize(inputs)
    first = (first_norm * gain_one).astype(BF16)

    query = project(first, q_pieces, cosine, sine, True)
    keys = project(first, k_pieces, cosine, sine, True)
    values = project(first, v_pieces, cosine, sine, False)
    prompt_own = jnp.concatenate(
        [
            lax.dynamic_slice_in_dim(keys, mine * CLEN, CLEN),
            lax.dynamic_slice_in_dim(values, mine * CLEN, CLEN),
        ],
        axis=1,
    )
    prompts = [prompt_own] + [fetch(prompt_own, "ctx", s) for s in range(1, ctx_count)]
    mixed, lse = attention_forward(order, rank, query, keys, values, prompts)
    middle = inputs + sum_over_tp(matmul_back(mixed, o_pieces).astype(BF16)).astype(F32)
    second_norm, second_scale = normalize(middle)
    second = (second_norm * gain_two).astype(BF16)

    ffn_part, dsecond_part = None, None
    ffn_grads = []
    for f in range(FFN_CHUNKS):
        gate_w = [p[:, :chunk] for p in ffn_pieces[f]]
        up_w = [p[:, chunk : 2 * chunk] for p in ffn_pieces[f]]
        down_w = [p[:, 2 * chunk :] for p in ffn_pieces[f]]
        gate = matmul_pieces(second, gate_w)
        upward = matmul_pieces(second, up_w)
        dhidden = matmul_pieces(cotangent_low, down_w)
        sigmoid_gate = jax.nn.sigmoid(gate)
        silu_gate = gate * sigmoid_gate
        hidden = (silu_gate * upward).astype(BF16)
        dgate = (
            dhidden * upward * (sigmoid_gate + gate * sigmoid_gate * (1.0 - sigmoid_gate))
        ).astype(BF16)
        dupward = (dhidden * silu_gate).astype(BF16)
        part = matmul_back(hidden, down_w)
        ffn_part = part if ffn_part is None else ffn_part + part
        part = matmul_back(dgate, gate_w) + matmul_back(dupward, up_w)
        dsecond_part = part if dsecond_part is None else dsecond_part + part
        grads = [
            jnp.concatenate(terms, axis=1)
            for terms in zip(
                row_grads(second, dgate, dp_count),
                row_grads(second, dupward, dp_count),
                row_grads(cotangent_low, hidden, dp_count),
            )
        ]
        ffn_grads.append(scatter_rows(grads))

    share = width // tp_count
    ffn_share = scatter_over_tp(ffn_part.astype(BF16), shift).astype(F32)

    def own_share(values):
        start = lax.rem(tp_index * share - shift + width, width)
        return lax.dynamic_slice_in_dim(values, start, share, values.ndim - 1)

    block_out = (own_share(middle) + ffn_share).astype(BF16)

    cotangent = cotangent_low.astype(F32)
    dsecond = sum_over_tp(dsecond_part.astype(BF16)).astype(F32)
    gain_two_grad = jnp.sum(dsecond * second_norm, axis=0)
    scaled_two = dsecond * gain_two
    dmiddle = cotangent + second_scale * (
        scaled_two - second_norm * jnp.mean(scaled_two * second_norm, axis=-1, keepdims=True)
    )
    dmiddle_low = dmiddle.astype(BF16)
    dmixed = matmul_pieces(dmiddle_low, o_pieces).astype(BF16)
    dquery_low, dkey_own, dvalue_own, dkey_prompt, dvalue_prompt = attention_backward(
        order, rank, query, keys, values, mixed, lse, dmixed, cosine, sine, prompts
    )
    dprompt = jnp.concatenate([dkey_prompt, dvalue_prompt], axis=1)
    extra = dprompt[:CLEN]
    for s in range(1, ctx_count):
        piece = dprompt[s * CLEN : (s + 1) * CLEN].astype(BF16)
        extra = extra + send(piece, "ctx", s).astype(F32)
    is_mine = (jnp.arange(rows, dtype=jnp.int32) // CLEN == mine)[:, None]
    wide = jnp.concatenate([extra] * (rows // CLEN), axis=0)
    dkey = dkey_own + jnp.where(is_mine, wide[:, :head_width], 0.0)
    dvalue_low = (dvalue_own + jnp.where(is_mine, wide[:, head_width:], 0.0)).astype(BF16)
    half = HEAD_DIM // 2
    turned_key = dkey.reshape(rows, head_width // HEAD_DIM, 2, half)[:, :, ::-1].reshape(rows, head_width)
    repeats = head_width // LANES
    dkey_low = (
        dkey * jnp.concatenate([cosine] * repeats, axis=1)
        - turned_key * jnp.concatenate([sine] * repeats, axis=1)
    ).astype(BF16)

    attn_blocks = [
        jnp.concatenate(terms, axis=1)
        for terms in zip(
            row_grads(first, dquery_low, dp_count),
            row_grads(first, dkey_low, dp_count),
            row_grads(first, dvalue_low, dp_count),
            row_grads(dmiddle_low, mixed, dp_count),
        )
    ]
    attn_grads = scatter_rows(attn_blocks)

    dfirst_part = (
        matmul_back(dquery_low, q_pieces)
        + matmul_back(dkey_low, k_pieces)
        + matmul_back(dvalue_low, v_pieces)
    )
    dfirst = scatter_over_tp(dfirst_part.astype(BF16), shift).astype(F32)
    norm_share = own_share(first_norm)
    gain_one_grad = jnp.sum(dfirst * norm_share, axis=0)
    scaled_one = dfirst * own_share(gain_one)
    inner = jnp.sum(scaled_one * norm_share, axis=-1).reshape(1, rows)
    mask = 1
    while mask < tp_count:
        inner = inner + swap(inner, "tp", mask)
        mask *= 2
    inner = inner.reshape(rows, 1) / width
    in_grad = (own_share(dmiddle) + first_scale * (scaled_one - norm_share * inner)).astype(BF16)

    gains = jnp.stack([gain_one_grad, own_share(gain_two_grad)])
    gains = lax.dynamic_update_slice_in_dim(
        jnp.zeros((2, width), F32), gains, tp_index * share, 1
    )
    gains = sum_everywhere(gains)
    part = width // (dp_count * ctx_count)
    gains = lax.dynamic_slice_in_dim(gains, (dp_index * ctx_count + ctx_index) * part, part, 1)

    attn_grads = attn_grads.astype(F32)
    ffn_out = [
        jnp.concatenate([g[:, i * chunk : (i + 1) * chunk].astype(F32) for g in ffn_grads], axis=1)
        for i in range(3)
    ]
    return (
        block_out,
        in_grad,
        gains[0],
        attn_grads[:, :head_width],
        attn_grads[:, head_width : 2 * head_width],
        attn_grads[:, 2 * head_width : 3 * head_width],
        attn_grads[:, 3 * head_width :],
        gains[1],
        ffn_out[0],
        ffn_out[1],
        ffn_out[2],
    )


def solution(mesh):
    split = P(("dp", "ctx"), "tp")
    rows = P(("dp", "ctx"), None)
    vector = P(("dp", "ctx"))
    return jax.shard_map(
        body,
        mesh=mesh,
        in_specs=(rows, P(), split, split, split, split, P(), split, split, split)
        + (P("dp", None), P("dp", None), rows),
        out_specs=(split, split, vector, split, split, split, split, vector, split, split, split),
        check_vma=False,
    )
```

```python
import functools
import math

import jax
import jax.numpy as jnp
from jax import lax
from jax.experimental import pallas as pl
from jax.experimental.pallas import tpu as pltpu
from jax.sharding import PartitionSpec as P

HEAD_DIM = 64
CLEN = 256
LANES = 128
EPS = 1e-05
ROPE_BASE = 130000.0
MASKED = -1e30
FFN_CHUNKS = 2
BF16 = jnp.bfloat16
F32 = jnp.float32
VMEM_LIMIT = 56 * 1024 * 1024


def swap(values, axis, mask):
    count = lax.axis_size(axis)
    return lax.ppermute(values, axis, [(i, i ^ mask) for i in range(count)])


def fetch(values, axis, shift):
    count = lax.axis_size(axis)
    return lax.ppermute(values, axis, [(i, (i - shift) % count) for i in range(count)])


def send(values, axis, shift):
    count = lax.axis_size(axis)
    return lax.ppermute(values, axis, [(i, (i + shift) % count) for i in range(count)])


def add(left, right):
    return left.astype(F32) + right.astype(F32)


def low(values):
    return values.astype(BF16)


def gather_dp(own):
    return [own] + [fetch(own, "dp", s) for s in range(1, lax.axis_size("dp"))]


def scatter_dp(blocks):
    total = blocks[0]
    extra = [send(block, "dp", s) for s, block in enumerate(blocks) if s]
    for term in extra:
        total = add(total, term)
    return low(total)


def dot(left, right, dims):
    return lax.dot_general(left, right, (dims, ((), ())), preferred_element_type=F32)


NN = ((1,), (0,))
NT = ((1,), (1,))
TN = ((0,), (0,))


def half_swap(values):
    lane = lax.broadcasted_iota(jnp.int32, values.shape, 1)
    ahead = pltpu.roll(values, LANES - 32, 1)
    behind = pltpu.roll(values, 32, 1)
    return jnp.where((lane & 63) < 32, ahead, behind)


def project_kernel(count, rope, x_ref, *refs):
    w_refs = refs[:count]
    cos_ref, sin_ref, out_ref = refs[count:]
    depth = w_refs[0].shape[0]
    total = None
    for piece in range(count):
        term = dot(x_ref[:, piece * depth : (piece + 1) * depth], w_refs[piece][...], NN)
        total = term if total is None else total + term
    if rope:
        cosine, sine = cos_ref[...], sin_ref[...]
        for at in range(0, total.shape[1], LANES):
            part = total[:, at : at + LANES]
            out_ref[:, at : at + LANES] = (part * cosine + half_swap(part) * sine).astype(BF16)
    else:
        out_ref[...] = total.astype(BF16)


def project(x, pieces, cosine, sine, rope):
    rows, width = x.shape[0], pieces[0].shape[1]
    count = len(pieces)
    full = lambda i: (0, 0)
    row = lambda i: (i, 0)
    return pl.pallas_call(
        functools.partial(project_kernel, count, rope),
        grid=(rows // CLEN,),
        in_specs=[pl.BlockSpec((CLEN, x.shape[1]), row)]
        + [pl.BlockSpec(p.shape, full) for p in pieces]
        + [pl.BlockSpec((CLEN, LANES), row)] * 2,
        out_specs=pl.BlockSpec((CLEN, width), row),
        out_shape=jax.ShapeDtypeStruct((rows, width), BF16),
        compiler_params=pltpu.CompilerParams(vmem_limit_bytes=VMEM_LIMIT),
        cost_estimate=pl.CostEstimate(
            flops=2 * rows * x.shape[1] * width,
            bytes_accessed=2 * (x.size + x.shape[1] * width + rows * width),
            transcendentals=0,
        ),
        name="project",
    )(x, *pieces, cosine, sine)


SCALE = HEAD_DIM**-0.5
SCALE_LOG2 = SCALE * math.log2(math.e)


def forward_kernel(pieces, order_ref, rank_ref, q_ref, ks_ref, vs_ref, *refs):
    kp_refs, vp_refs = refs[:pieces], refs[pieces : 2 * pieces]
    o_ref, lse_ref = refs[2 * pieces :]
    q = q_ref[...]
    size = q.shape[0]
    prompt = pl.program_id(1) == 0
    low_lane = lax.broadcasted_iota(jnp.int32, q.shape, 1) < HEAD_DIM
    causal = lax.broadcasted_iota(jnp.int32, (size, size), 0) >= lax.broadcasted_iota(
        jnp.int32, (size, size), 1
    )
    outs = []
    for head in range(2):
        own = low_lane if head == 0 else jnp.logical_not(low_lane)
        qh = jnp.where(own, q, jnp.zeros_like(q))
        raw = [jnp.where(causal, dot(qh, ks_ref[...], NT), MASKED)]
        for s in range(pieces):
            hidden = jnp.logical_and(prompt, rank_ref[s] >= rank_ref[0])
            raw.append(dot(qh, kp_refs[s][...], NT) + jnp.where(hidden, MASKED, 0.0))
        top = raw[0]
        for r in raw[1:]:
            top = jnp.maximum(top, r)
        top = jnp.max(top, axis=-1, keepdims=True) * SCALE_LOG2
        sums, acc = None, None
        for s, r in enumerate(raw):
            e = jnp.exp2(r * SCALE_LOG2 - top)
            v = vs_ref if s == 0 else vp_refs[s - 1]
            term = dot(e.astype(BF16), v[...], NN)
            sums = e if sums is None else sums + e
            acc = term if acc is None else acc + term
        total = jnp.sum(sums, axis=-1, keepdims=True)
        outs.append((acc / total, top + jnp.log2(total)))
    o_ref[...] = jnp.where(low_lane, outs[0][0], outs[1][0]).astype(BF16)
    lse_ref[...] = jnp.where(low_lane, outs[0][1], outs[1][1])


def backward_kernel(
    pieces, order_ref, rank_ref, q_ref, ks_ref, vs_ref, o_ref, lse_ref, do_ref, cos_ref, sin_ref, *refs
):
    kp_refs, vp_refs = refs[:pieces], refs[pieces : 2 * pieces]
    dq_ref, dks_ref, dvs_ref = refs[2 * pieces : 2 * pieces + 3]
    piece_refs = refs[2 * pieces + 3 : 3 * pieces + 3]
    acc_ref = refs[-1]
    pair, step = pl.program_id(0), pl.program_id(1)
    prompt = step == 0
    q, do = q_ref[...], do_ref[...]
    size = q.shape[0]
    low_lane = lax.broadcasted_iota(jnp.int32, q.shape, 1) < HEAD_DIM
    causal = lax.broadcasted_iota(jnp.int32, (size, size), 0) >= lax.broadcasted_iota(
        jnp.int32, (size, size), 1
    )
    product = do.astype(F32) * o_ref[...].astype(F32)
    lse = lse_ref[...]
    dq_heads = []
    dk_all = [None] * (pieces + 1)
    dv_all = [None] * (pieces + 1)
    for head in range(2):
        own = low_lane if head == 0 else jnp.logical_not(low_lane)
        qh = jnp.where(own, q, jnp.zeros_like(q))
        doh = jnp.where(own, do, jnp.zeros_like(do))
        delta = jnp.sum(jnp.where(own, product, 0.0), axis=-1, keepdims=True)
        log_sum = lse[:, head * HEAD_DIM : head * HEAD_DIM + 1]
        dq = None
        for s in range(pieces + 1):
            k = (ks_ref if s == 0 else kp_refs[s - 1])[...]
            v = (vs_ref if s == 0 else vp_refs[s - 1])[...]
            raw = dot(qh, k, NT)
            if s == 0:
                raw = jnp.where(causal, raw, MASKED)
            else:
                hidden = jnp.logical_and(prompt, rank_ref[s - 1] >= rank_ref[0])
                raw = raw + jnp.where(hidden, MASKED, 0.0)
            prob = jnp.exp2(raw * SCALE_LOG2 - log_sum)
            ds = (prob * (dot(doh, v, NT) - delta)).astype(BF16)
            term = dot(ds, k, NN)
            dq = term if dq is None else dq + term
            dk = dot(ds, qh, TN)
            dv = dot(prob.astype(BF16), doh, TN)
            dk_all[s] = dk if dk_all[s] is None else dk_all[s] + dk
            dv_all[s] = dv if dv_all[s] is None else dv_all[s] + dv
        dq_heads.append(dq)
    dq = jnp.where(low_lane, dq_heads[0], dq_heads[1]) * SCALE
    cosine, sine = cos_ref[...], sin_ref[...]
    dq_ref[...] = (dq * cosine - half_swap(dq) * sine).astype(BF16)
    dks_ref[...] = dk_all[0] * SCALE
    dvs_ref[...] = dv_all[0]
    for s in range(pieces):
        both = jnp.concatenate([dk_all[s + 1] * SCALE, dv_all[s + 1]], axis=1)
        at = slice(s * size, (s + 1) * size)

        @pl.when(prompt)
        def _(both=both, at=at):
            acc_ref[at, :] = both

        @pl.when(jnp.logical_not(prompt))
        def _(both=both, at=at):
            acc_ref[at, :] += both

    @pl.when(step == pl.num_programs(1) - 1)
    def _():
        wide = piece_refs[0].shape[1] // 2
        k_at = pl.ds(pl.multiple_of(pair * LANES, LANES), LANES)
        v_at = pl.ds(pl.multiple_of(wide + pair * LANES, LANES), LANES)
        for s in range(pieces):
            both = acc_ref[s * size : (s + 1) * size, :]
            piece_refs[s][:, k_at] = both[:, :LANES].astype(piece_refs[s].dtype)
            piece_refs[s][:, v_at] = both[:, LANES:].astype(piece_refs[s].dtype)


def merge_kernel(others, mine_ref, dk_ref, dv_ref, own_ref, *refs):
    got = refs[:others]
    cos_ref, sin_ref, dk_out, dv_out = refs[others:]
    width = dk_ref.shape[1]
    cosine, sine = cos_ref[...], sin_ref[...]

    def write(dk, dv):
        for at in range(0, width, LANES):
            part = dk[:, at : at + LANES]
            dk_out[:, at : at + LANES] = (part * cosine - half_swap(part) * sine).astype(BF16)
        dv_out[...] = dv.astype(BF16)

    mine = pl.program_id(0) == mine_ref[0]

    @pl.when(mine)
    def _():
        extra = own_ref[...]
        for ref in got:
            extra = extra + ref[...].astype(F32)
        write(dk_ref[...] + extra[:, :width], dv_ref[...] + extra[:, width:])

    @pl.when(jnp.logical_not(mine))
    def _():
        write(dk_ref[...], dv_ref[...])


def merge_keys(mine, dkey, dvalue, own, got, cosine, sine):
    rows, width = dkey.shape
    row = lambda i, mine: (i, 0)
    full = lambda i, mine: (0, 0)
    return pl.pallas_call(
        functools.partial(merge_kernel, len(got)),
        grid_spec=pltpu.PrefetchScalarGridSpec(
            num_scalar_prefetch=1,
            grid=(rows // CLEN,),
            in_specs=[pl.BlockSpec((CLEN, width), row)] * 2
            + [pl.BlockSpec((CLEN, 2 * width), full)] * (1 + len(got))
            + [pl.BlockSpec((CLEN, LANES), row)] * 2,
            out_specs=[pl.BlockSpec((CLEN, width), row)] * 2,
        ),
        out_shape=[jax.ShapeDtypeStruct((rows, width), BF16)] * 2,
        compiler_params=pltpu.CompilerParams(vmem_limit_bytes=VMEM_LIMIT),
        cost_estimate=pl.CostEstimate(flops=8 * rows * width, bytes_accessed=16 * rows * width, transcendentals=0),
        name="merge_keys",
    )(mine, dkey, dvalue, own, *got, cosine, sine)


def ffn_kernel(count, second_ref, cot_ref, *refs):
    w_refs = refs[:count]
    hidden_ref, dgate_ref, dup_ref = refs[count:]
    depth = w_refs[0].shape[0]
    wide = w_refs[0].shape[1] // 3
    step = min(wide, 256)
    for at in range(0, wide, step):
        gate, upward, dhidden = None, None, None
        for p in range(count):
            cols = slice(p * depth, (p + 1) * depth)
            x, g = second_ref[:, cols], cot_ref[:, cols]
            terms = (
                dot(x, w_refs[p][:, at : at + step], NN),
                dot(x, w_refs[p][:, wide + at : wide + at + step], NN),
                dot(g, w_refs[p][:, 2 * wide + at : 2 * wide + at + step], NN),
            )
            if p == 0:
                gate, upward, dhidden = terms
            else:
                gate, upward, dhidden = gate + terms[0], upward + terms[1], dhidden + terms[2]
        sig = 1.0 / (1.0 + jnp.exp(-gate))
        silu = gate * sig
        hidden_ref[:, at : at + step] = (silu * upward).astype(BF16)
        dup_ref[:, at : at + step] = (dhidden * silu).astype(BF16)
        dgate_ref[:, at : at + step] = (dhidden * upward * (sig + silu * (1.0 - sig))).astype(BF16)


def ffn(second, cotangent, pieces):
    rows, width = second.shape
    wide = pieces[0].shape[1] // 3
    count = len(pieces)
    row = lambda i: (i, 0)
    full = lambda i: (0, 0)
    tile = 256
    return pl.pallas_call(
        functools.partial(ffn_kernel, count),
        grid=(rows // tile,),
        in_specs=[pl.BlockSpec((tile, width), row)] * 2
        + [pl.BlockSpec(p.shape, full, pipeline_mode=pl.Buffered(1)) for p in pieces],
        out_specs=[pl.BlockSpec((tile, wide), row)] * 3,
        out_shape=[jax.ShapeDtypeStruct((rows, wide), BF16)] * 3,
        compiler_params=pltpu.CompilerParams(vmem_limit_bytes=VMEM_LIMIT),
        cost_estimate=pl.CostEstimate(
            flops=6 * rows * width * wide,
            bytes_accessed=2 * (2 * rows * width + 3 * width * wide + 3 * rows * wide),
            transcendentals=rows * wide,
        ),
        name="ffn",
    )(second, cotangent, *pieces)


def back_kernel(sides, count, spans, *refs):
    left_refs = refs[:sides]
    w_refs = refs[sides:-1]
    out_ref = refs[-1]
    depth = w_refs[0].shape[0]
    for p in range(count):
        total = None
        for n, (chunk, start, stop) in enumerate(spans):
            term = dot(left_refs[n][...], w_refs[chunk * count + p][:, start:stop], NT)
            total = term if total is None else total + term
        out_ref[:, p * depth : (p + 1) * depth] = total.astype(BF16)


def project_back(lefts, chunks, spans):
    rows = lefts[0].shape[0]
    count = len(chunks[0])
    width = count * chunks[0][0].shape[0]
    flat = [piece for chunk in chunks for piece in chunk]
    row = lambda i: (i, 0)
    full = lambda i: (0, 0)
    tile = 256
    depth = sum(left.shape[1] for left in lefts)
    return pl.pallas_call(
        functools.partial(back_kernel, len(lefts), count, spans),
        grid=(rows // tile,),
        in_specs=[pl.BlockSpec((tile, left.shape[1]), row) for left in lefts]
        + [pl.BlockSpec(p.shape, full, pipeline_mode=pl.Buffered(1)) for p in flat],
        out_specs=pl.BlockSpec((tile, width), row),
        out_shape=jax.ShapeDtypeStruct((rows, width), BF16),
        compiler_params=pltpu.CompilerParams(vmem_limit_bytes=VMEM_LIMIT),
        cost_estimate=pl.CostEstimate(
            flops=2 * rows * width * depth,
            bytes_accessed=2 * (rows * depth + width * depth + rows * width),
            transcendentals=0,
        ),
        name="project_back",
    )(*lefts, *flat)


def attention_specs(pieces, key_pairs):
    own = pl.BlockSpec((CLEN, LANES), lambda h, j, order, rank: (order[j], h))
    key = pl.BlockSpec((CLEN, LANES), lambda h, j, order, rank: (0, h))
    value = pl.BlockSpec((CLEN, LANES), lambda h, j, order, rank: (0, key_pairs + h))
    trig = pl.BlockSpec((CLEN, LANES), lambda h, j, order, rank: (order[j], 0))
    prompt = pl.BlockSpec((CLEN, 2 * key_pairs * LANES), lambda h, j, order, rank: (0, 0))
    return own, key, value, trig, prompt


def attention_forward(order, rank, query, keys, values, prompts):
    rows, width = query.shape
    pieces, pairs = len(prompts), width // LANES
    own, key, value, _, _ = attention_specs(pieces, pairs)
    scores = rows * (pieces + 1) * CLEN * (width // HEAD_DIM)
    return pl.pallas_call(
        functools.partial(forward_kernel, pieces),
        grid_spec=pltpu.PrefetchScalarGridSpec(
            num_scalar_prefetch=2,
            grid=(pairs, rows // CLEN),
            in_specs=[own] * 3 + [key] * pieces + [value] * pieces,
            out_specs=[own, own],
        ),
        out_shape=[jax.ShapeDtypeStruct((rows, width), BF16), jax.ShapeDtypeStruct((rows, width), F32)],
        compiler_params=pltpu.CompilerParams(vmem_limit_bytes=VMEM_LIMIT),
        cost_estimate=pl.CostEstimate(
            flops=16 * scores * HEAD_DIM, bytes_accessed=16 * rows * width, transcendentals=scores
        ),
        name="attend",
    )(order, rank, query, keys, values, *prompts, *prompts)


def attention_backward(order, rank, query, keys, values, mixed, lse, dmixed, cosine, sine, prompts):
    rows, width = query.shape
    pieces, pairs = len(prompts), width // LANES
    own, key, value, trig, prompt = attention_specs(pieces, pairs)
    scores = rows * (pieces + 1) * CLEN * (width // HEAD_DIM)
    return pl.pallas_call(
        functools.partial(backward_kernel, pieces),
        grid_spec=pltpu.PrefetchScalarGridSpec(
            num_scalar_prefetch=2,
            grid=(pairs, rows // CLEN),
            in_specs=[own] * 6 + [trig] * 2 + [key] * pieces + [value] * pieces,
            out_specs=[own, own, own] + [prompt] * pieces,
            scratch_shapes=[pltpu.VMEM((pieces * CLEN, 2 * LANES), F32)],
        ),
        out_shape=[
            jax.ShapeDtypeStruct((rows, width), BF16),
            jax.ShapeDtypeStruct((rows, width), F32),
            jax.ShapeDtypeStruct((rows, width), F32),
        ]
        + [jax.ShapeDtypeStruct((CLEN, 2 * width), BF16 if s else F32) for s in range(pieces)],
        compiler_params=pltpu.CompilerParams(vmem_limit_bytes=VMEM_LIMIT),
        cost_estimate=pl.CostEstimate(
            flops=40 * scores * HEAD_DIM, bytes_accessed=32 * rows * width, transcendentals=scores
        ),
        name="attend_back",
    )(order, rank, query, keys, values, mixed, lse, dmixed, cosine, sine, *prompts, *prompts)


def normalize(values):
    factor = lax.rsqrt(jnp.mean(values * values, axis=-1, keepdims=True) + EPS)
    return (values * factor, factor)


def rope_tables(where):
    half = HEAD_DIM // 2
    freqs = ROPE_BASE ** (-(jnp.arange(half).astype(F32) * 2.0) / HEAD_DIM)
    angles = where.astype(F32)[:, None] * freqs[None, :]
    cosine, sine = jnp.cos(angles), jnp.sin(angles)
    return (
        jnp.concatenate([cosine] * 4, axis=1),
        jnp.concatenate([-sine, sine, -sine, sine], axis=1),
    )


def matmul_back(left, pieces):
    return jnp.concatenate(
        [jnp.einsum("qf,df->qd", left, p, preferred_element_type=F32) for p in pieces], axis=1
    )


def row_grads(left, right, blocks):
    depth = left.shape[1] // blocks
    return [
        jnp.einsum(
            "tc,tf->cf", left[:, s * depth : (s + 1) * depth], right, preferred_element_type=F32
        ).astype(BF16)
        for s in range(blocks)
    ]


def body(
    tokens,
    attn_gain,
    query_weight,
    key_weight,
    value_weight,
    out_weight,
    ffn_gain,
    gate_weight,
    up_weight,
    down_weight,
    seq_ids,
    positions,
    out_grad,
):
    rows, width = tokens.shape
    head_width = query_weight.shape[1]
    own_rows, ffn_width = gate_weight.shape
    half_units = ffn_width // 2
    chunk = half_units // FFN_CHUNKS
    half = rows // 2
    dp_count = lax.axis_size("dp")
    ctx_count = lax.axis_size("ctx")
    tp_count = lax.axis_size("tp")
    dp_index = lax.axis_index("dp")
    ctx_index = lax.axis_index("ctx")
    tp_index = lax.axis_index("tp")
    bit = tp_index & 1
    parity = ctx_index & 1
    upper = (ctx_index // 2) & 1
    shift = dp_index * (width // dp_count)

    def turned(values, amount=shift):
        doubled = jnp.concatenate([values, values], axis=-1)
        return lax.dynamic_slice_in_dim(doubled, amount, width, values.ndim - 1)

    def natural(values):
        return turned(values, width - shift)

    def flip(values):
        split = values.reshape(values.shape[:-1] + (dp_count, 2, width // dp_count // 2))
        other = split[..., ::-1, :].reshape(values.shape)
        return jnp.where(upper == 0, values, other)

    def row_half(values):
        return lax.dynamic_slice_in_dim(values, bit * half, half)

    def assemble(mine, other):
        first = jnp.where(bit == 0, mine, other)
        last = jnp.where(bit == 0, other, mine)
        return jnp.concatenate([first, last], axis=0)

    def gather_rows(weight):
        return gather_dp(lax.all_gather(weight, "ctx", axis=0, tiled=True))

    k_pieces = gather_rows(key_weight)
    v_pieces = gather_rows(value_weight)
    q_pieces = gather_rows(query_weight)
    o_pieces = gather_rows(out_weight)
    ffn_pieces = []
    for f in range(FFN_CHUNKS):

        def columns(which):
            start = which * half_units + f * chunk
            return jnp.concatenate(
                [
                    lax.dynamic_slice_in_dim(w, start, chunk, 1)
                    for w in (gate_weight, up_weight, down_weight)
                ],
                axis=1,
            )

        keep = columns(parity)
        got = swap(columns(1 - parity), "ctx", 1)
        pair = jnp.concatenate(
            [jnp.where(parity == 0, keep, got), jnp.where(parity == 0, got, keep)], axis=0
        )
        near = gather_dp(pair)
        far = gather_dp(swap(pair, "ctx", 2))
        ffn_pieces.append([p for both in zip(near, far) for p in both])

    group_seq = seq_ids[0].reshape(ctx_count, rows // CLEN, CLEN)[:, :, 0]
    group_pos = positions[0].reshape(ctx_count, rows // CLEN, CLEN)[:, :, 0]
    prompt_at = jnp.argmax(group_seq == 0, axis=1).astype(jnp.int32)
    prompt_rank = jnp.sum(jnp.where(group_seq == 0, group_pos, 0), axis=1).astype(jnp.int32)
    rank = jnp.roll(prompt_rank, -ctx_index)
    mine = prompt_at[ctx_index]
    blocks = jnp.arange(rows // CLEN, dtype=jnp.int32)
    order = jnp.concatenate([mine[None], jnp.sort(jnp.where(blocks == mine, -1, blocks))[1:]])
    own_pos = lax.dynamic_slice_in_dim(positions[0], ctx_index * rows, rows)
    cosine, sine = rope_tables(own_pos)

    inputs_low = turned(tokens)
    cotangent_low = turned(out_grad)
    gain_one = turned(attn_gain).astype(F32)
    gain_two = turned(ffn_gain).astype(F32)
    first_norm, first_scale = normalize(inputs_low.astype(F32))
    first = low(first_norm * gain_one)

    keys = project(first, k_pieces, cosine, sine, True)
    values = project(first, v_pieces, cosine, sine, False)
    prompt_own = jnp.concatenate(
        [
            lax.dynamic_slice_in_dim(keys, mine * CLEN, CLEN),
            lax.dynamic_slice_in_dim(values, mine * CLEN, CLEN),
        ],
        axis=1,
    )
    prompts = [prompt_own] + [fetch(prompt_own, "ctx", s) for s in range(1, ctx_count)]
    query = project(first, q_pieces, cosine, sine, True)
    mixed, lse = attention_forward(order, rank, query, keys, values, prompts)

    def sum_halves(part):
        return low(add(row_half(part), swap(lax.dynamic_slice_in_dim(part, (1 - bit) * half, half), "tp", 1)))

    mixed_out = sum_halves(low(matmul_back(mixed, o_pieces)))
    inputs_half = row_half(inputs_low).astype(F32)
    middle = inputs_half + add(mixed_out, swap(mixed_out, "tp", 2))
    second_norm, second_scale = normalize(middle)
    second_half = flip(low(second_norm * gain_two))

    def spread(values_half):
        other = swap(values_half, "tp", 1)
        far = swap(values_half, "ctx", 1)
        far_other = swap(far, "tp", 1)
        return [
            jnp.concatenate([values_half, other], axis=0),
            jnp.concatenate([far, far_other], axis=0),
        ]

    seconds = spread(second_half)
    cotangent_half = row_half(cotangent_low)
    cotangents = spread(flip(cotangent_half))
    hiddens, dgates, dups = [], [], []
    for side in range(2):
        made = [ffn(seconds[side], cotangents[side], pieces) for pieces in ffn_pieces]
        hiddens.append([m[0] for m in made])
        dgates.append([m[1] for m in made])
        dups.append([m[2] for m in made])
    gate_spans = tuple((f, 0, chunk) for f in range(FFN_CHUNKS)) + tuple(
        (f, chunk, 2 * chunk) for f in range(FFN_CHUNKS)
    )
    down_spans = tuple((f, 2 * chunk, 3 * chunk) for f in range(FFN_CHUNKS))

    def collect(parts):
        near, far = [
            low(add(part[:half], swap(part[half:], "tp", 1))) for part in parts
        ]
        return low(flip(add(near, swap(far, "ctx", 1))))

    dsecond_parts = [
        project_back(dgates[side] + dups[side], ffn_pieces, gate_spans) for side in (1, 0)
    ][::-1]
    dsecond = collect(dsecond_parts)
    dsecond = add(dsecond, swap(dsecond, "tp", 2))

    ffn_grads = []
    for f in range(FFN_CHUNKS):
        left = jnp.concatenate(seconds, axis=0)
        left_cot = jnp.concatenate(cotangents, axis=0)
        grads = [
            jnp.concatenate(terms, axis=1)
            for terms in zip(
                row_grads(left, jnp.concatenate([dgates[0][f], dgates[1][f]], axis=0), dp_count),
                row_grads(left, jnp.concatenate([dups[0][f], dups[1][f]], axis=0), dp_count),
                row_grads(left_cot, jnp.concatenate([hiddens[0][f], hiddens[1][f]], axis=0), dp_count),
            )
        ]
        block = scatter_dp(grads)
        pair_rows = block.shape[0] // 2
        pair = add(block[:pair_rows], swap(block[pair_rows:], "ctx", 2))
        kept = lax.dynamic_slice_in_dim(pair, parity * own_rows, own_rows)
        given = lax.dynamic_slice_in_dim(low(pair), (1 - parity) * own_rows, own_rows)
        got = swap(given, "ctx", 1).astype(F32)
        ffn_grads.append((jnp.where(parity == 0, kept, got), jnp.where(parity == 0, got, kept)))

    gain_two_grad = jnp.sum(dsecond * second_norm, axis=0)
    scaled_two = dsecond * gain_two
    dmiddle = cotangent_half.astype(F32) + second_scale * (
        scaled_two - second_norm * jnp.mean(scaled_two * second_norm, axis=-1, keepdims=True)
    )
    dmiddle_half = low(dmiddle)
    dmiddle_low = assemble(dmiddle_half, swap(dmiddle_half, "tp", 1))
    dmixed = project(dmiddle_low, o_pieces, cosine, sine, False)
    dquery_low, dkey_own, dvalue_own, dprompt_own, *dprompts = attention_backward(
        order, rank, query, keys, values, mixed, lse, dmixed, cosine, sine, prompts
    )
    got = [send(piece, "ctx", s + 1) for s, piece in enumerate(dprompts)]
    dkey_low, dvalue_low = merge_keys(
        mine[None], dkey_own, dvalue_own, dprompt_own, got, cosine, sine
    )

    def attn_grads(pairs):
        grads = [
            jnp.concatenate(terms, axis=1)
            for terms in zip(*[row_grads(left, right, dp_count) for left, right in pairs])
        ]
        return lax.psum_scatter(scatter_dp(grads), "ctx", scatter_dimension=0, tiled=True).astype(F32)

    early = attn_grads([(dmiddle_low, mixed), (first, dquery_low)])
    late = attn_grads([(first, dkey_low), (first, dvalue_low)])

    dfirst_part = project_back(
        [dquery_low, dkey_low, dvalue_low],
        [q_pieces, k_pieces, v_pieces],
        ((0, 0, head_width), (1, 0, head_width), (2, 0, head_width)),
    )
    dfirst = sum_halves(dfirst_part)
    dfirst = add(dfirst, swap(dfirst, "tp", 2))
    norm_half = row_half(first_norm)
    gain_one_grad = jnp.sum(dfirst * norm_half, axis=0)
    scaled_one = dfirst * gain_one
    dinputs = dmiddle + row_half(first_scale) * (
        scaled_one - norm_half * jnp.mean(scaled_one * norm_half, axis=-1, keepdims=True)
    )

    share = width // tp_count

    def deliver(values_half):
        wide = lax.dynamic_slice_in_dim(values_half, (tp_index // 2) * 2 * share, 2 * share, 1)
        kept = lax.dynamic_slice_in_dim(wide, bit * share, share, 1)
        given = lax.dynamic_slice_in_dim(wide, (1 - bit) * share, share, 1)
        return assemble(kept, swap(given, "tp", 1))

    in_grad = deliver(natural(low(dinputs)))

    ffn_parts = [project_back(hiddens[side], ffn_pieces, down_spans) for side in (1, 0)][::-1]
    ffn_out = natural(collect(ffn_parts))
    top = (tp_index // 2) * 2 * share
    kept = lax.dynamic_slice_in_dim(ffn_out, top, 2 * share, 1)
    given = lax.dynamic_slice_in_dim(ffn_out, 2 * share - top, 2 * share, 1)
    ffn_out = add(kept, swap(given, "tp", 2))
    out_wide = low(lax.dynamic_slice_in_dim(natural(middle), top, 2 * share, 1) + ffn_out)
    kept = lax.dynamic_slice_in_dim(out_wide, bit * share, share, 1)
    given = lax.dynamic_slice_in_dim(out_wide, (1 - bit) * share, share, 1)
    block_out = assemble(kept, swap(given, "tp", 1))

    gains = natural(jnp.stack([gain_one_grad, gain_two_grad]))
    gains = gains + swap(gains, "tp", 1)
    for axis in ("ctx", "dp"):
        mask = 1
        while mask < lax.axis_size(axis):
            gains = gains + swap(gains, axis, mask)
            mask *= 2
    part = width // (dp_count * ctx_count)
    gains = lax.dynamic_slice_in_dim(gains, (dp_index * ctx_count + ctx_index) * part, part, 1)

    ffn_final = [
        jnp.concatenate(
            [
                ffn_grads[f][side][:, i * chunk : (i + 1) * chunk]
                for side in range(2)
                for f in range(FFN_CHUNKS)
            ],
            axis=1,
        )
        for i in range(3)
    ]
    return (
        block_out,
        in_grad,
        gains[0],
        early[:, head_width:],
        late[:, :head_width],
        late[:, head_width:],
        early[:, :head_width],
        gains[1],
        ffn_final[0],
        ffn_final[1],
        ffn_final[2],
    )


def solution(mesh):
    split = P(("dp", "ctx"), "tp")
    rows = P(("dp", "ctx"), None)
    vector = P(("dp", "ctx"))
    return jax.shard_map(
        body,
        mesh=mesh,
        in_specs=(rows, P(), split, split, split, split, P(), split, split, split)
        + (P("dp", None), P("dp", None), rows),
        out_specs=(split, split, vector, split, split, split, split, vector, split, split, split),
        check_vma=False,
    )
```

```python
import functools
import math

import jax
import jax.numpy as jnp
from jax import lax
from jax.experimental import pallas as pl
from jax.experimental.pallas import tpu as pltpu
from jax.sharding import Mesh
from jax.sharding import PartitionSpec as P

HEAD_DIM = 64
CLEN = 256
LANES = 128
EPS = 1e-05
ROPE_BASE = 130000.0
MASKED = -1e30
FFN_CHUNKS = 2
COST_SCALE = 16
BF16 = jnp.bfloat16
F32 = jnp.float32
VMEM_LIMIT = 32 * 1024 * 1024
CTX = ("hi", "lo")


def swap(values, axis, mask=1):
    count = lax.axis_size(axis)
    return lax.ppermute(values, axis, [(i, i ^ mask) for i in range(count)])


def turn(values, axis, shift):
    count = lax.axis_size(axis)
    return lax.ppermute(values, axis, [(i, (i + shift) % count) for i in range(count)])


def add(left, right):
    return left.astype(F32) + right.astype(F32)


def low(values):
    return values.astype(BF16)


def after(values, *needed):
    return lax.optimization_barrier((values,) + needed)[0]


def cost(flops, data, transcendentals=0):
    return pl.CostEstimate(
        flops=flops // COST_SCALE,
        bytes_accessed=data // COST_SCALE,
        transcendentals=transcendentals // COST_SCALE,
    )


def dot(left, right, dims):
    return lax.dot_general(left, right, (dims, ((), ())), preferred_element_type=F32)


NN = ((1,), (0,))
NT = ((1,), (1,))
TN = ((0,), (0,))
VMEM = pl.BlockSpec(memory_space=pltpu.VMEM)
SMEM = pl.BlockSpec(memory_space=pltpu.SMEM)


def at_block(index, size):
    return pl.ds(pl.multiple_of(index * size, size), size)


def half_swap(values):
    lane = lax.broadcasted_iota(jnp.int32, values.shape, 1)
    ahead = pltpu.roll(values, LANES - 32, 1)
    behind = pltpu.roll(values, 32, 1)
    return jnp.where((lane & 63) < 32, ahead, behind)


def call(kernel, operands, out_shape, name, flops, data, scratch=(), smem=(), transcendentals=0):
    many = isinstance(out_shape, list)
    return pl.pallas_call(
        kernel,
        in_specs=[SMEM] * len(smem) + [VMEM] * len(operands),
        out_specs=[VMEM] * len(out_shape) if many else VMEM,
        out_shape=out_shape,
        scratch_shapes=list(scratch),
        compiler_params=pltpu.CompilerParams(vmem_limit_bytes=VMEM_LIMIT),
        cost_estimate=cost(flops, data, transcendentals),
        name=name,
    )(*smem, *operands)


def fill(whole, pieces, place_ref, unit, column, width):
    at = 0
    for piece in pieces:
        for row in range(0, piece.shape[0], unit):
            whole[at_block(place_ref[at], unit), :] = piece[
                row : row + unit, column : column + width
            ]
            at += 1


def project_kernel(parts, column, width, rope_width, bit_ref, place_ref, *refs):
    x_refs = refs[:parts]
    w_refs = refs[parts:-5]
    cos_ref, sin_ref, out_ref, x_all, w_all = refs[-5:]
    fill(w_all, w_refs, place_ref, w_all.shape[0] // place_ref.shape[0], column, width)
    if parts == 2:
        rows = x_refs[0].shape[0]
        x_all[at_block(bit_ref[0], rows), :] = x_refs[0][...]
        x_all[at_block(1 - bit_ref[0], rows), :] = x_refs[1][...]
        x_ref = x_all
    else:
        x_ref = x_refs[0]
    tile = min(width, 256)

    def columns(first, rope):
        def step(t, carry):
            at = pl.multiple_of(first + t * tile, tile)
            total = dot(x_ref[...], w_all[:, pl.ds(at, tile)], NN)
            for c in range(0, tile, LANES):
                part = total[:, c : c + LANES]
                if rope:
                    part = part * cos_ref[...] + half_swap(part) * sin_ref[...]
                out_ref[:, pl.ds(pl.multiple_of(at + c, LANES), LANES)] = part.astype(BF16)
            return carry

        return step

    if rope_width:
        lax.fori_loop(0, rope_width // tile, columns(0, True), 0)
    if rope_width < width:
        lax.fori_loop(0, (width - rope_width) // tile, columns(rope_width, False), 0)


def project(x_parts, stack, places, bit, column, width, cosine, sine, rope_width):
    rows = sum(x.shape[0] for x in x_parts)
    depth = x_parts[0].shape[1]
    return call(
        functools.partial(project_kernel, len(x_parts), column, width, rope_width),
        [*x_parts, *stack, cosine, sine],
        jax.ShapeDtypeStruct((rows, width), BF16),
        "project",
        2 * rows * depth * width,
        2 * (rows * depth + depth * width + rows * width),
        [
            pltpu.VMEM((rows if len(x_parts) == 2 else 16, depth), BF16),
            pltpu.VMEM((depth, width), BF16),
        ],
        [bit, places],
    )


def place_kernel(count, place_ref, *refs):
    out_ref = refs[-1]
    unit = out_ref.shape[0] // count
    at = 0
    for ref in refs[:-1]:
        for row in range(0, ref.shape[0], unit):
            out_ref[at_block(place_ref[at], unit), :] = ref[row : row + unit, :]
            at += 1


def place_rows(pieces, places):
    rows, width = sum(p.shape[0] for p in pieces), pieces[0].shape[1]
    return call(
        functools.partial(place_kernel, places.shape[0]),
        pieces,
        jax.ShapeDtypeStruct((rows, width), BF16),
        "place_rows",
        0,
        4 * rows * width,
        smem=[places],
    )


def ffn_kernel(chunks, *refs):
    x_refs, cot_refs = refs[:2], refs[2:4]
    w_refs = refs[4 : 4 + chunks]
    hidden_ref, dpair_ref = refs[4 + chunks :]
    rows = x_refs[0].shape[0]
    wide = w_refs[0].shape[1] // 3
    tile = min(wide, 256)
    for f, w_ref in enumerate(w_refs):

        def step(t, carry, f=f, w_ref=w_ref):
            for part in range(2):
                x, g = x_refs[part][...], cot_refs[part][...]
                gate = dot(x, w_ref[:, pl.ds(pl.multiple_of(t * tile, tile), tile)], NN)
                upward = dot(x, w_ref[:, pl.ds(pl.multiple_of(wide + t * tile, tile), tile)], NN)
                dhidden = dot(g, w_ref[:, pl.ds(pl.multiple_of(2 * wide + t * tile, tile), tile)], NN)
                sig = 1.0 / (1.0 + jnp.exp(-gate))
                silu = gate * sig
                at = slice(part * rows, (part + 1) * rows)
                hidden_ref[at, pl.ds(pl.multiple_of(f * wide + t * tile, tile), tile)] = (
                    silu * upward
                ).astype(BF16)
                dpair_ref[at, pl.ds(pl.multiple_of(2 * f * wide + t * tile, tile), tile)] = (
                    dhidden * upward * (sig + silu * (1.0 - sig))
                ).astype(BF16)
                dpair_ref[at, pl.ds(pl.multiple_of((2 * f + 1) * wide + t * tile, tile), tile)] = (
                    dhidden * silu
                ).astype(BF16)
            return carry

        lax.fori_loop(0, wide // tile, step, 0)


def ffn(seconds, cotangents, weights):
    rows = 2 * seconds[0].shape[0]
    width = seconds[0].shape[1]
    units = sum(w.shape[1] for w in weights) // 3
    return call(
        functools.partial(ffn_kernel, len(weights)),
        [*seconds, *cotangents, *weights],
        [jax.ShapeDtypeStruct((rows, units), BF16), jax.ShapeDtypeStruct((rows, 2 * units), BF16)],
        "ffn",
        6 * rows * width * units,
        2 * (2 * rows * width + 3 * width * units + 3 * rows * units),
        transcendentals=rows * units,
    )


def back_kernel(spans, *refs):
    count = 1 + max(span[2] for span in spans)
    lefts = refs[: 1 + max(span[0] for span in spans)]
    rights = refs[len(lefts) : len(lefts) + count]
    outs = refs[len(lefts) + count :]
    rows, width = outs[0].shape
    tile = 256

    def step(t, carry):
        for part, out_ref in enumerate(outs):
            total = None
            for left, l_at, right, r_at, wide in spans:
                term = dot(
                    lefts[left][part * rows : (part + 1) * rows, l_at : l_at + wide],
                    rights[right][at_block(t, tile), r_at : r_at + wide],
                    NT,
                )
                total = term if total is None else total + term
            out_ref[:, at_block(t, tile)] = total.astype(BF16)
        return carry

    lax.fori_loop(0, width // tile, step, 0)


def ffn_back(lefts, weights, spans):
    rows = lefts[0].shape[0]
    width = weights[0].shape[0]
    depth = sum(span[4] for span in spans)
    return call(
        functools.partial(back_kernel, spans),
        [*lefts, *weights],
        [jax.ShapeDtypeStruct((rows // 2, width), BF16)] * 2,
        "ffn_back",
        2 * rows * width * depth,
        2 * (rows * depth + width * depth + rows * width),
    )


def project_back_kernel(columns, counts, bit_ref, place_ref, *refs):
    lefts = refs[: len(columns)]
    at, stacks = len(columns), []
    for count in counts:
        stacks.append(refs[at : at + count])
        at += count
    outs, w_all = refs[at : at + 2], refs[at + 2]
    rows, width = outs[0].shape
    unit = width // place_ref.shape[0]
    wide = lefts[0].shape[1]
    for n, (which, column) in enumerate(columns):
        at = 0
        for piece in stacks[which]:
            for row in range(0, piece.shape[0], unit):
                w_all[at_block(place_ref[at], unit), n * wide : (n + 1) * wide] = piece[
                    row : row + unit, column : column + wide
                ]
                at += 1
    tile = 256

    def step(t, carry):
        for part, out_ref in enumerate(outs):
            which = bit_ref[0] if part == 0 else 1 - bit_ref[0]
            total = None
            for n, left in enumerate(lefts):
                term = dot(
                    left[at_block(which, rows), :],
                    w_all[at_block(t, tile), n * wide : (n + 1) * wide],
                    NT,
                )
                total = term if total is None else total + term
            out_ref[:, at_block(t, tile)] = total.astype(BF16)
        return carry

    lax.fori_loop(0, width // tile, step, 0)


def project_back(lefts, columns, stacks, places, bit):
    rows, wide = lefts[0].shape
    width = sum(piece.shape[0] for piece in stacks[0])
    depth = wide * len(lefts)
    return call(
        functools.partial(project_back_kernel, columns, tuple(len(s) for s in stacks)),
        [*lefts, *[piece for stack in stacks for piece in stack]],
        [jax.ShapeDtypeStruct((rows // 2, width), BF16)] * 2,
        "project_back",
        2 * rows * width * depth,
        2 * (rows * depth + width * depth + rows * width),
        [pltpu.VMEM((width, depth), BF16)],
        [bit, places],
    )


def store_blocks(out_ref, values, first, unit, slot_ref, column):
    wide = values.shape[1]
    for row in range(0, values.shape[0], unit):
        slot = slot_ref[(first + row) // unit]
        out_ref[at_block(slot, unit), column : column + wide] = values[row : row + unit]


def ffn_grads_kernel(s, unit, dp_ref, slot_ref, *refs):
    x_refs, cot_refs = refs[:4], refs[4:8]
    hiddens, dpairs, out_ref = refs[8:10], refs[10:12], refs[12]
    rows = x_refs[0].shape[0]
    wide = hiddens[0].shape[1]
    count = out_ref.shape[0]
    tile = 256

    def step(t, carry):
        where = pl.ds(pl.multiple_of(dp_ref[s] * count + t * tile, tile), tile)

        def product(lefts, rights):
            total = None
            for n, left in enumerate(lefts):
                part = slice((n % 2) * rows, (n % 2 + 1) * rows)
                term = dot(left[:, where], rights[n // 2][part, :], TN)
                total = term if total is None else total + term
            return total.astype(BF16)

        store_blocks(out_ref, product(x_refs, dpairs), t * tile, unit, slot_ref, 0)
        store_blocks(out_ref, product(cot_refs, hiddens), t * tile, unit, slot_ref, 2 * wide)
        return carry

    lax.fori_loop(0, count // tile, step, 0)


def ffn_grads(seconds, cotangents, hiddens, dpairs, owners, slots, s, count, unit):
    wide = hiddens[0].shape[1]
    rows = 4 * seconds[0].shape[0]
    return call(
        functools.partial(ffn_grads_kernel, s, unit),
        [*seconds, *cotangents, *hiddens, *dpairs],
        jax.ShapeDtypeStruct((count, 3 * wide), BF16),
        "ffn_grads",
        6 * rows * count * wide,
        2 * (2 * rows * count + 3 * rows * wide + 3 * count * wide),
        smem=[owners, slots],
    )


def attn_grads_kernel(kinds, s, unit, bit_ref, dp_ref, slot_ref, *refs):
    at, pairs = 0, []
    for parts in kinds:
        pairs.append((refs[at : at + parts], refs[at + parts]))
        at += parts + 1
    out_ref = refs[at]
    count = out_ref.shape[0]
    tile = 256

    def step(t, carry):
        where = pl.ds(pl.multiple_of(dp_ref[s] * count + t * tile, tile), tile)
        column = 0
        for lefts, right in pairs:
            if len(lefts) == 1:
                total = dot(lefts[0][:, where], right[...], TN)
            else:
                rows = lefts[0].shape[0]
                total = dot(lefts[0][:, where], right[at_block(bit_ref[0], rows), :], TN) + dot(
                    lefts[1][:, where], right[at_block(1 - bit_ref[0], rows), :], TN
                )
            store_blocks(out_ref, total.astype(BF16), t * tile, unit, slot_ref, column)
            column += right.shape[1]
        return carry

    lax.fori_loop(0, count // tile, step, 0)


def attn_grads_block(pairs, bit, owners, slots, s, count, unit):
    kinds = tuple(len(lefts) for lefts, _ in pairs)
    width = sum(right.shape[1] for _, right in pairs)
    rows = pairs[0][1].shape[0]
    return call(
        functools.partial(attn_grads_kernel, kinds, s, unit),
        [x for lefts, right in pairs for x in (*lefts, right)],
        jax.ShapeDtypeStruct((count, width), BF16),
        "attn_grads",
        2 * rows * width * count,
        2 * (rows * count + rows * width + count * width),
        smem=[bit, owners, slots],
    )


SCALE = HEAD_DIM**-0.5
SCALE_LOG2 = SCALE * math.log2(math.e)


def forward_kernel(pieces, order_ref, rank_ref, q_ref, ks_ref, vs_ref, *refs):
    kp_refs, vp_refs = refs[:pieces], refs[pieces : 2 * pieces]
    o_ref, lse_ref = refs[2 * pieces :]
    q = q_ref[...]
    size = q.shape[0]
    prompt = pl.program_id(1) == 0
    low_lane = lax.broadcasted_iota(jnp.int32, q.shape, 1) < HEAD_DIM
    causal = lax.broadcasted_iota(jnp.int32, (size, size), 0) >= lax.broadcasted_iota(
        jnp.int32, (size, size), 1
    )
    outs = []
    for head in range(2):
        own = low_lane if head == 0 else jnp.logical_not(low_lane)
        qh = jnp.where(own, q, jnp.zeros_like(q))
        raw = [jnp.where(causal, dot(qh, ks_ref[...], NT), MASKED)]
        for s in range(pieces):
            hidden = jnp.logical_and(prompt, rank_ref[s] >= rank_ref[0])
            raw.append(dot(qh, kp_refs[s][...], NT) + jnp.where(hidden, MASKED, 0.0))
        top = raw[0]
        for r in raw[1:]:
            top = jnp.maximum(top, r)
        top = jnp.max(top, axis=-1, keepdims=True) * SCALE_LOG2
        sums, acc = None, None
        for s, r in enumerate(raw):
            e = jnp.exp2(r * SCALE_LOG2 - top)
            v = vs_ref if s == 0 else vp_refs[s - 1]
            term = dot(e.astype(BF16), v[...], NN)
            sums = e if sums is None else sums + e
            acc = term if acc is None else acc + term
        total = jnp.sum(sums, axis=-1, keepdims=True)
        outs.append((acc / total, top + jnp.log2(total)))
    o_ref[...] = jnp.where(low_lane, outs[0][0], outs[1][0]).astype(BF16)
    lse_ref[...] = jnp.where(low_lane, outs[0][1], outs[1][1])


def backward_kernel(
    pieces, order_ref, rank_ref, q_ref, ks_ref, vs_ref, o_ref, lse_ref, do_ref, cos_ref, sin_ref, *refs
):
    kp_refs, vp_refs = refs[:pieces], refs[pieces : 2 * pieces]
    dq_ref, dks_ref, dvs_ref = refs[2 * pieces : 2 * pieces + 3]
    piece_refs = refs[2 * pieces + 3 : 3 * pieces + 3]
    acc_ref = refs[-1]
    pair, step = pl.program_id(0), pl.program_id(1)
    prompt = step == 0
    q, do = q_ref[...], do_ref[...]
    size = q.shape[0]
    low_lane = lax.broadcasted_iota(jnp.int32, q.shape, 1) < HEAD_DIM
    causal = lax.broadcasted_iota(jnp.int32, (size, size), 0) >= lax.broadcasted_iota(
        jnp.int32, (size, size), 1
    )
    product = do.astype(F32) * o_ref[...].astype(F32)
    lse = lse_ref[...]
    dq_heads = []
    dk_all = [None] * (pieces + 1)
    dv_all = [None] * (pieces + 1)
    for head in range(2):
        own = low_lane if head == 0 else jnp.logical_not(low_lane)
        qh = jnp.where(own, q, jnp.zeros_like(q))
        doh = jnp.where(own, do, jnp.zeros_like(do))
        delta = jnp.sum(jnp.where(own, product, 0.0), axis=-1, keepdims=True)
        log_sum = lse[:, head * HEAD_DIM : head * HEAD_DIM + 1]
        dq = None
        for s in range(pieces + 1):
            k = (ks_ref if s == 0 else kp_refs[s - 1])[...]
            v = (vs_ref if s == 0 else vp_refs[s - 1])[...]
            raw = dot(qh, k, NT)
            if s == 0:
                raw = jnp.where(causal, raw, MASKED)
            else:
                hidden = jnp.logical_and(prompt, rank_ref[s - 1] >= rank_ref[0])
                raw = raw + jnp.where(hidden, MASKED, 0.0)
            prob = jnp.exp2(raw * SCALE_LOG2 - log_sum)
            ds = (prob * (dot(doh, v, NT) - delta)).astype(BF16)
            term = dot(ds, k, NN)
            dq = term if dq is None else dq + term
            dk = dot(ds, qh, TN)
            dv = dot(prob.astype(BF16), doh, TN)
            dk_all[s] = dk if dk_all[s] is None else dk_all[s] + dk
            dv_all[s] = dv if dv_all[s] is None else dv_all[s] + dv
        dq_heads.append(dq)
    dq = jnp.where(low_lane, dq_heads[0], dq_heads[1]) * SCALE
    cosine, sine = cos_ref[...], sin_ref[...]
    dq_ref[...] = (dq * cosine - half_swap(dq) * sine).astype(BF16)
    dks_ref[...] = dk_all[0] * SCALE
    dvs_ref[...] = dv_all[0]
    for s in range(pieces):
        both = jnp.concatenate([dk_all[s + 1] * SCALE, dv_all[s + 1]], axis=1)
        at = slice(s * size, (s + 1) * size)

        @pl.when(prompt)
        def _(both=both, at=at):
            acc_ref[at, :] = both

        @pl.when(jnp.logical_not(prompt))
        def _(both=both, at=at):
            acc_ref[at, :] += both

    @pl.when(step == pl.num_programs(1) - 1)
    def _():
        wide = piece_refs[0].shape[1] // 2
        k_at = pl.ds(pl.multiple_of(pair * LANES, LANES), LANES)
        v_at = pl.ds(pl.multiple_of(wide + pair * LANES, LANES), LANES)
        for s in range(pieces):
            both = acc_ref[s * size : (s + 1) * size, :]
            piece_refs[s][:, k_at] = both[:, :LANES].astype(piece_refs[s].dtype)
            piece_refs[s][:, v_at] = both[:, LANES:].astype(piece_refs[s].dtype)


def merge_kernel(others, mine_ref, dk_ref, dv_ref, own_ref, *refs):
    got = refs[:others]
    cos_ref, sin_ref, dk_out, dv_out = refs[others:]
    width = dk_ref.shape[1]
    cosine, sine = cos_ref[...], sin_ref[...]

    def write(dk, dv):
        for at in range(0, width, LANES):
            part = dk[:, at : at + LANES]
            dk_out[:, at : at + LANES] = (part * cosine - half_swap(part) * sine).astype(BF16)
        dv_out[...] = dv.astype(BF16)

    mine = pl.program_id(0) == mine_ref[0]

    @pl.when(mine)
    def _():
        extra = own_ref[...]
        for ref in got:
            extra = extra + ref[...].astype(F32)
        write(dk_ref[...] + extra[:, :width], dv_ref[...] + extra[:, width:])

    @pl.when(jnp.logical_not(mine))
    def _():
        write(dk_ref[...], dv_ref[...])


def merge_keys(mine, dkey, dvalue, own, got, cosine, sine):
    rows, width = dkey.shape
    row = lambda i, mine: (i, 0)
    full = lambda i, mine: (0, 0)
    return pl.pallas_call(
        functools.partial(merge_kernel, len(got)),
        grid_spec=pltpu.PrefetchScalarGridSpec(
            num_scalar_prefetch=1,
            grid=(rows // CLEN,),
            in_specs=[pl.BlockSpec((CLEN, width), row)] * 2
            + [pl.BlockSpec((CLEN, 2 * width), full)] * (1 + len(got))
            + [pl.BlockSpec((CLEN, LANES), row)] * 2,
            out_specs=[pl.BlockSpec((CLEN, width), row)] * 2,
        ),
        out_shape=[jax.ShapeDtypeStruct((rows, width), BF16)] * 2,
        compiler_params=pltpu.CompilerParams(vmem_limit_bytes=VMEM_LIMIT),
        cost_estimate=cost(8 * rows * width, 16 * rows * width, 0),
        name="merge_keys",
    )(mine, dkey, dvalue, own, *got, cosine, sine)


def attention_specs(pieces, key_pairs):
    own = pl.BlockSpec((CLEN, LANES), lambda h, j, order, rank: (order[j], h))
    own_value = pl.BlockSpec((CLEN, LANES), lambda h, j, order, rank: (order[j], key_pairs + h))
    key = pl.BlockSpec((CLEN, LANES), lambda h, j, order, rank: (0, h))
    value = pl.BlockSpec((CLEN, LANES), lambda h, j, order, rank: (0, key_pairs + h))
    trig = pl.BlockSpec((CLEN, LANES), lambda h, j, order, rank: (order[j], 0))
    prompt = pl.BlockSpec((CLEN, 2 * key_pairs * LANES), lambda h, j, order, rank: (0, 0))
    return own, own_value, key, value, trig, prompt


def attention_forward(order, rank, query, kv, prompts):
    rows, width = query.shape
    pieces, pairs = len(prompts), width // LANES
    own, own_value, key, value, _, _ = attention_specs(pieces, pairs)
    scores = rows * (pieces + 1) * CLEN * (width // HEAD_DIM)
    return pl.pallas_call(
        functools.partial(forward_kernel, pieces),
        grid_spec=pltpu.PrefetchScalarGridSpec(
            num_scalar_prefetch=2,
            grid=(pairs, rows // CLEN),
            in_specs=[own, own, own_value] + [key] * pieces + [value] * pieces,
            out_specs=[own, own],
        ),
        out_shape=[jax.ShapeDtypeStruct((rows, width), BF16), jax.ShapeDtypeStruct((rows, width), F32)],
        compiler_params=pltpu.CompilerParams(vmem_limit_bytes=VMEM_LIMIT),
        cost_estimate=cost(
            16 * scores * HEAD_DIM, 16 * rows * width, scores
        ),
        name="attend",
    )(order, rank, query, kv, kv, *prompts, *prompts)


def attention_backward(order, rank, query, kv, mixed, lse, dmixed, cosine, sine, prompts):
    rows, width = query.shape
    pieces, pairs = len(prompts), width // LANES
    own, own_value, key, value, trig, prompt = attention_specs(pieces, pairs)
    scores = rows * (pieces + 1) * CLEN * (width // HEAD_DIM)
    return pl.pallas_call(
        functools.partial(backward_kernel, pieces),
        grid_spec=pltpu.PrefetchScalarGridSpec(
            num_scalar_prefetch=2,
            grid=(pairs, rows // CLEN),
            in_specs=[own, own, own_value, own, own, own] + [trig] * 2 + [key] * pieces + [value] * pieces,
            out_specs=[own, own, own] + [prompt] * pieces,
            scratch_shapes=[pltpu.VMEM((pieces * CLEN, 2 * LANES), F32)],
        ),
        out_shape=[
            jax.ShapeDtypeStruct((rows, width), BF16),
            jax.ShapeDtypeStruct((rows, width), F32),
            jax.ShapeDtypeStruct((rows, width), F32),
        ]
        + [jax.ShapeDtypeStruct((CLEN, 2 * width), BF16 if s else F32) for s in range(pieces)],
        compiler_params=pltpu.CompilerParams(vmem_limit_bytes=VMEM_LIMIT),
        cost_estimate=cost(
            40 * scores * HEAD_DIM, 32 * rows * width, scores
        ),
        name="attend_back",
    )(order, rank, query, kv, kv, mixed, lse, dmixed, cosine, sine, *prompts, *prompts)


def normalize(values):
    factor = lax.rsqrt(jnp.mean(values * values, axis=-1, keepdims=True) + EPS)
    return (values * factor, factor)


def rope_tables(where):
    half = HEAD_DIM // 2
    freqs = ROPE_BASE ** (-(jnp.arange(half).astype(F32) * 2.0) / HEAD_DIM)
    angles = where.astype(F32)[:, None] * freqs[None, :]
    cosine, sine = jnp.cos(angles), jnp.sin(angles)
    return (
        jnp.concatenate([cosine] * 4, axis=1),
        jnp.concatenate([-sine, sine, -sine, sine], axis=1),
    )


def body(
    tokens,
    attn_gain,
    query_weight,
    key_weight,
    value_weight,
    out_weight,
    ffn_gain,
    gate_weight,
    up_weight,
    down_weight,
    seq_ids,
    positions,
    out_grad,
):
    rows, width = tokens.shape
    head_width = query_weight.shape[1]
    own_rows, ffn_width = gate_weight.shape
    half_units = ffn_width // 2
    chunk = half_units // FFN_CHUNKS
    half = rows // 2
    dp_count = lax.axis_size("dp")
    ctx_count = lax.axis_size("hi") * 2
    tp_count = lax.axis_size("tp")
    dp_index = lax.axis_index("dp")
    parity = lax.axis_index("lo")
    ctx_index = lax.axis_index("hi") * 2 + parity
    tp_index = lax.axis_index("tp")
    bit = tp_index & 1
    bit_ref = bit.astype(jnp.int32)[None]

    def row_half(values, which=bit):
        return lax.dynamic_slice_in_dim(values, which * half, half)

    def assemble(mine, other):
        first = jnp.where(bit == 0, mine, other)
        last = jnp.where(bit == 0, other, mine)
        return jnp.concatenate([first, last], axis=0)

    slots = jnp.arange(dp_count * ctx_count, dtype=jnp.int32)

    def places_of(order_k):
        slot_k = jnp.array(order_k, jnp.int32)[slots % ctx_count]
        return (
            lax.rem(dp_index + slots // ctx_count, dp_count) * ctx_count + (ctx_index ^ slot_k)
        ).astype(jnp.int32)

    def slots_of(order_k):
        slot_of = jnp.array([order_k.index(k) for k in range(ctx_count)], jnp.int32)
        return slot_of[ctx_index ^ jnp.arange(ctx_count, dtype=jnp.int32)]

    attn_order, ffn_order = (0, 2, 1, 3), (0, 1, 2, 3)
    places, places_ffn = places_of(attn_order), places_of(ffn_order)
    slots_attn, slots_ffn = slots_of(attn_order), slots_of(ffn_order)
    owners = lax.rem(dp_index + jnp.arange(dp_count, dtype=jnp.int32), dp_count).astype(jnp.int32)
    near_rows = width // dp_count

    def over_dp(blocks):
        return blocks + [turn(x, "dp", -s) for s in range(1, dp_count) for x in blocks]

    kv_weight = jnp.concatenate([key_weight, value_weight], axis=1)
    kv_one, kv_two = swap(kv_weight, "lo"), swap(kv_weight, "hi")
    kv_three = swap(kv_two, "lo")
    kv_stack = over_dp([kv_weight, kv_two, kv_one, kv_three])
    qo_weight = after(jnp.concatenate([query_weight, out_weight], axis=1), kv_three)
    qo_even = jnp.concatenate([qo_weight, swap(qo_weight, "hi")], axis=0)
    qo_odd = swap(qo_even, "lo")
    qo_stack = over_dp([qo_even, qo_odd])

    def ffn_columns(f, which):
        first = which * half_units + f * chunk
        return jnp.concatenate(
            [
                lax.dynamic_slice_in_dim(w, first, chunk, 1)
                for w in (gate_weight, up_weight, down_weight)
            ],
            axis=1,
        )

    def ffn_sends(f, *needed):
        keep, give = after((ffn_columns(f, parity), ffn_columns(f, 1 - parity)), *needed)
        near = jnp.concatenate([keep, swap(give, "lo")], axis=0)
        return near, swap(keep, "hi"), give

    def ffn_stack(near, far):
        stack = [near, far]
        for s in range(1, dp_count):
            stack += [turn(near, "dp", -s), turn(far, "dp", -s)]
        return place_rows(stack, places_ffn)

    group_seq = seq_ids[0].reshape(ctx_count, rows // CLEN, CLEN)[:, :, 0]
    group_pos = positions[0].reshape(ctx_count, rows // CLEN, CLEN)[:, :, 0]
    prompt_at = jnp.argmax(group_seq == 0, axis=1).astype(jnp.int32)
    prompt_rank = jnp.sum(jnp.where(group_seq == 0, group_pos, 0), axis=1).astype(jnp.int32)
    rank = prompt_rank[ctx_index ^ jnp.arange(ctx_count, dtype=jnp.int32)]
    mine = prompt_at[ctx_index]
    pieces = jnp.arange(rows // CLEN, dtype=jnp.int32)
    order = jnp.where(pieces == 0, mine, jnp.where(pieces <= mine, pieces - 1, pieces))
    own_pos = lax.dynamic_slice_in_dim(positions[0], ctx_index * rows, rows)
    cosine, sine = rope_tables(own_pos)

    gain_one = attn_gain[None].astype(F32)
    gain_two = ffn_gain[None].astype(F32)
    first_norm, first_scale = normalize(tokens.astype(F32))
    first = low(first_norm * gain_one)

    kv = project(
        [first], kv_stack, places, bit_ref, 0, 2 * head_width, cosine, sine, head_width
    )
    prompt_own = lax.dynamic_slice_in_dim(kv, mine * CLEN, CLEN)
    prompts = [prompt_own] + [swap(prompt_own, CTX, k) for k in range(1, ctx_count)]
    near_one, two_one, give_one = ffn_sends(0, kv_three)
    query = project(
        [after(first, two_one, near_one)],
        qo_stack,
        places,
        bit_ref,
        0,
        head_width,
        cosine,
        sine,
        head_width,
    )
    mixed, lse = attention_forward(order, rank, query, kv, prompts)
    three_one = swap(after(give_one, *prompts[1:]), CTX, 3)
    near_two, two_two, give_two = ffn_sends(1, *prompts[1:])
    three_two = swap(give_two, CTX, 3)
    ffn_weights = [
        ffn_stack(near_one, jnp.concatenate([two_one, three_one], axis=0)),
        ffn_stack(near_two, jnp.concatenate([two_two, three_two], axis=0)),
    ]

    kept, given = project_back([mixed], ((0, head_width),), [qo_stack], places, bit_ref)
    mixed_out = low(add(kept, swap(given, "tp")))
    mixed_far = after(swap(mixed_out, "tp", 2), three_one, two_two)
    middle = row_half(tokens).astype(F32) + add(mixed_out, mixed_far)
    second_norm, second_scale = normalize(middle)
    second_half = low(second_norm * gain_two)

    cotangent_half = row_half(out_grad)
    cotangent_far = swap(after(cotangent_half, prompts[1]), "lo")
    cotangents = [
        [cotangent_half, row_half(out_grad, 1 - bit)],
        [cotangent_far, swap(cotangent_far, "tp")],
    ]
    second_far = swap(second_half, "lo")
    near = [second_half, swap(second_half, "tp")]
    made = [[ffn(near, cotangents[0], [w]) for w in ffn_weights]]
    second_far = after(second_far, made[0][0][0])
    far = [second_far, swap(second_far, "tp")]
    made.append([ffn(far, cotangents[1], [w]) for w in ffn_weights])
    seconds = [near, far]
    hiddens = [[m[0] for m in side] for side in made]
    dpairs = [[m[1] for m in side] for side in made]
    gate_spans = tuple((f, 0, f, 0, 2 * chunk) for f in range(FFN_CHUNKS))
    down_spans = tuple((f, 0, f, 2 * chunk, chunk) for f in range(FFN_CHUNKS))

    def collect(near, far):
        far = low(add(far[0], swap(far[1], "tp")))
        near = low(add(near[0], swap(near[1], "tp")))
        return low(add(near, swap(far, "lo")))

    dsecond_far = ffn_back(dpairs[1], ffn_weights, gate_spans)
    dsecond_near = ffn_back(dpairs[0], ffn_weights, gate_spans)
    dsecond = collect(dsecond_near, dsecond_far)
    dsecond = add(dsecond, swap(dsecond, "tp", 2))

    lefts, left_cots = after(
        (seconds[0] + seconds[1], cotangents[0] + cotangents[1]), *dsecond_near, *dsecond_far
    )
    ffn_blocks = []
    for f in range(FFN_CHUNKS):

        def part(s, f=f):
            return ffn_grads(
                lefts,
                left_cots,
                [side[f] for side in hiddens],
                [side[f] for side in dpairs],
                owners,
                slots_ffn,
                s,
                near_rows,
                own_rows,
            )

        sent = [turn(part(s), "dp", s) for s in range(1, dp_count)]
        ffn_blocks.append((part(0), sent))

    def ffn_scatter(own, got, first, second, third):
        total = own
        for part in got:
            total = add(total, after(part, first))
        total = low(total)
        pair = add(total[: 2 * own_rows], after(swap(total[2 * own_rows :], "hi"), second))
        kept = pair[:own_rows]
        got = after(swap(low(pair[own_rows:]), "lo"), third).astype(F32)
        return (jnp.where(parity == 0, kept, got), jnp.where(parity == 0, got, kept))

    gain_two_grad = jnp.sum(dsecond * second_norm, axis=0)
    scaled_two = dsecond * gain_two
    dmiddle = cotangent_half.astype(F32) + second_scale * (
        scaled_two - second_norm * jnp.mean(scaled_two * second_norm, axis=-1, keepdims=True)
    )
    dmiddle_low = [low(dmiddle), swap(low(dmiddle), "tp")]
    dmixed = project(dmiddle_low, qo_stack, places, bit_ref, head_width, head_width, cosine, sine, 0)
    dquery_low, dkey_own, dvalue_own, dprompt_own, *dprompts = attention_backward(
        order, rank, query, kv, mixed, lse, dmixed, cosine, sine, prompts
    )
    got = [swap(piece, CTX, k + 1) for k, piece in enumerate(dprompts)]
    dkey_low, dvalue_low = merge_keys(
        mine[None], dkey_own, dvalue_own, dprompt_own, got, cosine, sine
    )

    def attn_grads(pairs):
        parts = [
            attn_grads_block(pairs, bit_ref, owners, slots_attn, s, near_rows, own_rows)
            for s in range(dp_count)
        ]
        total = parts[0]
        for s in range(1, dp_count):
            total = add(total, turn(parts[s], "dp", s))
        total = low(total)
        pair = add(total[: 2 * own_rows], swap(total[2 * own_rows :], "lo"))
        return pair[:own_rows] + swap(low(pair[own_rows:]), "hi").astype(F32)

    early = attn_grads([(dmiddle_low, mixed), ([first], dquery_low)])
    late = attn_grads([([first], dkey_low), ([first], dvalue_low)])
    ffn_sums = [
        ffn_scatter(*ffn_blocks[0], dmiddle, dquery_low, dkey_low),
        ffn_scatter(*ffn_blocks[1], dquery_low, dkey_low, dkey_low),
    ]

    kept, given = project_back(
        [dquery_low, dkey_low, dvalue_low],
        ((0, 0), (1, 0), (1, head_width)),
        [qo_stack, kv_stack],
        places,
        bit_ref,
    )
    norm_half, norm_other = row_half(first_norm), row_half(first_norm, 1 - bit)
    gain_one_grad = jnp.sum(kept.astype(F32) * norm_half, axis=0) + jnp.sum(
        given.astype(F32) * norm_other, axis=0
    )
    dfirst = low(add(kept, swap(given, "tp")))
    dfirst = add(dfirst, swap(dfirst, "tp", 2))
    scaled_one = dfirst * gain_one
    dinputs = dmiddle + row_half(first_scale) * (
        scaled_one - norm_half * jnp.mean(scaled_one * norm_half, axis=-1, keepdims=True)
    )

    share = width // tp_count
    here = tp_index // 2

    def wide_part(values, which):
        return lax.dynamic_slice_in_dim(values, which * 2 * share, 2 * share, 1)

    def deliver(wide):
        kept = lax.dynamic_slice_in_dim(wide, bit * share, share, 1)
        given = lax.dynamic_slice_in_dim(wide, (1 - bit) * share, share, 1)
        return assemble(kept, swap(given, "tp"))

    in_grad = deliver(low(wide_part(dinputs, here)))

    hiddens = after(hiddens, dmixed)
    ffn_out = collect(
        ffn_back(hiddens[0], ffn_weights, down_spans),
        ffn_back(hiddens[1], ffn_weights, down_spans),
    )
    ffn_out = add(wide_part(ffn_out, here), swap(wide_part(ffn_out, 1 - here), "tp", 2))
    block_out = deliver(low(wide_part(middle, here) + ffn_out))

    gains = jnp.stack([gain_one_grad, jnp.where(here == 0, gain_two_grad, 0.0)])
    for axis in ("tp", "lo", "hi", "dp"):
        mask = 1
        while mask < lax.axis_size(axis):
            gains = gains + swap(gains, axis, mask)
            mask *= 2
    part = width // (dp_count * ctx_count)
    gains = lax.dynamic_slice_in_dim(gains, (dp_index * ctx_count + ctx_index) * part, part, 1)

    ffn_final = [
        jnp.concatenate(
            [
                ffn_sums[f][side][:, i * chunk : (i + 1) * chunk]
                for side in range(2)
                for f in range(FFN_CHUNKS)
            ],
            axis=1,
        )
        for i in range(3)
    ]
    return (
        block_out,
        in_grad,
        gains[0],
        early[:, head_width:],
        late[:, :head_width],
        late[:, head_width:],
        early[:, :head_width],
        gains[1],
        ffn_final[0],
        ffn_final[1],
        ffn_final[2],
    )


def solution(mesh):
    dp, ctx, tp = (mesh.shape[name] for name in ("dp", "ctx", "tp"))
    split_mesh = Mesh(mesh.devices.reshape(dp, ctx // 2, 2, tp), ("dp", "hi", "lo", "tp"))
    every = ("dp",) + CTX
    split = P(every, "tp")
    rows = P(every, None)
    vector = P(every)
    return jax.shard_map(
        body,
        mesh=split_mesh,
        in_specs=(rows, P(), split, split, split, split, P(), split, split, split)
        + (P("dp", None), P("dp", None), rows),
        out_specs=(split, split, vector, split, split, split, split, vector, split, split, split),
        check_vma=False,
    )
```

```python
import functools
import math

import jax
import jax.numpy as jnp
from jax import lax
from jax.experimental import pallas as pl
from jax.experimental.pallas import tpu as pltpu
from jax.sharding import Mesh
from jax.sharding import PartitionSpec as P

HEAD_DIM = 64
CLEN = 256
LANES = 128
EPS = 1e-05
ROPE_BASE = 130000.0
MASKED = -1e30
FFN_CHUNKS = 2
COST_SCALE = 16
BF16 = jnp.bfloat16
F32 = jnp.float32
VMEM_LIMIT = 32 * 1024 * 1024
VMEM_WHOLE = 60 * 1024 * 1024
CTX = ("hi", "lo")


def swap(values, axis, mask=1):
    count = lax.axis_size(axis)
    return lax.ppermute(values, axis, [(i, i ^ mask) for i in range(count)])


def turn(values, axis, shift):
    count = lax.axis_size(axis)
    return lax.ppermute(values, axis, [(i, (i + shift) % count) for i in range(count)])


def add(left, right):
    return left.astype(F32) + right.astype(F32)


def low(values):
    return values.astype(BF16)


def after(values, *needed):
    return lax.optimization_barrier((values,) + needed)[0]


def cost(flops, data, transcendentals=0):
    return pl.CostEstimate(
        flops=flops // COST_SCALE,
        bytes_accessed=data // COST_SCALE,
        transcendentals=transcendentals // COST_SCALE,
    )


def dot(left, right, dims):
    return lax.dot_general(left, right, (dims, ((), ())), preferred_element_type=F32)


NN = ((1,), (0,))
NT = ((1,), (1,))
TN = ((0,), (0,))
VMEM = pl.BlockSpec(memory_space=pltpu.VMEM)
SMEM = pl.BlockSpec(memory_space=pltpu.SMEM)


def at_block(index, size):
    return pl.ds(pl.multiple_of(index * size, size), size)


def half_swap(values):
    lane = lax.broadcasted_iota(jnp.int32, values.shape, 1)
    ahead = pltpu.roll(values, LANES - 32, 1)
    behind = pltpu.roll(values, 32, 1)
    return jnp.where((lane & 63) < 32, ahead, behind)


def call(kernel, operands, out_shape, name, flops, data, scratch=(), smem=(), transcendentals=0):
    many = isinstance(out_shape, list)
    return pl.pallas_call(
        kernel,
        in_specs=[SMEM] * len(smem) + [VMEM] * len(operands),
        out_specs=[VMEM] * len(out_shape) if many else VMEM,
        out_shape=out_shape,
        scratch_shapes=list(scratch),
        compiler_params=pltpu.CompilerParams(vmem_limit_bytes=VMEM_LIMIT),
        cost_estimate=cost(flops, data, transcendentals),
        name=name,
    )(*smem, *operands)


def fill(whole, pieces, place_ref, unit, column, width):
    at = 0
    for piece in pieces:
        for row in range(0, piece.shape[0], unit):
            whole[at_block(place_ref[at], unit), :] = piece[
                row : row + unit, column : column + width
            ]
            at += 1


def project_kernel(parts, column, width, rope_width, bit_ref, place_ref, *refs):
    x_refs = refs[:parts]
    w_refs = refs[parts:-5]
    cos_ref, sin_ref, out_ref, x_all, w_all = refs[-5:]
    fill(w_all, w_refs, place_ref, w_all.shape[0] // place_ref.shape[0], column, width)
    if parts == 2:
        rows = x_refs[0].shape[0]
        x_all[at_block(bit_ref[0], rows), :] = x_refs[0][...]
        x_all[at_block(1 - bit_ref[0], rows), :] = x_refs[1][...]
        x_ref = x_all
    else:
        x_ref = x_refs[0]
    tile = min(width, 256)

    def columns(first, rope):
        def step(t, carry):
            at = pl.multiple_of(first + t * tile, tile)
            total = dot(x_ref[...], w_all[:, pl.ds(at, tile)], NN)
            for c in range(0, tile, LANES):
                part = total[:, c : c + LANES]
                if rope:
                    part = part * cos_ref[...] + half_swap(part) * sin_ref[...]
                out_ref[:, pl.ds(pl.multiple_of(at + c, LANES), LANES)] = part.astype(BF16)
            return carry

        return step

    if rope_width:
        lax.fori_loop(0, rope_width // tile, columns(0, True), 0)
    if rope_width < width:
        lax.fori_loop(0, (width - rope_width) // tile, columns(rope_width, False), 0)


def project(x_parts, stack, places, bit, column, width, cosine, sine, rope_width):
    rows = sum(x.shape[0] for x in x_parts)
    depth = x_parts[0].shape[1]
    return call(
        functools.partial(project_kernel, len(x_parts), column, width, rope_width),
        [*x_parts, *stack, cosine, sine],
        jax.ShapeDtypeStruct((rows, width), BF16),
        "project",
        2 * rows * depth * width,
        2 * (rows * depth + depth * width + rows * width),
        [
            pltpu.VMEM((rows if len(x_parts) == 2 else 16, depth), BF16),
            pltpu.VMEM((depth, width), BF16),
        ],
        [bit, places],
    )


def place_kernel(count, place_ref, *refs):
    out_ref = refs[-1]
    unit = out_ref.shape[0] // count
    at = 0
    for ref in refs[:-1]:
        for row in range(0, ref.shape[0], unit):
            out_ref[at_block(place_ref[at], unit), :] = ref[row : row + unit, :]
            at += 1


def place_rows(pieces, places):
    rows, width = sum(p.shape[0] for p in pieces), pieces[0].shape[1]
    return call(
        functools.partial(place_kernel, places.shape[0]),
        pieces,
        jax.ShapeDtypeStruct((rows, width), BF16),
        "place_rows",
        0,
        4 * rows * width,
        smem=[places],
    )


def ffn_kernel(chunks, *refs):
    x_refs, cot_refs = refs[:2], refs[2:4]
    w_refs = refs[4 : 4 + chunks]
    hidden_ref, dpair_ref = refs[4 + chunks :]
    rows = x_refs[0].shape[0]
    wide = w_refs[0].shape[1] // 3
    tile = min(wide, 256)
    for f, w_ref in enumerate(w_refs):

        def step(t, carry, f=f, w_ref=w_ref):
            for part in range(2):
                x, g = x_refs[part][...], cot_refs[part][...]
                gate = dot(x, w_ref[:, pl.ds(pl.multiple_of(t * tile, tile), tile)], NN)
                upward = dot(x, w_ref[:, pl.ds(pl.multiple_of(wide + t * tile, tile), tile)], NN)
                dhidden = dot(g, w_ref[:, pl.ds(pl.multiple_of(2 * wide + t * tile, tile), tile)], NN)
                sig = 1.0 / (1.0 + jnp.exp(-gate))
                silu = gate * sig
                at = slice(part * rows, (part + 1) * rows)
                hidden_ref[at, pl.ds(pl.multiple_of(f * wide + t * tile, tile), tile)] = (
                    silu * upward
                ).astype(BF16)
                dpair_ref[at, pl.ds(pl.multiple_of(2 * f * wide + t * tile, tile), tile)] = (
                    dhidden * upward * (sig + silu * (1.0 - sig))
                ).astype(BF16)
                dpair_ref[at, pl.ds(pl.multiple_of((2 * f + 1) * wide + t * tile, tile), tile)] = (
                    dhidden * silu
                ).astype(BF16)
            return carry

        lax.fori_loop(0, wide // tile, step, 0)


def ffn(seconds, cotangents, weights):
    rows = 2 * seconds[0].shape[0]
    width = seconds[0].shape[1]
    units = sum(w.shape[1] for w in weights) // 3
    return call(
        functools.partial(ffn_kernel, len(weights)),
        [*seconds, *cotangents, *weights],
        [jax.ShapeDtypeStruct((rows, units), BF16), jax.ShapeDtypeStruct((rows, 2 * units), BF16)],
        "ffn",
        6 * rows * width * units,
        2 * (2 * rows * width + 3 * width * units + 3 * rows * units),
        transcendentals=rows * units,
    )


def back_kernel(spans, *refs):
    count = 1 + max(span[2] for span in spans)
    lefts = refs[: 1 + max(span[0] for span in spans)]
    rights = refs[len(lefts) : len(lefts) + count]
    outs = refs[len(lefts) + count :]
    rows, width = outs[0].shape
    tile = 256

    def step(t, carry):
        for part, out_ref in enumerate(outs):
            total = None
            for left, l_at, right, r_at, wide in spans:
                term = dot(
                    lefts[left][part * rows : (part + 1) * rows, l_at : l_at + wide],
                    rights[right][at_block(t, tile), r_at : r_at + wide],
                    NT,
                )
                total = term if total is None else total + term
            out_ref[:, at_block(t, tile)] = total.astype(BF16)
        return carry

    lax.fori_loop(0, width // tile, step, 0)


def ffn_back(lefts, weights, spans):
    rows = lefts[0].shape[0]
    width = weights[0].shape[0]
    depth = sum(span[4] for span in spans)
    return call(
        functools.partial(back_kernel, spans),
        [*lefts, *weights],
        [jax.ShapeDtypeStruct((rows // 2, width), BF16)] * 2,
        "ffn_back",
        2 * rows * width * depth,
        2 * (rows * depth + width * depth + rows * width),
    )


def project_back_kernel(columns, counts, bit_ref, place_ref, *refs):
    lefts = refs[: len(columns)]
    at, stacks = len(columns), []
    for count in counts:
        stacks.append(refs[at : at + count])
        at += count
    outs, w_all = refs[at : at + 2], refs[at + 2]
    rows, width = outs[0].shape
    unit = width // place_ref.shape[0]
    wide = lefts[0].shape[1]
    for n, (which, column) in enumerate(columns):
        at = 0
        for piece in stacks[which]:
            for row in range(0, piece.shape[0], unit):
                w_all[at_block(place_ref[at], unit), n * wide : (n + 1) * wide] = piece[
                    row : row + unit, column : column + wide
                ]
                at += 1
    tile = 256

    def step(t, carry):
        for part, out_ref in enumerate(outs):
            which = bit_ref[0] if part == 0 else 1 - bit_ref[0]
            total = None
            for n, left in enumerate(lefts):
                term = dot(
                    left[at_block(which, rows), :],
                    w_all[at_block(t, tile), n * wide : (n + 1) * wide],
                    NT,
                )
                total = term if total is None else total + term
            out_ref[:, at_block(t, tile)] = total.astype(BF16)
        return carry

    lax.fori_loop(0, width // tile, step, 0)


def project_back(lefts, columns, stacks, places, bit):
    rows, wide = lefts[0].shape
    width = sum(piece.shape[0] for piece in stacks[0])
    depth = wide * len(lefts)
    return call(
        functools.partial(project_back_kernel, columns, tuple(len(s) for s in stacks)),
        [*lefts, *[piece for stack in stacks for piece in stack]],
        [jax.ShapeDtypeStruct((rows // 2, width), BF16)] * 2,
        "project_back",
        2 * rows * width * depth,
        2 * (rows * depth + width * depth + rows * width),
        [pltpu.VMEM((width, depth), BF16)],
        [bit, places],
    )


def store_blocks(out_ref, values, first, unit, slot_ref, column):
    wide = values.shape[1]
    for row in range(0, values.shape[0], unit):
        slot = slot_ref[(first + row) // unit]
        out_ref[at_block(slot, unit), column : column + wide] = values[row : row + unit]


def ffn_grads_kernel(tile, unit, dp_ref, slot_ref, *refs):
    del dp_ref
    x_refs, cot_refs = refs[:4], refs[4:8]
    hiddens, dpairs, out_ref = refs[8:10], refs[10:12], refs[12]
    rows = x_refs[0].shape[0]
    wide = hiddens[0].shape[1]

    def product(lefts, rights):
        total = None
        for n, left in enumerate(lefts):
            part = slice((n % 2) * rows, (n % 2 + 1) * rows)
            term = dot(left[...], rights[n // 2][part, :], TN)
            total = term if total is None else total + term
        return total.astype(BF16)

    first = pl.program_id(0) * tile
    store_blocks(out_ref, product(x_refs, dpairs), first, unit, slot_ref, 0)
    store_blocks(out_ref, product(cot_refs, hiddens), first, unit, slot_ref, 2 * wide)


def ffn_grads(seconds, cotangents, hiddens, dpairs, owners, slots, s, count, unit):
    half, wide = seconds[0].shape[0], hiddens[0].shape[1]
    rows = 4 * half
    tile = 256
    left = pl.BlockSpec((half, tile), lambda t, dp, slot: (0, dp[s] * (count // tile) + t))
    whole = lambda x: pl.BlockSpec(x.shape, lambda t, dp, slot: (0, 0))
    return pl.pallas_call(
        functools.partial(ffn_grads_kernel, tile, unit),
        grid_spec=pltpu.PrefetchScalarGridSpec(
            num_scalar_prefetch=2,
            grid=(count // tile,),
            in_specs=[left] * 8 + [whole(x) for x in (*hiddens, *dpairs)],
            out_specs=pl.BlockSpec((count, 3 * wide), lambda t, dp, slot: (0, 0)),
        ),
        out_shape=jax.ShapeDtypeStruct((count, 3 * wide), BF16),
        compiler_params=pltpu.CompilerParams(vmem_limit_bytes=VMEM_WHOLE),
        cost_estimate=cost(
            6 * rows * count * wide,
            2 * (2 * rows * count + 3 * rows * wide + 3 * count * wide),
        ),
        name="ffn_grads",
    )(owners, slots, *seconds, *cotangents, *hiddens, *dpairs)


def attn_grads_kernel(kinds, s, unit, bit_ref, dp_ref, slot_ref, *refs):
    at, pairs = 0, []
    for parts in kinds:
        pairs.append((refs[at : at + parts], refs[at + parts]))
        at += parts + 1
    out_ref = refs[at]
    count = out_ref.shape[0]
    tile = 256

    def step(t, carry):
        where = pl.ds(pl.multiple_of(dp_ref[s] * count + t * tile, tile), tile)
        column = 0
        for lefts, right in pairs:
            if len(lefts) == 1:
                total = dot(lefts[0][:, where], right[...], TN)
            else:
                rows = lefts[0].shape[0]
                total = dot(lefts[0][:, where], right[at_block(bit_ref[0], rows), :], TN) + dot(
                    lefts[1][:, where], right[at_block(1 - bit_ref[0], rows), :], TN
                )
            store_blocks(out_ref, total.astype(BF16), t * tile, unit, slot_ref, column)
            column += right.shape[1]
        return carry

    lax.fori_loop(0, count // tile, step, 0)


def attn_grads_block(pairs, bit, owners, slots, s, count, unit):
    kinds = tuple(len(lefts) for lefts, _ in pairs)
    width = sum(right.shape[1] for _, right in pairs)
    rows = pairs[0][1].shape[0]
    return call(
        functools.partial(attn_grads_kernel, kinds, s, unit),
        [x for lefts, right in pairs for x in (*lefts, right)],
        jax.ShapeDtypeStruct((count, width), BF16),
        "attn_grads",
        2 * rows * width * count,
        2 * (rows * count + rows * width + count * width),
        smem=[bit, owners, slots],
    )


SCALE = HEAD_DIM**-0.5
SCALE_LOG2 = SCALE * math.log2(math.e)


def forward_kernel(pieces, order_ref, rank_ref, q_ref, ks_ref, vs_ref, *refs):
    kp_refs, vp_refs = refs[:pieces], refs[pieces : 2 * pieces]
    o_ref, lse_ref = refs[2 * pieces :]
    q = q_ref[...]
    size = q.shape[0]
    prompt = pl.program_id(1) == 0
    low_lane = lax.broadcasted_iota(jnp.int32, q.shape, 1) < HEAD_DIM
    causal = lax.broadcasted_iota(jnp.int32, (size, size), 0) >= lax.broadcasted_iota(
        jnp.int32, (size, size), 1
    )
    outs = []
    for head in range(2):
        own = low_lane if head == 0 else jnp.logical_not(low_lane)
        qh = jnp.where(own, q, jnp.zeros_like(q))
        raw = [jnp.where(causal, dot(qh, ks_ref[...], NT), MASKED)]
        for s in range(pieces):
            hidden = jnp.logical_and(prompt, rank_ref[s] >= rank_ref[0])
            raw.append(dot(qh, kp_refs[s][...], NT) + jnp.where(hidden, MASKED, 0.0))
        top = raw[0]
        for r in raw[1:]:
            top = jnp.maximum(top, r)
        top = jnp.max(top, axis=-1, keepdims=True) * SCALE_LOG2
        sums, acc = None, None
        for s, r in enumerate(raw):
            e = jnp.exp2(r * SCALE_LOG2 - top)
            v = vs_ref if s == 0 else vp_refs[s - 1]
            term = dot(e.astype(BF16), v[...], NN)
            sums = e if sums is None else sums + e
            acc = term if acc is None else acc + term
        total = jnp.sum(sums, axis=-1, keepdims=True)
        outs.append((acc / total, top + jnp.log2(total)))
    o_ref[...] = jnp.where(low_lane, outs[0][0], outs[1][0]).astype(BF16)
    lse_ref[...] = jnp.where(low_lane, outs[0][1], outs[1][1])


def backward_kernel(
    pieces, order_ref, rank_ref, q_ref, ks_ref, vs_ref, o_ref, lse_ref, do_ref, cos_ref, sin_ref, *refs
):
    kp_refs, vp_refs = refs[:pieces], refs[pieces : 2 * pieces]
    dq_ref, dks_ref, dvs_ref = refs[2 * pieces : 2 * pieces + 3]
    piece_refs = refs[2 * pieces + 3 : 3 * pieces + 3]
    acc_ref = refs[-1]
    pair, step = pl.program_id(0), pl.program_id(1)
    prompt = step == 0
    q, do = q_ref[...], do_ref[...]
    size = q.shape[0]
    low_lane = lax.broadcasted_iota(jnp.int32, q.shape, 1) < HEAD_DIM
    causal = lax.broadcasted_iota(jnp.int32, (size, size), 0) >= lax.broadcasted_iota(
        jnp.int32, (size, size), 1
    )
    product = do.astype(F32) * o_ref[...].astype(F32)
    lse = lse_ref[...]
    dq_heads = []
    dk_all = [None] * (pieces + 1)
    dv_all = [None] * (pieces + 1)
    for head in range(2):
        own = low_lane if head == 0 else jnp.logical_not(low_lane)
        qh = jnp.where(own, q, jnp.zeros_like(q))
        doh = jnp.where(own, do, jnp.zeros_like(do))
        delta = jnp.sum(jnp.where(own, product, 0.0), axis=-1, keepdims=True)
        log_sum = lse[:, head * HEAD_DIM : head * HEAD_DIM + 1]
        dq = None
        for s in range(pieces + 1):
            k = (ks_ref if s == 0 else kp_refs[s - 1])[...]
            v = (vs_ref if s == 0 else vp_refs[s - 1])[...]
            raw = dot(qh, k, NT)
            if s == 0:
                raw = jnp.where(causal, raw, MASKED)
            else:
                hidden = jnp.logical_and(prompt, rank_ref[s - 1] >= rank_ref[0])
                raw = raw + jnp.where(hidden, MASKED, 0.0)
            prob = jnp.exp2(raw * SCALE_LOG2 - log_sum)
            ds = (prob * (dot(doh, v, NT) - delta)).astype(BF16)
            term = dot(ds, k, NN)
            dq = term if dq is None else dq + term
            dk = dot(ds, qh, TN)
            dv = dot(prob.astype(BF16), doh, TN)
            dk_all[s] = dk if dk_all[s] is None else dk_all[s] + dk
            dv_all[s] = dv if dv_all[s] is None else dv_all[s] + dv
        dq_heads.append(dq)
    dq = jnp.where(low_lane, dq_heads[0], dq_heads[1]) * SCALE
    cosine, sine = cos_ref[...], sin_ref[...]
    dq_ref[...] = (dq * cosine - half_swap(dq) * sine).astype(BF16)
    dks_ref[...] = dk_all[0] * SCALE
    dvs_ref[...] = dv_all[0]
    for s in range(pieces):
        both = jnp.concatenate([dk_all[s + 1] * SCALE, dv_all[s + 1]], axis=1)
        at = slice(s * size, (s + 1) * size)

        @pl.when(prompt)
        def _(both=both, at=at):
            acc_ref[at, :] = both

        @pl.when(jnp.logical_not(prompt))
        def _(both=both, at=at):
            acc_ref[at, :] += both

    @pl.when(step == pl.num_programs(1) - 1)
    def _():
        wide = piece_refs[0].shape[1] // 2
        k_at = pl.ds(pl.multiple_of(pair * LANES, LANES), LANES)
        v_at = pl.ds(pl.multiple_of(wide + pair * LANES, LANES), LANES)
        for s in range(pieces):
            both = acc_ref[s * size : (s + 1) * size, :]
            piece_refs[s][:, k_at] = both[:, :LANES].astype(piece_refs[s].dtype)
            piece_refs[s][:, v_at] = both[:, LANES:].astype(piece_refs[s].dtype)


def merge_kernel(others, mine_ref, dk_ref, dv_ref, own_ref, *refs):
    got = refs[:others]
    cos_ref, sin_ref, dk_out, dv_out = refs[others:]
    width = dk_ref.shape[1]
    cosine, sine = cos_ref[...], sin_ref[...]

    def write(dk, dv):
        for at in range(0, width, LANES):
            part = dk[:, at : at + LANES]
            dk_out[:, at : at + LANES] = (part * cosine - half_swap(part) * sine).astype(BF16)
        dv_out[...] = dv.astype(BF16)

    mine = pl.program_id(0) == mine_ref[0]

    @pl.when(mine)
    def _():
        extra = own_ref[...]
        for ref in got:
            extra = extra + ref[...].astype(F32)
        write(dk_ref[...] + extra[:, :width], dv_ref[...] + extra[:, width:])

    @pl.when(jnp.logical_not(mine))
    def _():
        write(dk_ref[...], dv_ref[...])


def merge_keys(mine, dkey, dvalue, own, got, cosine, sine):
    rows, width = dkey.shape
    row = lambda i, mine: (i, 0)
    full = lambda i, mine: (0, 0)
    return pl.pallas_call(
        functools.partial(merge_kernel, len(got)),
        grid_spec=pltpu.PrefetchScalarGridSpec(
            num_scalar_prefetch=1,
            grid=(rows // CLEN,),
            in_specs=[pl.BlockSpec((CLEN, width), row)] * 2
            + [pl.BlockSpec((CLEN, 2 * width), full)] * (1 + len(got))
            + [pl.BlockSpec((CLEN, LANES), row)] * 2,
            out_specs=[pl.BlockSpec((CLEN, width), row)] * 2,
        ),
        out_shape=[jax.ShapeDtypeStruct((rows, width), BF16)] * 2,
        compiler_params=pltpu.CompilerParams(vmem_limit_bytes=VMEM_LIMIT),
        cost_estimate=cost(8 * rows * width, 16 * rows * width, 0),
        name="merge_keys",
    )(mine, dkey, dvalue, own, *got, cosine, sine)


def attention_specs(pieces, key_pairs):
    own = pl.BlockSpec((CLEN, LANES), lambda h, j, order, rank: (order[j], h))
    own_value = pl.BlockSpec((CLEN, LANES), lambda h, j, order, rank: (order[j], key_pairs + h))
    key = pl.BlockSpec((CLEN, LANES), lambda h, j, order, rank: (0, h))
    value = pl.BlockSpec((CLEN, LANES), lambda h, j, order, rank: (0, key_pairs + h))
    trig = pl.BlockSpec((CLEN, LANES), lambda h, j, order, rank: (order[j], 0))
    prompt = pl.BlockSpec((CLEN, 2 * key_pairs * LANES), lambda h, j, order, rank: (0, 0))
    return own, own_value, key, value, trig, prompt


def attention_forward(order, rank, query, kv, prompts):
    rows, width = query.shape
    pieces, pairs = len(prompts), width // LANES
    own, own_value, key, value, _, _ = attention_specs(pieces, pairs)
    scores = rows * (pieces + 1) * CLEN * (width // HEAD_DIM)
    return pl.pallas_call(
        functools.partial(forward_kernel, pieces),
        grid_spec=pltpu.PrefetchScalarGridSpec(
            num_scalar_prefetch=2,
            grid=(pairs, rows // CLEN),
            in_specs=[own, own, own_value] + [key] * pieces + [value] * pieces,
            out_specs=[own, own],
        ),
        out_shape=[jax.ShapeDtypeStruct((rows, width), BF16), jax.ShapeDtypeStruct((rows, width), F32)],
        compiler_params=pltpu.CompilerParams(vmem_limit_bytes=VMEM_LIMIT),
        cost_estimate=cost(
            16 * scores * HEAD_DIM, 16 * rows * width, scores
        ),
        name="attend",
    )(order, rank, query, kv, kv, *prompts, *prompts)


def attention_backward(order, rank, query, kv, mixed, lse, dmixed, cosine, sine, prompts):
    rows, width = query.shape
    pieces, pairs = len(prompts), width // LANES
    own, own_value, key, value, trig, prompt = attention_specs(pieces, pairs)
    scores = rows * (pieces + 1) * CLEN * (width // HEAD_DIM)
    return pl.pallas_call(
        functools.partial(backward_kernel, pieces),
        grid_spec=pltpu.PrefetchScalarGridSpec(
            num_scalar_prefetch=2,
            grid=(pairs, rows // CLEN),
            in_specs=[own, own, own_value, own, own, own] + [trig] * 2 + [key] * pieces + [value] * pieces,
            out_specs=[own, own, own] + [prompt] * pieces,
            scratch_shapes=[pltpu.VMEM((pieces * CLEN, 2 * LANES), F32)],
        ),
        out_shape=[
            jax.ShapeDtypeStruct((rows, width), BF16),
            jax.ShapeDtypeStruct((rows, width), F32),
            jax.ShapeDtypeStruct((rows, width), F32),
        ]
        + [jax.ShapeDtypeStruct((CLEN, 2 * width), BF16 if s else F32) for s in range(pieces)],
        compiler_params=pltpu.CompilerParams(vmem_limit_bytes=VMEM_LIMIT),
        cost_estimate=cost(
            40 * scores * HEAD_DIM, 32 * rows * width, scores
        ),
        name="attend_back",
    )(order, rank, query, kv, kv, mixed, lse, dmixed, cosine, sine, *prompts, *prompts)


def normalize(values):
    factor = lax.rsqrt(jnp.mean(values * values, axis=-1, keepdims=True) + EPS)
    return (values * factor, factor)


def rope_tables(where):
    half = HEAD_DIM // 2
    freqs = ROPE_BASE ** (-(jnp.arange(half).astype(F32) * 2.0) / HEAD_DIM)
    angles = where.astype(F32)[:, None] * freqs[None, :]
    cosine, sine = jnp.cos(angles), jnp.sin(angles)
    return (
        jnp.concatenate([cosine] * 4, axis=1),
        jnp.concatenate([-sine, sine, -sine, sine], axis=1),
    )


def body(
    tokens,
    attn_gain,
    query_weight,
    key_weight,
    value_weight,
    out_weight,
    ffn_gain,
    gate_weight,
    up_weight,
    down_weight,
    seq_ids,
    positions,
    out_grad,
):
    rows, width = tokens.shape
    head_width = query_weight.shape[1]
    own_rows, ffn_width = gate_weight.shape
    half_units = ffn_width // 2
    chunk = half_units // FFN_CHUNKS
    half = rows // 2
    dp_count = lax.axis_size("dp")
    ctx_count = lax.axis_size("hi") * 2
    tp_count = lax.axis_size("tp")
    dp_index = lax.axis_index("dp")
    parity = lax.axis_index("lo")
    ctx_index = lax.axis_index("hi") * 2 + parity
    tp_index = lax.axis_index("tp")
    bit = tp_index & 1
    bit_ref = bit.astype(jnp.int32)[None]

    def row_half(values, which=bit):
        return lax.dynamic_slice_in_dim(values, which * half, half)

    def assemble(mine, other):
        first = jnp.where(bit == 0, mine, other)
        last = jnp.where(bit == 0, other, mine)
        return jnp.concatenate([first, last], axis=0)

    slots = jnp.arange(dp_count * ctx_count, dtype=jnp.int32)

    def places_of(order_k):
        slot_k = jnp.array(order_k, jnp.int32)[slots % ctx_count]
        return (
            lax.rem(dp_index + slots // ctx_count, dp_count) * ctx_count + (ctx_index ^ slot_k)
        ).astype(jnp.int32)

    def slots_of(order_k):
        slot_of = jnp.array([order_k.index(k) for k in range(ctx_count)], jnp.int32)
        return slot_of[ctx_index ^ jnp.arange(ctx_count, dtype=jnp.int32)]

    attn_order, ffn_order = (0, 2, 1, 3), (0, 1, 2, 3)
    places, places_ffn = places_of(attn_order), places_of(ffn_order)
    slots_attn, slots_ffn = slots_of(attn_order), slots_of(ffn_order)
    owners = lax.rem(dp_index + jnp.arange(dp_count, dtype=jnp.int32), dp_count).astype(jnp.int32)
    near_rows = width // dp_count

    def over_dp(blocks):
        return blocks + [turn(x, "dp", -s) for s in range(1, dp_count) for x in blocks]

    kv_weight = jnp.concatenate([key_weight, value_weight], axis=1)
    kv_one, kv_two = swap(kv_weight, "lo"), swap(kv_weight, "hi")
    kv_three = swap(kv_two, "lo")
    kv_stack = over_dp([kv_weight, kv_two, kv_one, kv_three])
    qo_weight = after(jnp.concatenate([query_weight, out_weight], axis=1), kv_three)
    qo_even = jnp.concatenate([qo_weight, swap(qo_weight, "hi")], axis=0)
    qo_odd = swap(qo_even, "lo")
    qo_stack = over_dp([qo_even, qo_odd])

    def ffn_columns(f, which):
        first = which * half_units + f * chunk
        return jnp.concatenate(
            [
                lax.dynamic_slice_in_dim(w, first, chunk, 1)
                for w in (gate_weight, up_weight, down_weight)
            ],
            axis=1,
        )

    def ffn_sends(f, *needed):
        keep, give = after((ffn_columns(f, parity), ffn_columns(f, 1 - parity)), *needed)
        near = jnp.concatenate([keep, swap(give, "lo")], axis=0)
        return near, swap(keep, "hi"), give

    def ffn_stack(near_blocks, far):
        return place_rows(
            [x for both in zip(near_blocks, gather_dp(far)) for x in both], places_ffn
        )

    def gather_dp(own):
        return [own] + [turn(own, "dp", -s) for s in range(1, dp_count)]

    group_seq = seq_ids[0].reshape(ctx_count, rows // CLEN, CLEN)[:, :, 0]
    group_pos = positions[0].reshape(ctx_count, rows // CLEN, CLEN)[:, :, 0]
    prompt_at = jnp.argmax(group_seq == 0, axis=1).astype(jnp.int32)
    prompt_rank = jnp.sum(jnp.where(group_seq == 0, group_pos, 0), axis=1).astype(jnp.int32)
    rank = prompt_rank[ctx_index ^ jnp.arange(ctx_count, dtype=jnp.int32)]
    mine = prompt_at[ctx_index]
    pieces = jnp.arange(rows // CLEN, dtype=jnp.int32)
    order = jnp.where(pieces == 0, mine, jnp.where(pieces <= mine, pieces - 1, pieces))
    own_pos = lax.dynamic_slice_in_dim(positions[0], ctx_index * rows, rows)
    cosine, sine = rope_tables(own_pos)

    gain_one = attn_gain[None].astype(F32)
    gain_two = ffn_gain[None].astype(F32)
    first_norm, first_scale = normalize(tokens.astype(F32))
    first = low(first_norm * gain_one)

    kv = project(
        [first], kv_stack, places, bit_ref, 0, 2 * head_width, cosine, sine, head_width
    )
    prompt_own = lax.dynamic_slice_in_dim(kv, mine * CLEN, CLEN)
    prompts = [prompt_own] + [swap(prompt_own, CTX, k) for k in range(1, ctx_count)]
    near_one, two_one, give_one = ffn_sends(0, kv_three)
    query = project(
        [after(first, two_one, near_one)],
        qo_stack,
        places,
        bit_ref,
        0,
        head_width,
        cosine,
        sine,
        head_width,
    )
    near_one = gather_dp(near_one)
    cotangent_half = row_half(out_grad)
    cotangent_far = swap(after(cotangent_half, *prompts[1:]), "lo")
    three_one = swap(after(give_one, kv_stack[-1]), CTX, 3)
    query = after(query, *near_one[1:], three_one)
    mixed, lse = attention_forward(order, rank, query, kv, prompts)
    near_two, two_two, give_two = ffn_sends(1, *prompts[1:])
    mixed = after(mixed, two_two, near_two)
    near_two = gather_dp(near_two)
    three_two = swap(after(give_two, three_one), CTX, 3)
    ffn_weights = [
        ffn_stack(near_one, jnp.concatenate([two_one, three_one], axis=0)),
        ffn_stack(near_two, jnp.concatenate([two_two, three_two], axis=0)),
    ]

    kept, given = project_back(
        [mixed], ((0, head_width),), [qo_stack], places, bit_ref
    )
    mixed_out = low(add(kept, swap(given, "tp")))
    mixed_far = after(
        swap(mixed_out, "tp", 2), three_two, ffn_weights[0], *near_two[1:], cotangent_far
    )
    middle = row_half(tokens).astype(F32) + add(mixed_out, mixed_far)
    second_norm, second_scale = normalize(middle)
    second_half = low(second_norm * gain_two)

    cotangents = [
        [cotangent_half, row_half(out_grad, 1 - bit)],
        [cotangent_far, swap(cotangent_far, "tp")],
    ]
    second_far = swap(second_half, "lo")
    near = [second_half, swap(second_half, "tp")]
    made = [[ffn(near, cotangents[0], [w]) for w in ffn_weights]]
    second_far = after(second_far, made[0][0][0])
    far = [second_far, swap(second_far, "tp")]
    made.append([ffn(far, cotangents[1], [w]) for w in ffn_weights])
    seconds = [near, far]
    hiddens = [[m[0] for m in side] for side in made]
    dpairs = [[m[1] for m in side] for side in made]
    gate_spans = tuple((f, 0, f, 0, 2 * chunk) for f in range(FFN_CHUNKS))
    down_spans = tuple((f, 0, f, 2 * chunk, chunk) for f in range(FFN_CHUNKS))

    def cores(part):
        return low(add(part[0], swap(part[1], "tp")))

    dsecond_far = ffn_back(dpairs[1], ffn_weights, gate_spans)
    dsecond_near = ffn_back(dpairs[0], ffn_weights, gate_spans)
    dsecond_got, dsecond_half = swap(cores(dsecond_far), "lo"), cores(dsecond_near)

    lefts, left_cots = after(
        (seconds[0] + seconds[1], cotangents[0] + cotangents[1]), *dsecond_near, *dsecond_far
    )
    ffn_given, ffn_own = [], []
    for f in range(FFN_CHUNKS):

        def part(s, f=f):
            return ffn_grads(
                lefts,
                left_cots,
                [side[f] for side in hiddens],
                [side[f] for side in dpairs],
                owners,
                slots_ffn,
                s,
                near_rows,
                own_rows,
            )

        ffn_given.append([part(s) for s in range(1, dp_count)])
        ffn_own.append(part(0))
    pair_rows = 2 * own_rows

    def over_dp_rows(f, first, *needed):
        return [
            turn(after(x[first : first + pair_rows], *needed), "dp", s + 1)
            for s, x in enumerate(ffn_given[f])
        ]

    def total_rows(f, first, got):
        total = ffn_own[f][first : first + pair_rows]
        for x in got:
            total = add(total, x)
        return low(total)

    far_one = over_dp_rows(0, pair_rows)
    near_one_got = over_dp_rows(0, 0, *far_one)
    far_two = over_dp_rows(1, pair_rows, *near_one_got)
    near_two_got = over_dp_rows(1, 0, *far_two)
    dsecond_got = after(dsecond_got, *ffn_given[1], ffn_own[0], *far_one)
    dsecond = low(add(dsecond_half, dsecond_got))
    hi_one = swap(total_rows(0, pair_rows, far_one), "hi")
    hiddens_late = after(hiddens, dsecond)
    out_far = ffn_back(hiddens_late[1], ffn_weights, down_spans)
    out_near = ffn_back(hiddens_late[0], ffn_weights, down_spans)

    def ffn_deliver(near, hi_got, needed):
        pair = add(near, hi_got)
        kept = pair[:own_rows]
        got = after(swap(low(pair[own_rows:]), "lo"), needed).astype(F32)
        return (jnp.where(parity == 0, kept, got), jnp.where(parity == 0, got, kept))

    dsecond = add(dsecond, after(
        swap(dsecond, "tp", 2), *ffn_own, *out_far, *out_near, *near_one_got
    ))
    gain_two_grad = jnp.sum(dsecond * second_norm, axis=0)
    scaled_two = dsecond * gain_two
    dmiddle = cotangent_half.astype(F32) + second_scale * (
        scaled_two - second_norm * jnp.mean(scaled_two * second_norm, axis=-1, keepdims=True)
    )
    out_half, out_far_got = cores(out_near), swap(cores(out_far), "lo")
    dmiddle_low = [low(dmiddle), after(swap(low(dmiddle), "tp"), out_half)]
    dmixed = project(dmiddle_low, qo_stack, places, bit_ref, head_width, head_width, cosine, sine, 0)
    dquery_low, dkey_own, dvalue_own, dprompt_own, *dprompts = attention_backward(
        order, rank, query, kv, mixed, lse, dmixed, cosine, sine, prompts
    )
    got = [swap(piece, CTX, k + 1) for k, piece in enumerate(dprompts)]
    far_two = after(far_two, dquery_low)
    hi_two = swap(total_rows(1, pair_rows, far_two), "hi")
    dkey_low, dvalue_low = merge_keys(
        mine[None], dkey_own, dvalue_own, dprompt_own, got, cosine, sine
    )

    def attn_grads(pairs):
        parts = [
            attn_grads_block(pairs, bit_ref, owners, slots_attn, s, near_rows, own_rows)
            for s in range(dp_count)
        ]
        total = parts[0]
        for s in range(1, dp_count):
            total = add(total, turn(parts[s], "dp", s))
        total = low(total)
        pair = add(total[: 2 * own_rows], swap(total[2 * own_rows :], "lo"))
        return total, pair[:own_rows] + swap(low(pair[own_rows:]), "hi").astype(F32)

    _, early = attn_grads([(dmiddle_low, mixed), ([first], dquery_low)])
    late_total, late = attn_grads([([first], dkey_low), ([first], dvalue_low)])
    ffn_sums = [
        ffn_deliver(total_rows(0, 0, near_one_got), after(hi_one, dquery_low), dkey_low),
        ffn_deliver(
            total_rows(1, 0, after(near_two_got, dquery_low)),
            after(hi_two, late_total),
            late_total,
        ),
    ]

    kept, given = project_back(
        [dquery_low, dkey_low, dvalue_low],
        ((0, 0), (1, 0), (1, head_width)),
        [qo_stack, kv_stack],
        places,
        bit_ref,
    )
    norm_half, norm_other = row_half(first_norm), row_half(first_norm, 1 - bit)
    gain_one_grad = jnp.sum(kept.astype(F32) * norm_half, axis=0) + jnp.sum(
        given.astype(F32) * norm_other, axis=0
    )
    dfirst = after(low(add(kept, swap(given, "tp"))), gain_one_grad)
    dfirst = add(dfirst, swap(dfirst, "tp", 2))
    scaled_one = dfirst * gain_one
    dinputs = dmiddle + row_half(first_scale) * (
        scaled_one - norm_half * jnp.mean(scaled_one * norm_half, axis=-1, keepdims=True)
    )

    share = width // tp_count
    here = tp_index // 2
    gains = jnp.stack([gain_one_grad, jnp.where(here == 0, gain_two_grad, 0.0)])
    for axis in ("tp", "lo", "hi", "dp"):
        mask = 1
        while mask < lax.axis_size(axis):
            gains = gains + swap(gains, axis, mask)
            mask *= 2

    def wide_part(values, which):
        return lax.dynamic_slice_in_dim(values, which * 2 * share, 2 * share, 1)

    def deliver(wide):
        kept = lax.dynamic_slice_in_dim(wide, bit * share, share, 1)
        given = lax.dynamic_slice_in_dim(wide, (1 - bit) * share, share, 1)
        return assemble(kept, swap(given, "tp"))

    in_grad = deliver(after(low(wide_part(dinputs, here)), gains))

    ffn_out = low(add(out_half, after(out_far_got, dquery_low)))
    ffn_out = add(wide_part(ffn_out, here), swap(wide_part(ffn_out, 1 - here), "tp", 2))
    block_out = deliver(low(wide_part(middle, here) + ffn_out))

    part = width // (dp_count * ctx_count)
    gains = lax.dynamic_slice_in_dim(gains, (dp_index * ctx_count + ctx_index) * part, part, 1)

    ffn_final = [
        jnp.concatenate(
            [
                ffn_sums[f][side][:, i * chunk : (i + 1) * chunk]
                for side in range(2)
                for f in range(FFN_CHUNKS)
            ],
            axis=1,
        )
        for i in range(3)
    ]
    return (
        block_out,
        in_grad,
        gains[0],
        early[:, head_width:],
        late[:, :head_width],
        late[:, head_width:],
        early[:, :head_width],
        gains[1],
        ffn_final[0],
        ffn_final[1],
        ffn_final[2],
    )


def solution(mesh):
    dp, ctx, tp = (mesh.shape[name] for name in ("dp", "ctx", "tp"))
    split_mesh = Mesh(mesh.devices.reshape(dp, ctx // 2, 2, tp), ("dp", "hi", "lo", "tp"))
    every = ("dp",) + CTX
    split = P(every, "tp")
    rows = P(every, None)
    vector = P(every)
    return jax.shard_map(
        body,
        mesh=split_mesh,
        in_specs=(rows, P(), split, split, split, split, P(), split, split, split)
        + (P("dp", None), P("dp", None), rows),
        out_specs=(split, split, vector, split, split, split, split, vector, split, split, split),
        check_vma=False,
    )
```

```python
import functools
import math

import jax
import jax.numpy as jnp
from jax import lax
from jax.experimental import pallas as pl
from jax.experimental.pallas import tpu as pltpu
from jax.sharding import Mesh
from jax.sharding import PartitionSpec as P

HEAD_DIM = 64
CLEN = 256
LANES = 128
EPS = 1e-05
ROPE_BASE = 130000.0
MASKED = -1e30
FFN_CHUNKS = 2
COST_SCALE = 16
BF16 = jnp.bfloat16
F32 = jnp.float32
VMEM_LIMIT = 32 * 1024 * 1024
VMEM_WHOLE = 60 * 1024 * 1024
CTX = ("hi", "lo")


def swap(values, axis, mask=1):
    count = lax.axis_size(axis)
    return lax.ppermute(values, axis, [(i, i ^ mask) for i in range(count)])


def turn(values, axis, shift):
    count = lax.axis_size(axis)
    return lax.ppermute(values, axis, [(i, (i + shift) % count) for i in range(count)])


def add(left, right):
    return left.astype(F32) + right.astype(F32)


def low(values):
    return values.astype(BF16)


def after(values, *needed):
    return lax.optimization_barrier((values,) + needed)[0]


def cost(flops, data, transcendentals=0):
    return pl.CostEstimate(
        flops=flops // COST_SCALE,
        bytes_accessed=data // COST_SCALE,
        transcendentals=transcendentals // COST_SCALE,
    )


def dot(left, right, dims):
    return lax.dot_general(left, right, (dims, ((), ())), preferred_element_type=F32)


NN = ((1,), (0,))
NT = ((1,), (1,))
TN = ((0,), (0,))
VMEM = pl.BlockSpec(memory_space=pltpu.VMEM)
SMEM = pl.BlockSpec(memory_space=pltpu.SMEM)


def at_block(index, size):
    return pl.ds(pl.multiple_of(index * size, size), size)


def half_swap(values):
    lane = lax.broadcasted_iota(jnp.int32, values.shape, 1)
    ahead = pltpu.roll(values, LANES - 32, 1)
    behind = pltpu.roll(values, 32, 1)
    return jnp.where((lane & 63) < 32, ahead, behind)


def call(kernel, operands, out_shape, name, flops, data, scratch=(), smem=(), transcendentals=0):
    many = isinstance(out_shape, list)
    return pl.pallas_call(
        kernel,
        in_specs=[SMEM] * len(smem) + [VMEM] * len(operands),
        out_specs=[VMEM] * len(out_shape) if many else VMEM,
        out_shape=out_shape,
        scratch_shapes=list(scratch),
        compiler_params=pltpu.CompilerParams(vmem_limit_bytes=VMEM_LIMIT),
        cost_estimate=cost(flops, data, transcendentals),
        name=name,
    )(*smem, *operands)


def fill(whole, pieces, place_ref, unit, column, width):
    at = 0
    for piece in pieces:
        for row in range(0, piece.shape[0], unit):
            whole[at_block(place_ref[at], unit), :] = piece[
                row : row + unit, column : column + width
            ]
            at += 1


def project_kernel(parts, column, width, rope_width, bit_ref, place_ref, *refs):
    x_refs = refs[:parts]
    w_refs = refs[parts:-5]
    cos_ref, sin_ref, out_ref, x_all, w_all = refs[-5:]
    fill(w_all, w_refs, place_ref, w_all.shape[0] // place_ref.shape[0], column, width)
    if parts == 2:
        rows = x_refs[0].shape[0]
        x_all[at_block(bit_ref[0], rows), :] = x_refs[0][...]
        x_all[at_block(1 - bit_ref[0], rows), :] = x_refs[1][...]
        x_ref = x_all
    else:
        x_ref = x_refs[0]
    tile = min(width, 256)

    def columns(first, rope):
        def step(t, carry):
            at = pl.multiple_of(first + t * tile, tile)
            total = dot(x_ref[...], w_all[:, pl.ds(at, tile)], NN)
            for c in range(0, tile, LANES):
                part = total[:, c : c + LANES]
                if rope:
                    part = part * cos_ref[...] + half_swap(part) * sin_ref[...]
                out_ref[:, pl.ds(pl.multiple_of(at + c, LANES), LANES)] = part.astype(BF16)
            return carry

        return step

    if rope_width:
        lax.fori_loop(0, rope_width // tile, columns(0, True), 0)
    if rope_width < width:
        lax.fori_loop(0, (width - rope_width) // tile, columns(rope_width, False), 0)


def project(x_parts, stack, places, bit, column, width, cosine, sine, rope_width):
    rows = sum(x.shape[0] for x in x_parts)
    depth = x_parts[0].shape[1]
    return call(
        functools.partial(project_kernel, len(x_parts), column, width, rope_width),
        [*x_parts, *stack, cosine, sine],
        jax.ShapeDtypeStruct((rows, width), BF16),
        "project",
        2 * rows * depth * width,
        2 * (rows * depth + depth * width + rows * width),
        [
            pltpu.VMEM((rows if len(x_parts) == 2 else 16, depth), BF16),
            pltpu.VMEM((depth, width), BF16),
        ],
        [bit, places],
    )


def place_kernel(count, place_ref, *refs):
    out_ref = refs[-1]
    unit = out_ref.shape[0] // count
    at = 0
    for ref in refs[:-1]:
        for row in range(0, ref.shape[0], unit):
            out_ref[at_block(place_ref[at], unit), :] = ref[row : row + unit, :]
            at += 1


def place_rows(pieces, places):
    rows, width = sum(p.shape[0] for p in pieces), pieces[0].shape[1]
    return call(
        functools.partial(place_kernel, places.shape[0]),
        pieces,
        jax.ShapeDtypeStruct((rows, width), BF16),
        "place_rows",
        0,
        4 * rows * width,
        smem=[places],
    )


def ffn_kernel(chunks, *refs):
    x_refs, cot_refs = refs[:2], refs[2:4]
    w_refs = refs[4 : 4 + chunks]
    hidden_ref, dpair_ref = refs[4 + chunks :]
    rows = x_refs[0].shape[0]
    wide = w_refs[0].shape[1] // 3
    tile = min(wide, 256)
    for f, w_ref in enumerate(w_refs):

        def step(t, carry, f=f, w_ref=w_ref):
            for part in range(2):
                x, g = x_refs[part][...], cot_refs[part][...]
                gate = dot(x, w_ref[:, pl.ds(pl.multiple_of(t * tile, tile), tile)], NN)
                upward = dot(x, w_ref[:, pl.ds(pl.multiple_of(wide + t * tile, tile), tile)], NN)
                dhidden = dot(g, w_ref[:, pl.ds(pl.multiple_of(2 * wide + t * tile, tile), tile)], NN)
                sig = 1.0 / (1.0 + jnp.exp(-gate))
                silu = gate * sig
                at = slice(part * rows, (part + 1) * rows)
                hidden_ref[at, pl.ds(pl.multiple_of(f * wide + t * tile, tile), tile)] = (
                    silu * upward
                ).astype(BF16)
                dpair_ref[at, pl.ds(pl.multiple_of(2 * f * wide + t * tile, tile), tile)] = (
                    dhidden * upward * (sig + silu * (1.0 - sig))
                ).astype(BF16)
                dpair_ref[at, pl.ds(pl.multiple_of((2 * f + 1) * wide + t * tile, tile), tile)] = (
                    dhidden * silu
                ).astype(BF16)
            return carry

        lax.fori_loop(0, wide // tile, step, 0)


def ffn(seconds, cotangents, weights):
    rows = 2 * seconds[0].shape[0]
    width = seconds[0].shape[1]
    units = sum(w.shape[1] for w in weights) // 3
    return call(
        functools.partial(ffn_kernel, len(weights)),
        [*seconds, *cotangents, *weights],
        [jax.ShapeDtypeStruct((rows, units), BF16), jax.ShapeDtypeStruct((rows, 2 * units), BF16)],
        "ffn",
        6 * rows * width * units,
        2 * (2 * rows * width + 3 * width * units + 3 * rows * units),
        transcendentals=rows * units,
    )


def back_kernel(spans, *refs):
    count = 1 + max(span[2] for span in spans)
    lefts = refs[: 1 + max(span[0] for span in spans)]
    rights = refs[len(lefts) : len(lefts) + count]
    outs = refs[len(lefts) + count :]
    rows, width = outs[0].shape
    tile = 256

    def step(t, carry):
        for part, out_ref in enumerate(outs):
            total = None
            for left, l_at, right, r_at, wide in spans:
                term = dot(
                    lefts[left][part * rows : (part + 1) * rows, l_at : l_at + wide],
                    rights[right][at_block(t, tile), r_at : r_at + wide],
                    NT,
                )
                total = term if total is None else total + term
            out_ref[:, at_block(t, tile)] = total.astype(BF16)
        return carry

    lax.fori_loop(0, width // tile, step, 0)


def ffn_back(lefts, weights, spans):
    rows = lefts[0].shape[0]
    width = weights[0].shape[0]
    depth = sum(span[4] for span in spans)
    return call(
        functools.partial(back_kernel, spans),
        [*lefts, *weights],
        [jax.ShapeDtypeStruct((rows // 2, width), BF16)] * 2,
        "ffn_back",
        2 * rows * width * depth,
        2 * (rows * depth + width * depth + rows * width),
    )


def project_back_kernel(columns, counts, bit_ref, place_ref, *refs):
    lefts = refs[: len(columns)]
    at, stacks = len(columns), []
    for count in counts:
        stacks.append(refs[at : at + count])
        at += count
    outs, w_all = refs[at : at + 2], refs[at + 2]
    rows, width = outs[0].shape
    unit = width // place_ref.shape[0]
    wide = lefts[0].shape[1]
    for n, (which, column) in enumerate(columns):
        at = 0
        for piece in stacks[which]:
            for row in range(0, piece.shape[0], unit):
                w_all[at_block(place_ref[at], unit), n * wide : (n + 1) * wide] = piece[
                    row : row + unit, column : column + wide
                ]
                at += 1
    tile = 256

    def step(t, carry):
        for part, out_ref in enumerate(outs):
            which = bit_ref[0] if part == 0 else 1 - bit_ref[0]
            total = None
            for n, left in enumerate(lefts):
                term = dot(
                    left[at_block(which, rows), :],
                    w_all[at_block(t, tile), n * wide : (n + 1) * wide],
                    NT,
                )
                total = term if total is None else total + term
            out_ref[:, at_block(t, tile)] = total.astype(BF16)
        return carry

    lax.fori_loop(0, width // tile, step, 0)


def project_back(lefts, columns, stacks, places, bit):
    rows, wide = lefts[0].shape
    width = sum(piece.shape[0] for piece in stacks[0])
    depth = wide * len(lefts)
    return call(
        functools.partial(project_back_kernel, columns, tuple(len(s) for s in stacks)),
        [*lefts, *[piece for stack in stacks for piece in stack]],
        [jax.ShapeDtypeStruct((rows // 2, width), BF16)] * 2,
        "project_back",
        2 * rows * width * depth,
        2 * (rows * depth + width * depth + rows * width),
        [pltpu.VMEM((width, depth), BF16)],
        [bit, places],
    )


def store_blocks(out_ref, values, first, unit, slot_ref, column):
    wide = values.shape[1]
    for row in range(0, values.shape[0], unit):
        slot = slot_ref[(first + row) // unit]
        out_ref[at_block(slot, unit), column : column + wide] = values[row : row + unit]


def ffn_grads_kernel(tile, unit, dp_ref, slot_ref, *refs):
    del dp_ref
    x_refs, cot_refs = refs[:4], refs[4:8]
    hiddens, dpairs, out_ref = refs[8:10], refs[10:12], refs[12]
    rows = x_refs[0].shape[0]
    wide = hiddens[0].shape[1]

    def product(lefts, rights):
        total = None
        for n, left in enumerate(lefts):
            part = slice((n % 2) * rows, (n % 2 + 1) * rows)
            term = dot(left[...], rights[n // 2][part, :], TN)
            total = term if total is None else total + term
        return total.astype(BF16)

    first = pl.program_id(0) * tile
    store_blocks(out_ref, product(x_refs, dpairs), first, unit, slot_ref, 0)
    store_blocks(out_ref, product(cot_refs, hiddens), first, unit, slot_ref, 2 * wide)


def ffn_grads(seconds, cotangents, hiddens, dpairs, owners, slots, s, count, unit):
    half, wide = seconds[0].shape[0], hiddens[0].shape[1]
    rows = 4 * half
    tile = 256
    left = pl.BlockSpec((half, tile), lambda t, dp, slot: (0, dp[s] * (count // tile) + t))
    whole = lambda x: pl.BlockSpec(x.shape, lambda t, dp, slot: (0, 0))
    return pl.pallas_call(
        functools.partial(ffn_grads_kernel, tile, unit),
        grid_spec=pltpu.PrefetchScalarGridSpec(
            num_scalar_prefetch=2,
            grid=(count // tile,),
            in_specs=[left] * 8 + [whole(x) for x in (*hiddens, *dpairs)],
            out_specs=pl.BlockSpec((count, 3 * wide), lambda t, dp, slot: (0, 0)),
        ),
        out_shape=jax.ShapeDtypeStruct((count, 3 * wide), BF16),
        compiler_params=pltpu.CompilerParams(vmem_limit_bytes=VMEM_WHOLE),
        cost_estimate=cost(
            6 * rows * count * wide,
            2 * (2 * rows * count + 3 * rows * wide + 3 * count * wide),
        ),
        name="ffn_grads",
    )(owners, slots, *seconds, *cotangents, *hiddens, *dpairs)


def attn_grads_kernel(kinds, s, unit, bit_ref, dp_ref, slot_ref, *refs):
    at, pairs = 0, []
    for parts in kinds:
        pairs.append((refs[at : at + parts], refs[at + parts]))
        at += parts + 1
    out_ref = refs[at]
    count = out_ref.shape[0]
    tile = 256

    def step(t, carry):
        where = pl.ds(pl.multiple_of(dp_ref[s] * count + t * tile, tile), tile)
        column = 0
        for lefts, right in pairs:
            if len(lefts) == 1:
                total = dot(lefts[0][:, where], right[...], TN)
            else:
                rows = lefts[0].shape[0]
                total = dot(lefts[0][:, where], right[at_block(bit_ref[0], rows), :], TN) + dot(
                    lefts[1][:, where], right[at_block(1 - bit_ref[0], rows), :], TN
                )
            store_blocks(out_ref, total.astype(BF16), t * tile, unit, slot_ref, column)
            column += right.shape[1]
        return carry

    lax.fori_loop(0, count // tile, step, 0)


def attn_grads_block(pairs, bit, owners, slots, s, count, unit):
    kinds = tuple(len(lefts) for lefts, _ in pairs)
    width = sum(right.shape[1] for _, right in pairs)
    rows = pairs[0][1].shape[0]
    return call(
        functools.partial(attn_grads_kernel, kinds, s, unit),
        [x for lefts, right in pairs for x in (*lefts, right)],
        jax.ShapeDtypeStruct((count, width), BF16),
        "attn_grads",
        2 * rows * width * count,
        2 * (rows * count + rows * width + count * width),
        smem=[bit, owners, slots],
    )


SCALE = HEAD_DIM**-0.5
SCALE_LOG2 = SCALE * math.log2(math.e)


def forward_kernel(pieces, order_ref, rank_ref, q_ref, ks_ref, vs_ref, *refs):
    kp_refs, vp_refs = refs[:pieces], refs[pieces : 2 * pieces]
    o_ref, lse_ref = refs[2 * pieces :]
    q = q_ref[...]
    size = q.shape[0]
    prompt = pl.program_id(1) == 0
    low_lane = lax.broadcasted_iota(jnp.int32, q.shape, 1) < HEAD_DIM
    causal = lax.broadcasted_iota(jnp.int32, (size, size), 0) >= lax.broadcasted_iota(
        jnp.int32, (size, size), 1
    )
    outs = []
    for head in range(2):
        own = low_lane if head == 0 else jnp.logical_not(low_lane)
        qh = jnp.where(own, q, jnp.zeros_like(q))
        raw = [jnp.where(causal, dot(qh, ks_ref[...], NT), MASKED)]
        for s in range(pieces):
            hidden = jnp.logical_and(prompt, rank_ref[s] >= rank_ref[0])
            raw.append(dot(qh, kp_refs[s][...], NT) + jnp.where(hidden, MASKED, 0.0))
        top = raw[0]
        for r in raw[1:]:
            top = jnp.maximum(top, r)
        top = jnp.max(top, axis=-1, keepdims=True) * SCALE_LOG2
        sums, acc = None, None
        for s, r in enumerate(raw):
            e = jnp.exp2(r * SCALE_LOG2 - top)
            v = vs_ref if s == 0 else vp_refs[s - 1]
            term = dot(e.astype(BF16), v[...], NN)
            sums = e if sums is None else sums + e
            acc = term if acc is None else acc + term
        total = jnp.sum(sums, axis=-1, keepdims=True)
        outs.append((acc / total, top + jnp.log2(total)))
    o_ref[...] = jnp.where(low_lane, outs[0][0], outs[1][0]).astype(BF16)
    lse_ref[...] = jnp.where(low_lane, outs[0][1], outs[1][1])


def backward_kernel(
    pieces, order_ref, rank_ref, q_ref, ks_ref, vs_ref, o_ref, lse_ref, do_ref, cos_ref, sin_ref, *refs
):
    kp_refs, vp_refs = refs[:pieces], refs[pieces : 2 * pieces]
    dq_ref, dks_ref, dvs_ref = refs[2 * pieces : 2 * pieces + 3]
    piece_refs = refs[2 * pieces + 3 : 3 * pieces + 3]
    acc_ref = refs[-1]
    pair, step = pl.program_id(0), pl.program_id(1)
    prompt = step == 0
    q, do = q_ref[...], do_ref[...]
    size = q.shape[0]
    low_lane = lax.broadcasted_iota(jnp.int32, q.shape, 1) < HEAD_DIM
    causal = lax.broadcasted_iota(jnp.int32, (size, size), 0) >= lax.broadcasted_iota(
        jnp.int32, (size, size), 1
    )
    product = do.astype(F32) * o_ref[...].astype(F32)
    lse = lse_ref[...]
    dq_heads = []
    dk_all = [None] * (pieces + 1)
    dv_all = [None] * (pieces + 1)
    for head in range(2):
        own = low_lane if head == 0 else jnp.logical_not(low_lane)
        qh = jnp.where(own, q, jnp.zeros_like(q))
        doh = jnp.where(own, do, jnp.zeros_like(do))
        delta = jnp.sum(jnp.where(own, product, 0.0), axis=-1, keepdims=True)
        log_sum = lse[:, head * HEAD_DIM : head * HEAD_DIM + 1]
        dq = None
        for s in range(pieces + 1):
            k = (ks_ref if s == 0 else kp_refs[s - 1])[...]
            v = (vs_ref if s == 0 else vp_refs[s - 1])[...]
            raw = dot(qh, k, NT)
            if s == 0:
                raw = jnp.where(causal, raw, MASKED)
            else:
                hidden = jnp.logical_and(prompt, rank_ref[s - 1] >= rank_ref[0])
                raw = raw + jnp.where(hidden, MASKED, 0.0)
            prob = jnp.exp2(raw * SCALE_LOG2 - log_sum)
            ds = (prob * (dot(doh, v, NT) - delta)).astype(BF16)
            term = dot(ds, k, NN)
            dq = term if dq is None else dq + term
            dk = dot(ds, qh, TN)
            dv = dot(prob.astype(BF16), doh, TN)
            dk_all[s] = dk if dk_all[s] is None else dk_all[s] + dk
            dv_all[s] = dv if dv_all[s] is None else dv_all[s] + dv
        dq_heads.append(dq)
    dq = jnp.where(low_lane, dq_heads[0], dq_heads[1]) * SCALE
    cosine, sine = cos_ref[...], sin_ref[...]
    dq_ref[...] = (dq * cosine - half_swap(dq) * sine).astype(BF16)
    dks_ref[...] = dk_all[0] * SCALE
    dvs_ref[...] = dv_all[0]
    for s in range(pieces):
        both = jnp.concatenate([dk_all[s + 1] * SCALE, dv_all[s + 1]], axis=1)
        at = slice(s * size, (s + 1) * size)

        @pl.when(prompt)
        def _(both=both, at=at):
            acc_ref[at, :] = both

        @pl.when(jnp.logical_not(prompt))
        def _(both=both, at=at):
            acc_ref[at, :] += both

    @pl.when(step == pl.num_programs(1) - 1)
    def _():
        wide = piece_refs[0].shape[1] // 2
        k_at = pl.ds(pl.multiple_of(pair * LANES, LANES), LANES)
        v_at = pl.ds(pl.multiple_of(wide + pair * LANES, LANES), LANES)
        for s in range(pieces):
            both = acc_ref[s * size : (s + 1) * size, :]
            piece_refs[s][:, k_at] = both[:, :LANES].astype(piece_refs[s].dtype)
            piece_refs[s][:, v_at] = both[:, LANES:].astype(piece_refs[s].dtype)


def merge_kernel(others, mine_ref, dk_ref, dv_ref, own_ref, *refs):
    got = refs[:others]
    cos_ref, sin_ref, dk_out, dv_out = refs[others:]
    width = dk_ref.shape[1]
    cosine, sine = cos_ref[...], sin_ref[...]

    def write(dk, dv):
        for at in range(0, width, LANES):
            part = dk[:, at : at + LANES]
            dk_out[:, at : at + LANES] = (part * cosine - half_swap(part) * sine).astype(BF16)
        dv_out[...] = dv.astype(BF16)

    mine = pl.program_id(0) == mine_ref[0]

    @pl.when(mine)
    def _():
        extra = own_ref[...]
        for ref in got:
            extra = extra + ref[...].astype(F32)
        write(dk_ref[...] + extra[:, :width], dv_ref[...] + extra[:, width:])

    @pl.when(jnp.logical_not(mine))
    def _():
        write(dk_ref[...], dv_ref[...])


def merge_keys(mine, dkey, dvalue, own, got, cosine, sine):
    rows, width = dkey.shape
    row = lambda i, mine: (i, 0)
    full = lambda i, mine: (0, 0)
    return pl.pallas_call(
        functools.partial(merge_kernel, len(got)),
        grid_spec=pltpu.PrefetchScalarGridSpec(
            num_scalar_prefetch=1,
            grid=(rows // CLEN,),
            in_specs=[pl.BlockSpec((CLEN, width), row)] * 2
            + [pl.BlockSpec((CLEN, 2 * width), full)] * (1 + len(got))
            + [pl.BlockSpec((CLEN, LANES), row)] * 2,
            out_specs=[pl.BlockSpec((CLEN, width), row)] * 2,
        ),
        out_shape=[jax.ShapeDtypeStruct((rows, width), BF16)] * 2,
        compiler_params=pltpu.CompilerParams(vmem_limit_bytes=VMEM_LIMIT),
        cost_estimate=cost(8 * rows * width, 16 * rows * width, 0),
        name="merge_keys",
    )(mine, dkey, dvalue, own, *got, cosine, sine)


def attention_specs(pieces, key_pairs):
    own = pl.BlockSpec((CLEN, LANES), lambda h, j, order, rank: (order[j], h))
    own_value = pl.BlockSpec((CLEN, LANES), lambda h, j, order, rank: (order[j], key_pairs + h))
    key = pl.BlockSpec((CLEN, LANES), lambda h, j, order, rank: (0, h))
    value = pl.BlockSpec((CLEN, LANES), lambda h, j, order, rank: (0, key_pairs + h))
    trig = pl.BlockSpec((CLEN, LANES), lambda h, j, order, rank: (order[j], 0))
    prompt = pl.BlockSpec((CLEN, 2 * key_pairs * LANES), lambda h, j, order, rank: (0, 0))
    return own, own_value, key, value, trig, prompt


def attention_forward(order, rank, query, kv, prompts):
    rows, width = query.shape
    pieces, pairs = len(prompts), width // LANES
    own, own_value, key, value, _, _ = attention_specs(pieces, pairs)
    scores = rows * (pieces + 1) * CLEN * (width // HEAD_DIM)
    return pl.pallas_call(
        functools.partial(forward_kernel, pieces),
        grid_spec=pltpu.PrefetchScalarGridSpec(
            num_scalar_prefetch=2,
            grid=(pairs, rows // CLEN),
            in_specs=[own, own, own_value] + [key] * pieces + [value] * pieces,
            out_specs=[own, own],
        ),
        out_shape=[jax.ShapeDtypeStruct((rows, width), BF16), jax.ShapeDtypeStruct((rows, width), F32)],
        compiler_params=pltpu.CompilerParams(vmem_limit_bytes=VMEM_LIMIT),
        cost_estimate=cost(
            16 * scores * HEAD_DIM, 16 * rows * width, scores
        ),
        name="attend",
    )(order, rank, query, kv, kv, *prompts, *prompts)


def attention_backward(order, rank, query, kv, mixed, lse, dmixed, cosine, sine, prompts):
    rows, width = query.shape
    pieces, pairs = len(prompts), width // LANES
    own, own_value, key, value, trig, prompt = attention_specs(pieces, pairs)
    scores = rows * (pieces + 1) * CLEN * (width // HEAD_DIM)
    return pl.pallas_call(
        functools.partial(backward_kernel, pieces),
        grid_spec=pltpu.PrefetchScalarGridSpec(
            num_scalar_prefetch=2,
            grid=(pairs, rows // CLEN),
            in_specs=[own, own, own_value, own, own, own] + [trig] * 2 + [key] * pieces + [value] * pieces,
            out_specs=[own, own, own] + [prompt] * pieces,
            scratch_shapes=[pltpu.VMEM((pieces * CLEN, 2 * LANES), F32)],
        ),
        out_shape=[
            jax.ShapeDtypeStruct((rows, width), BF16),
            jax.ShapeDtypeStruct((rows, width), F32),
            jax.ShapeDtypeStruct((rows, width), F32),
        ]
        + [jax.ShapeDtypeStruct((CLEN, 2 * width), BF16 if s else F32) for s in range(pieces)],
        compiler_params=pltpu.CompilerParams(vmem_limit_bytes=VMEM_LIMIT),
        cost_estimate=cost(
            40 * scores * HEAD_DIM, 32 * rows * width, scores
        ),
        name="attend_back",
    )(order, rank, query, kv, kv, mixed, lse, dmixed, cosine, sine, *prompts, *prompts)


def normalize(values):
    factor = lax.rsqrt(jnp.mean(values * values, axis=-1, keepdims=True) + EPS)
    return (values * factor, factor)


def rope_tables(where):
    half = HEAD_DIM // 2
    freqs = ROPE_BASE ** (-(jnp.arange(half).astype(F32) * 2.0) / HEAD_DIM)
    angles = where.astype(F32)[:, None] * freqs[None, :]
    cosine, sine = jnp.cos(angles), jnp.sin(angles)
    return (
        jnp.concatenate([cosine] * 4, axis=1),
        jnp.concatenate([-sine, sine, -sine, sine], axis=1),
    )


def body(
    tokens,
    attn_gain,
    query_weight,
    key_weight,
    value_weight,
    out_weight,
    ffn_gain,
    gate_weight,
    up_weight,
    down_weight,
    seq_ids,
    positions,
    out_grad,
):
    rows, width = tokens.shape
    head_width = query_weight.shape[1]
    own_rows, ffn_width = gate_weight.shape
    half_units = ffn_width // 2
    chunk = half_units // FFN_CHUNKS
    half = rows // 2
    dp_count = lax.axis_size("dp")
    ctx_count = lax.axis_size("hi") * 2
    tp_count = lax.axis_size("tp")
    dp_index = lax.axis_index("dp")
    parity = lax.axis_index("lo")
    ctx_index = lax.axis_index("hi") * 2 + parity
    tp_index = lax.axis_index("tp")
    bit = tp_index & 1
    bit_ref = bit.astype(jnp.int32)[None]

    def row_half(values, which=bit):
        return lax.dynamic_slice_in_dim(values, which * half, half)

    def assemble(mine, other):
        first = jnp.where(bit == 0, mine, other)
        last = jnp.where(bit == 0, other, mine)
        return jnp.concatenate([first, last], axis=0)

    slots = jnp.arange(dp_count * ctx_count, dtype=jnp.int32)

    def places_of(order_k):
        slot_k = jnp.array(order_k, jnp.int32)[slots % ctx_count]
        return (
            lax.rem(dp_index + slots // ctx_count, dp_count) * ctx_count + (ctx_index ^ slot_k)
        ).astype(jnp.int32)

    def slots_of(order_k):
        slot_of = jnp.array([order_k.index(k) for k in range(ctx_count)], jnp.int32)
        return slot_of[ctx_index ^ jnp.arange(ctx_count, dtype=jnp.int32)]

    attn_order, ffn_order = (0, 2, 1, 3), (0, 1, 2, 3)
    places, places_ffn = places_of(attn_order), places_of(ffn_order)
    slots_attn, slots_ffn = slots_of(attn_order), slots_of(ffn_order)
    owners = lax.rem(dp_index + jnp.arange(dp_count, dtype=jnp.int32), dp_count).astype(jnp.int32)
    near_rows = width // dp_count

    def over_dp(blocks):
        return blocks + [turn(x, "dp", -s) for s in range(1, dp_count) for x in blocks]

    kv_weight = jnp.concatenate([key_weight, value_weight], axis=1)
    kv_one, kv_two = swap(kv_weight, "lo"), swap(kv_weight, "hi")
    kv_three = swap(kv_two, "lo")
    kv_stack = over_dp([kv_weight, kv_two, kv_one, kv_three])
    qo_weight = after(jnp.concatenate([query_weight, out_weight], axis=1), kv_three)
    qo_two = swap(qo_weight, "hi")
    qo_even = jnp.concatenate([qo_weight, qo_two], axis=0)
    qo_odd = swap(qo_even, "lo")
    qo_stack = over_dp([qo_even, qo_odd])

    def ffn_columns(f, which):
        first = which * half_units + f * chunk
        return jnp.concatenate(
            [
                lax.dynamic_slice_in_dim(w, first, chunk, 1)
                for w in (gate_weight, up_weight, down_weight)
            ],
            axis=1,
        )

    def ffn_sends(f, *needed):
        keep, give = after((ffn_columns(f, parity), ffn_columns(f, 1 - parity)), *needed)
        near = jnp.concatenate([keep, swap(give, "lo")], axis=0)
        return near, swap(keep, "hi"), give

    def ffn_stack(near_blocks, far_blocks):
        return place_rows([x for both in zip(near_blocks, far_blocks) for x in both], places_ffn)

    def gather_dp(own):
        return [own] + [turn(own, "dp", -s) for s in range(1, dp_count)]

    group_seq = seq_ids[0].reshape(ctx_count, rows // CLEN, CLEN)[:, :, 0]
    group_pos = positions[0].reshape(ctx_count, rows // CLEN, CLEN)[:, :, 0]
    prompt_at = jnp.argmax(group_seq == 0, axis=1).astype(jnp.int32)
    prompt_rank = jnp.sum(jnp.where(group_seq == 0, group_pos, 0), axis=1).astype(jnp.int32)
    rank = prompt_rank[ctx_index ^ jnp.arange(ctx_count, dtype=jnp.int32)]
    mine = prompt_at[ctx_index]
    pieces = jnp.arange(rows // CLEN, dtype=jnp.int32)
    order = jnp.where(pieces == 0, mine, jnp.where(pieces <= mine, pieces - 1, pieces))
    own_pos = lax.dynamic_slice_in_dim(positions[0], ctx_index * rows, rows)
    cosine, sine = rope_tables(own_pos)

    gain_one = attn_gain[None].astype(F32)
    gain_two = ffn_gain[None].astype(F32)
    first_norm, first_scale = normalize(tokens.astype(F32))
    first = low(first_norm * gain_one)

    kv = project(
        [after(first, qo_two)], kv_stack, places, bit_ref, 0, 2 * head_width, cosine, sine, head_width
    )
    prompt_own = lax.dynamic_slice_in_dim(kv, mine * CLEN, CLEN)
    prompts = [prompt_own] + [swap(prompt_own, CTX, k) for k in range(1, ctx_count)]
    near_one, two_one, give_one = ffn_sends(0, kv_three)
    query = project(
        [after(first, two_one, near_one)],
        qo_stack,
        places,
        bit_ref,
        0,
        head_width,
        cosine,
        sine,
        head_width,
    )
    near_one = gather_dp(near_one)
    cotangent_half = row_half(out_grad)
    cotangent_far = swap(after(cotangent_half, *prompts[1:]), "lo")
    three_one = swap(after(give_one, kv_stack[-1]), CTX, 3)
    query = after(query, *near_one[1:], three_one)
    mixed, lse = attention_forward(order, rank, query, kv, prompts)
    near_two, two_two, give_two = ffn_sends(1, *prompts[1:])
    near_two = gather_dp(after(near_two, two_one, *qo_stack[2:]))
    mixed = after(mixed, two_two, *near_two[1:])
    three_two = swap(after(give_two, three_one), CTX, 3)
    far_one_blocks = gather_dp(jnp.concatenate([two_one, three_one], axis=0))
    far_two_blocks = gather_dp(jnp.concatenate([two_two, three_two], axis=0))
    ffn_weights = [ffn_stack(near_one, far_one_blocks), ffn_stack(near_two, far_two_blocks)]

    kept, given = project_back(
        [mixed], ((0, head_width),), [qo_stack], places, bit_ref
    )
    mixed_out = low(add(kept, after(swap(given, "tp"), three_two)))
    mixed_far = after(
        swap(mixed_out, "tp", 2), ffn_weights[0], cotangent_far
    )
    middle = row_half(tokens).astype(F32) + add(mixed_out, mixed_far)
    second_norm, second_scale = normalize(middle)
    second_half = low(second_norm * gain_two)

    cotangents = [
        [cotangent_half, row_half(out_grad, 1 - bit)],
        [cotangent_far, swap(cotangent_far, "tp")],
    ]
    second_far = swap(second_half, "lo")
    near = [second_half, after(swap(second_half, "tp"), *far_two_blocks[1:])]
    made = [[ffn(near, cotangents[0], [w]) for w in ffn_weights]]
    gate_spans = tuple((f, 0, f, 0, 2 * chunk) for f in range(FFN_CHUNKS))
    down_spans = tuple((f, 0, f, 2 * chunk, chunk) for f in range(FFN_CHUNKS))
    dsecond_near = ffn_back([m[1] for m in made[0]], ffn_weights, gate_spans)
    second_far = after(second_far, *dsecond_near)
    far = [second_far, swap(second_far, "tp")]
    made.append([ffn(far, cotangents[1], [w]) for w in ffn_weights])
    seconds = [near, far]
    hiddens = [[m[0] for m in side] for side in made]
    dpairs = [[m[1] for m in side] for side in made]

    def cores(part):
        return low(add(part[0], swap(part[1], "tp")))

    dsecond_far = ffn_back(dpairs[1], ffn_weights, gate_spans)
    dsecond_got, dsecond_half = swap(cores(dsecond_far), "lo"), cores(dsecond_near)

    lefts, left_cots = after(
        (seconds[0] + seconds[1], cotangents[0] + cotangents[1]), *dsecond_near, *dsecond_far
    )
    ffn_given, ffn_own = [], []
    for f in range(FFN_CHUNKS):

        def part(s, f=f):
            return ffn_grads(
                lefts,
                left_cots,
                [side[f] for side in hiddens],
                [side[f] for side in dpairs],
                owners,
                slots_ffn,
                s,
                near_rows,
                own_rows,
            )

        ffn_given.append([part(s) for s in range(1, dp_count)])
        ffn_own.append(part(0))
    pair_rows = 2 * own_rows

    def over_dp_rows(f, first, *needed):
        return [
            turn(after(x[first : first + pair_rows], *needed), "dp", s + 1)
            for s, x in enumerate(ffn_given[f])
        ]

    def total_rows(f, first, got):
        total = ffn_own[f][first : first + pair_rows]
        for x in got:
            total = add(total, x)
        return low(total)

    far_one = over_dp_rows(0, pair_rows)
    near_one_got = over_dp_rows(0, 0, *far_one)
    far_two = over_dp_rows(1, pair_rows, *near_one_got)
    near_two_got = over_dp_rows(1, 0, *near_one_got)
    dsecond_got = after(dsecond_got, *ffn_given[1], ffn_own[0], *far_one)
    dsecond = low(add(dsecond_half, dsecond_got))
    hi_one = swap(total_rows(0, pair_rows, far_one), "hi")
    hiddens_late = after(hiddens, dsecond)
    out_far = ffn_back(hiddens_late[1], ffn_weights, down_spans)
    out_near = ffn_back(hiddens_late[0], ffn_weights, down_spans)

    def ffn_deliver(near, hi_got, needed):
        pair = add(near, hi_got)
        kept = pair[:own_rows]
        got = after(swap(low(pair[own_rows:]), "lo"), needed).astype(F32)
        return (jnp.where(parity == 0, kept, got), jnp.where(parity == 0, got, kept))

    dsecond = add(dsecond, after(
        swap(dsecond, "tp", 2), *ffn_own, *out_far, *out_near, *near_one_got
    ))
    gain_two_grad = jnp.sum(dsecond * second_norm, axis=0)
    scaled_two = dsecond * gain_two
    dmiddle = cotangent_half.astype(F32) + second_scale * (
        scaled_two - second_norm * jnp.mean(scaled_two * second_norm, axis=-1, keepdims=True)
    )
    out_half, out_far_got = cores(out_near), swap(cores(out_far), "lo")
    dmiddle_low = [low(dmiddle), after(swap(low(dmiddle), "tp"), out_half)]
    dmixed = project(dmiddle_low, qo_stack, places, bit_ref, head_width, head_width, cosine, sine, 0)
    dquery_low, dkey_own, dvalue_own, dprompt_own, *dprompts = attention_backward(
        order, rank, query, kv, mixed, lse, dmixed, cosine, sine, prompts
    )
    got = [swap(piece, CTX, k + 1) for k, piece in enumerate(dprompts)]
    far_two = after(far_two, dquery_low)
    hi_two = swap(total_rows(1, pair_rows, far_two), "hi")
    dkey_low, dvalue_low = merge_keys(
        mine[None], dkey_own, dvalue_own, dprompt_own, got, cosine, sine
    )

    def attn_grads(pairs):
        parts = [
            attn_grads_block(pairs, bit_ref, owners, slots_attn, s, near_rows, own_rows)
            for s in range(dp_count)
        ]
        total = parts[0]
        for s in range(1, dp_count):
            total = add(total, turn(parts[s], "dp", s))
        total = low(total)
        pair = add(total[: 2 * own_rows], swap(total[2 * own_rows :], "lo"))
        return total, pair[:own_rows] + swap(low(pair[own_rows:]), "hi").astype(F32)

    _, early = attn_grads([(dmiddle_low, mixed), ([first], dquery_low)])
    late_total, late = attn_grads([([first], dkey_low), ([first], dvalue_low)])
    ffn_sums = [
        ffn_deliver(total_rows(0, 0, near_one_got), after(hi_one, dquery_low), dkey_low),
        ffn_deliver(
            total_rows(1, 0, after(near_two_got, dquery_low)),
            after(hi_two, late_total),
            late_total,
        ),
    ]

    kept, given = project_back(
        [dquery_low, dkey_low, dvalue_low],
        ((0, 0), (1, 0), (1, head_width)),
        [qo_stack, kv_stack],
        places,
        bit_ref,
    )
    norm_half, norm_other = row_half(first_norm), row_half(first_norm, 1 - bit)
    gain_one_grad = jnp.sum(kept.astype(F32) * norm_half, axis=0) + jnp.sum(
        given.astype(F32) * norm_other, axis=0
    )
    dfirst = after(low(add(kept, swap(given, "tp"))), gain_one_grad)
    dfirst = add(dfirst, swap(dfirst, "tp", 2))
    scaled_one = dfirst * gain_one
    dinputs = dmiddle + row_half(first_scale) * (
        scaled_one - norm_half * jnp.mean(scaled_one * norm_half, axis=-1, keepdims=True)
    )

    share = width // tp_count
    here = tp_index // 2
    gains = jnp.stack([gain_one_grad, jnp.where(here == 0, gain_two_grad, 0.0)])
    for axis in ("tp", "lo", "hi", "dp"):
        mask = 1
        while mask < lax.axis_size(axis):
            gains = gains + swap(gains, axis, mask)
            mask *= 2

    def wide_part(values, which):
        return lax.dynamic_slice_in_dim(values, which * 2 * share, 2 * share, 1)

    def deliver(wide):
        kept = lax.dynamic_slice_in_dim(wide, bit * share, share, 1)
        given = lax.dynamic_slice_in_dim(wide, (1 - bit) * share, share, 1)
        return assemble(kept, swap(given, "tp"))

    in_grad = deliver(after(low(wide_part(dinputs, here)), gains))

    ffn_out = low(add(out_half, after(out_far_got, dquery_low)))
    ffn_out = add(wide_part(ffn_out, here), swap(wide_part(ffn_out, 1 - here), "tp", 2))
    block_out = deliver(low(wide_part(middle, here) + ffn_out))

    part = width // (dp_count * ctx_count)
    gains = lax.dynamic_slice_in_dim(gains, (dp_index * ctx_count + ctx_index) * part, part, 1)

    ffn_final = [
        jnp.concatenate(
            [
                ffn_sums[f][side][:, i * chunk : (i + 1) * chunk]
                for side in range(2)
                for f in range(FFN_CHUNKS)
            ],
            axis=1,
        )
        for i in range(3)
    ]
    return (
        block_out,
        in_grad,
        gains[0],
        early[:, head_width:],
        late[:, :head_width],
        late[:, head_width:],
        early[:, :head_width],
        gains[1],
        ffn_final[0],
        ffn_final[1],
        ffn_final[2],
    )


def solution(mesh):
    dp, ctx, tp = (mesh.shape[name] for name in ("dp", "ctx", "tp"))
    split_mesh = Mesh(mesh.devices.reshape(dp, ctx // 2, 2, tp), ("dp", "hi", "lo", "tp"))
    every = ("dp",) + CTX
    split = P(every, "tp")
    rows = P(every, None)
    vector = P(every)
    return jax.shard_map(
        body,
        mesh=split_mesh,
        in_specs=(rows, P(), split, split, split, split, P(), split, split, split)
        + (P("dp", None), P("dp", None), rows),
        out_specs=(split, split, vector, split, split, split, split, vector, split, split, split),
        check_vma=False,
    )
```

```python
import functools
import math

import jax
import jax.numpy as jnp
from jax import lax
from jax.experimental import pallas as pl
from jax.experimental.pallas import tpu as pltpu
from jax.sharding import Mesh
from jax.sharding import PartitionSpec as P

HEAD_DIM = 64
CLEN = 256
LANES = 128
EPS = 1e-05
ROPE_BASE = 130000.0
MASKED = -1e30
FFN_CHUNKS = 2
COST_SCALE = 4
BF16 = jnp.bfloat16
F32 = jnp.float32
VMEM_LIMIT = 32 * 1024 * 1024
VMEM_WHOLE = 60 * 1024 * 1024
CTX = ("hi", "lo")


def swap(values, axis, mask=1):
    count = lax.axis_size(axis)
    return lax.ppermute(values, axis, [(i, i ^ mask) for i in range(count)])


def turn(values, axis, shift):
    count = lax.axis_size(axis)
    return lax.ppermute(values, axis, [(i, (i + shift) % count) for i in range(count)])


def add(left, right):
    return left.astype(F32) + right.astype(F32)


def low(values):
    return values.astype(BF16)


def after(values, *needed):
    return lax.optimization_barrier((values,) + needed)[0]


def cost(flops, data, transcendentals=0):
    return pl.CostEstimate(
        flops=flops // COST_SCALE,
        bytes_accessed=data // COST_SCALE,
        transcendentals=transcendentals // COST_SCALE,
    )


def dot(left, right, dims):
    return lax.dot_general(left, right, (dims, ((), ())), preferred_element_type=F32)


NN = ((1,), (0,))
NT = ((1,), (1,))
TN = ((0,), (0,))
VMEM = pl.BlockSpec(memory_space=pltpu.VMEM)
SMEM = pl.BlockSpec(memory_space=pltpu.SMEM)


def at_block(index, size):
    return pl.ds(pl.multiple_of(index * size, size), size)


def half_swap(values):
    lane = lax.broadcasted_iota(jnp.int32, values.shape, 1)
    ahead = pltpu.roll(values, LANES - 32, 1)
    behind = pltpu.roll(values, 32, 1)
    return jnp.where((lane & 63) < 32, ahead, behind)


def call(kernel, operands, out_shape, name, flops, data, scratch=(), smem=(), transcendentals=0):
    many = isinstance(out_shape, list)
    return pl.pallas_call(
        kernel,
        in_specs=[SMEM] * len(smem) + [VMEM] * len(operands),
        out_specs=[VMEM] * len(out_shape) if many else VMEM,
        out_shape=out_shape,
        scratch_shapes=list(scratch),
        compiler_params=pltpu.CompilerParams(vmem_limit_bytes=VMEM_LIMIT),
        cost_estimate=cost(flops, data, transcendentals),
        name=name,
    )(*smem, *operands)


def fill(whole, pieces, place_ref, unit, column, width):
    at = 0
    for piece in pieces:
        for row in range(0, piece.shape[0], unit):
            whole[at_block(place_ref[at], unit), :] = piece[
                row : row + unit, column : column + width
            ]
            at += 1


def project_kernel(parts, column, width, rope_width, bit_ref, place_ref, *refs):
    x_refs = refs[:parts]
    w_refs = refs[parts:-5]
    cos_ref, sin_ref, out_ref, x_all, w_all = refs[-5:]
    fill(w_all, w_refs, place_ref, w_all.shape[0] // place_ref.shape[0], column, width)
    if parts == 2:
        rows = x_refs[0].shape[0]
        x_all[at_block(bit_ref[0], rows), :] = x_refs[0][...]
        x_all[at_block(1 - bit_ref[0], rows), :] = x_refs[1][...]
        x_ref = x_all
    else:
        x_ref = x_refs[0]
    tile = min(width, 256)

    def columns(first, rope):
        def step(t, carry):
            at = pl.multiple_of(first + t * tile, tile)
            total = dot(x_ref[...], w_all[:, pl.ds(at, tile)], NN)
            for c in range(0, tile, LANES):
                part = total[:, c : c + LANES]
                if rope:
                    part = part * cos_ref[...] + half_swap(part) * sin_ref[...]
                out_ref[:, pl.ds(pl.multiple_of(at + c, LANES), LANES)] = part.astype(BF16)
            return carry

        return step

    if rope_width:
        lax.fori_loop(0, rope_width // tile, columns(0, True), 0)
    if rope_width < width:
        lax.fori_loop(0, (width - rope_width) // tile, columns(rope_width, False), 0)


def project(x_parts, stack, places, bit, column, width, cosine, sine, rope_width):
    rows = sum(x.shape[0] for x in x_parts)
    depth = x_parts[0].shape[1]
    return call(
        functools.partial(project_kernel, len(x_parts), column, width, rope_width),
        [*x_parts, *stack, cosine, sine],
        jax.ShapeDtypeStruct((rows, width), BF16),
        "project",
        2 * rows * depth * width,
        2 * (rows * depth + depth * width + rows * width),
        [
            pltpu.VMEM((rows if len(x_parts) == 2 else 16, depth), BF16),
            pltpu.VMEM((depth, width), BF16),
        ],
        [bit, places],
    )


def place_kernel(count, place_ref, *refs):
    out_ref = refs[-1]
    unit = out_ref.shape[0] // count
    at = 0
    for ref in refs[:-1]:
        for row in range(0, ref.shape[0], unit):
            out_ref[at_block(place_ref[at], unit), :] = ref[row : row + unit, :]
            at += 1


def place_rows(pieces, places):
    rows, width = sum(p.shape[0] for p in pieces), pieces[0].shape[1]
    return call(
        functools.partial(place_kernel, places.shape[0]),
        pieces,
        jax.ShapeDtypeStruct((rows, width), BF16),
        "place_rows",
        0,
        4 * rows * width,
        smem=[places],
    )


def ffn_kernel(chunks, *refs):
    x_refs, cot_refs = refs[:2], refs[2:4]
    w_refs = refs[4 : 4 + chunks]
    hidden_ref, dpair_ref = refs[4 + chunks :]
    rows = x_refs[0].shape[0]
    wide = w_refs[0].shape[1] // 3
    tile = min(wide, 256)
    for f, w_ref in enumerate(w_refs):

        def step(t, carry, f=f, w_ref=w_ref):
            for part in range(2):
                x, g = x_refs[part][...], cot_refs[part][...]
                gate = dot(x, w_ref[:, pl.ds(pl.multiple_of(t * tile, tile), tile)], NN)
                upward = dot(x, w_ref[:, pl.ds(pl.multiple_of(wide + t * tile, tile), tile)], NN)
                dhidden = dot(g, w_ref[:, pl.ds(pl.multiple_of(2 * wide + t * tile, tile), tile)], NN)
                sig = 1.0 / (1.0 + jnp.exp(-gate))
                silu = gate * sig
                at = slice(part * rows, (part + 1) * rows)
                hidden_ref[at, pl.ds(pl.multiple_of(f * wide + t * tile, tile), tile)] = (
                    silu * upward
                ).astype(BF16)
                dpair_ref[at, pl.ds(pl.multiple_of(2 * f * wide + t * tile, tile), tile)] = (
                    dhidden * upward * (sig + silu * (1.0 - sig))
                ).astype(BF16)
                dpair_ref[at, pl.ds(pl.multiple_of((2 * f + 1) * wide + t * tile, tile), tile)] = (
                    dhidden * silu
                ).astype(BF16)
            return carry

        lax.fori_loop(0, wide // tile, step, 0)


def ffn(seconds, cotangents, weights):
    rows = 2 * seconds[0].shape[0]
    width = seconds[0].shape[1]
    units = sum(w.shape[1] for w in weights) // 3
    return call(
        functools.partial(ffn_kernel, len(weights)),
        [*seconds, *cotangents, *weights],
        [jax.ShapeDtypeStruct((rows, units), BF16), jax.ShapeDtypeStruct((rows, 2 * units), BF16)],
        "ffn",
        6 * rows * width * units,
        2 * (2 * rows * width + 3 * width * units + 3 * rows * units),
        transcendentals=rows * units,
    )


def back_kernel(spans, *refs):
    count = 1 + max(span[2] for span in spans)
    lefts = refs[: 1 + max(span[0] for span in spans)]
    rights = refs[len(lefts) : len(lefts) + count]
    outs = refs[len(lefts) + count :]
    rows, width = outs[0].shape
    tile = 256

    def step(t, carry):
        for part, out_ref in enumerate(outs):
            total = None
            for left, l_at, right, r_at, wide in spans:
                term = dot(
                    lefts[left][part * rows : (part + 1) * rows, l_at : l_at + wide],
                    rights[right][at_block(t, tile), r_at : r_at + wide],
                    NT,
                )
                total = term if total is None else total + term
            out_ref[:, at_block(t, tile)] = total.astype(BF16)
        return carry

    lax.fori_loop(0, width // tile, step, 0)


def ffn_back(lefts, weights, spans):
    rows = lefts[0].shape[0]
    width = weights[0].shape[0]
    depth = sum(span[4] for span in spans)
    return call(
        functools.partial(back_kernel, spans),
        [*lefts, *weights],
        [jax.ShapeDtypeStruct((rows // 2, width), BF16)] * 2,
        "ffn_back",
        2 * rows * width * depth,
        2 * (rows * depth + width * depth + rows * width),
    )


def project_back_kernel(columns, counts, bit_ref, place_ref, *refs):
    lefts = refs[: len(columns)]
    at, stacks = len(columns), []
    for count in counts:
        stacks.append(refs[at : at + count])
        at += count
    outs, w_all = refs[at : at + 2], refs[at + 2]
    rows, width = outs[0].shape
    unit = width // place_ref.shape[0]
    wide = lefts[0].shape[1]
    for n, (which, column) in enumerate(columns):
        at = 0
        for piece in stacks[which]:
            for row in range(0, piece.shape[0], unit):
                w_all[at_block(place_ref[at], unit), n * wide : (n + 1) * wide] = piece[
                    row : row + unit, column : column + wide
                ]
                at += 1
    tile = 256

    def step(t, carry):
        for part, out_ref in enumerate(outs):
            which = bit_ref[0] if part == 0 else 1 - bit_ref[0]
            total = None
            for n, left in enumerate(lefts):
                term = dot(
                    left[at_block(which, rows), :],
                    w_all[at_block(t, tile), n * wide : (n + 1) * wide],
                    NT,
                )
                total = term if total is None else total + term
            out_ref[:, at_block(t, tile)] = total.astype(BF16)
        return carry

    lax.fori_loop(0, width // tile, step, 0)


def project_back(lefts, columns, stacks, places, bit):
    rows, wide = lefts[0].shape
    width = sum(piece.shape[0] for piece in stacks[0])
    depth = wide * len(lefts)
    return call(
        functools.partial(project_back_kernel, columns, tuple(len(s) for s in stacks)),
        [*lefts, *[piece for stack in stacks for piece in stack]],
        [jax.ShapeDtypeStruct((rows // 2, width), BF16)] * 2,
        "project_back",
        2 * rows * width * depth,
        2 * (rows * depth + width * depth + rows * width),
        [pltpu.VMEM((width, depth), BF16)],
        [bit, places],
    )


def store_blocks(out_ref, values, first, unit, slot_ref, column):
    wide = values.shape[1]
    for row in range(0, values.shape[0], unit):
        slot = slot_ref[(first + row) // unit]
        out_ref[at_block(slot, unit), column : column + wide] = values[row : row + unit]


def ffn_grads_kernel(tile, unit, dp_ref, slot_ref, *refs):
    del dp_ref
    x_refs, cot_refs = refs[:4], refs[4:8]
    hiddens, dpairs, out_ref = refs[8:10], refs[10:12], refs[12]
    rows = x_refs[0].shape[0]
    wide = hiddens[0].shape[1]

    def product(lefts, rights):
        total = None
        for n, left in enumerate(lefts):
            part = slice((n % 2) * rows, (n % 2 + 1) * rows)
            term = dot(left[...], rights[n // 2][part, :], TN)
            total = term if total is None else total + term
        return total.astype(BF16)

    first = pl.program_id(0) * tile
    store_blocks(out_ref, product(x_refs, dpairs), first, unit, slot_ref, 0)
    store_blocks(out_ref, product(cot_refs, hiddens), first, unit, slot_ref, 2 * wide)


def ffn_grads(seconds, cotangents, hiddens, dpairs, owners, slots, s, count, unit):
    half, wide = seconds[0].shape[0], hiddens[0].shape[1]
    rows = 4 * half
    tile = 256
    left = pl.BlockSpec((half, tile), lambda t, dp, slot: (0, dp[s] * (count // tile) + t))
    whole = lambda x: pl.BlockSpec(x.shape, lambda t, dp, slot: (0, 0))
    return pl.pallas_call(
        functools.partial(ffn_grads_kernel, tile, unit),
        grid_spec=pltpu.PrefetchScalarGridSpec(
            num_scalar_prefetch=2,
            grid=(count // tile,),
            in_specs=[left] * 8 + [whole(x) for x in (*hiddens, *dpairs)],
            out_specs=pl.BlockSpec((count, 3 * wide), lambda t, dp, slot: (0, 0)),
        ),
        out_shape=jax.ShapeDtypeStruct((count, 3 * wide), BF16),
        compiler_params=pltpu.CompilerParams(vmem_limit_bytes=VMEM_WHOLE),
        cost_estimate=cost(
            6 * rows * count * wide,
            2 * (2 * rows * count + 3 * rows * wide + 3 * count * wide),
        ),
        name="ffn_grads",
    )(owners, slots, *seconds, *cotangents, *hiddens, *dpairs)


def attn_grads_kernel(kinds, s, unit, bit_ref, dp_ref, slot_ref, *refs):
    at, pairs = 0, []
    for parts in kinds:
        pairs.append((refs[at : at + parts], refs[at + parts]))
        at += parts + 1
    out_ref = refs[at]
    count = out_ref.shape[0]
    tile = 256

    def step(t, carry):
        where = pl.ds(pl.multiple_of(dp_ref[s] * count + t * tile, tile), tile)
        column = 0
        for lefts, right in pairs:
            if len(lefts) == 1:
                total = dot(lefts[0][:, where], right[...], TN)
            else:
                rows = lefts[0].shape[0]
                total = dot(lefts[0][:, where], right[at_block(bit_ref[0], rows), :], TN) + dot(
                    lefts[1][:, where], right[at_block(1 - bit_ref[0], rows), :], TN
                )
            store_blocks(out_ref, total.astype(BF16), t * tile, unit, slot_ref, column)
            column += right.shape[1]
        return carry

    lax.fori_loop(0, count // tile, step, 0)


def attn_grads_block(pairs, bit, owners, slots, s, count, unit):
    kinds = tuple(len(lefts) for lefts, _ in pairs)
    width = sum(right.shape[1] for _, right in pairs)
    rows = pairs[0][1].shape[0]
    return call(
        functools.partial(attn_grads_kernel, kinds, s, unit),
        [x for lefts, right in pairs for x in (*lefts, right)],
        jax.ShapeDtypeStruct((count, width), BF16),
        "attn_grads",
        2 * rows * width * count,
        2 * (rows * count + rows * width + count * width),
        smem=[bit, owners, slots],
    )


SCALE = HEAD_DIM**-0.5
SCALE_LOG2 = SCALE * math.log2(math.e)


def forward_kernel(pieces, order_ref, rank_ref, q_ref, ks_ref, vs_ref, *refs):
    kp_refs, vp_refs = refs[:pieces], refs[pieces : 2 * pieces]
    o_ref, lse_ref = refs[2 * pieces :]
    q = q_ref[...]
    size = q.shape[0]
    prompt = pl.program_id(1) == 0
    low_lane = lax.broadcasted_iota(jnp.int32, q.shape, 1) < HEAD_DIM
    causal = lax.broadcasted_iota(jnp.int32, (size, size), 0) >= lax.broadcasted_iota(
        jnp.int32, (size, size), 1
    )
    outs = []
    for head in range(2):
        own = low_lane if head == 0 else jnp.logical_not(low_lane)
        qh = jnp.where(own, q, jnp.zeros_like(q))
        raw = [jnp.where(causal, dot(qh, ks_ref[...], NT), MASKED)]
        for s in range(pieces):
            hidden = jnp.logical_and(prompt, rank_ref[s] >= rank_ref[0])
            raw.append(dot(qh, kp_refs[s][...], NT) + jnp.where(hidden, MASKED, 0.0))
        top = raw[0]
        for r in raw[1:]:
            top = jnp.maximum(top, r)
        top = jnp.max(top, axis=-1, keepdims=True) * SCALE_LOG2
        sums, acc = None, None
        for s, r in enumerate(raw):
            e = jnp.exp2(r * SCALE_LOG2 - top)
            v = vs_ref if s == 0 else vp_refs[s - 1]
            term = dot(e.astype(BF16), v[...], NN)
            sums = e if sums is None else sums + e
            acc = term if acc is None else acc + term
        total = jnp.sum(sums, axis=-1, keepdims=True)
        outs.append((acc / total, top + jnp.log2(total)))
    o_ref[...] = jnp.where(low_lane, outs[0][0], outs[1][0]).astype(BF16)
    lse_ref[...] = jnp.where(low_lane, outs[0][1], outs[1][1])


def backward_kernel(
    pieces, order_ref, rank_ref, q_ref, ks_ref, vs_ref, o_ref, lse_ref, do_ref, cos_ref, sin_ref, *refs
):
    kp_refs, vp_refs = refs[:pieces], refs[pieces : 2 * pieces]
    dq_ref, dks_ref, dvs_ref = refs[2 * pieces : 2 * pieces + 3]
    piece_refs = refs[2 * pieces + 3 : 3 * pieces + 3]
    acc_ref = refs[-1]
    pair, step = pl.program_id(0), pl.program_id(1)
    prompt = step == 0
    q, do = q_ref[...], do_ref[...]
    size = q.shape[0]
    low_lane = lax.broadcasted_iota(jnp.int32, q.shape, 1) < HEAD_DIM
    causal = lax.broadcasted_iota(jnp.int32, (size, size), 0) >= lax.broadcasted_iota(
        jnp.int32, (size, size), 1
    )
    product = do.astype(F32) * o_ref[...].astype(F32)
    lse = lse_ref[...]
    dq_heads = []
    dk_all = [None] * (pieces + 1)
    dv_all = [None] * (pieces + 1)
    for head in range(2):
        own = low_lane if head == 0 else jnp.logical_not(low_lane)
        qh = jnp.where(own, q, jnp.zeros_like(q))
        doh = jnp.where(own, do, jnp.zeros_like(do))
        delta = jnp.sum(jnp.where(own, product, 0.0), axis=-1, keepdims=True)
        log_sum = lse[:, head * HEAD_DIM : head * HEAD_DIM + 1]
        dq = None
        for s in range(pieces + 1):
            k = (ks_ref if s == 0 else kp_refs[s - 1])[...]
            v = (vs_ref if s == 0 else vp_refs[s - 1])[...]
            raw = dot(qh, k, NT)
            if s == 0:
                raw = jnp.where(causal, raw, MASKED)
            else:
                hidden = jnp.logical_and(prompt, rank_ref[s - 1] >= rank_ref[0])
                raw = raw + jnp.where(hidden, MASKED, 0.0)
            prob = jnp.exp2(raw * SCALE_LOG2 - log_sum)
            ds = (prob * (dot(doh, v, NT) - delta)).astype(BF16)
            term = dot(ds, k, NN)
            dq = term if dq is None else dq + term
            dk = dot(ds, qh, TN)
            dv = dot(prob.astype(BF16), doh, TN)
            dk_all[s] = dk if dk_all[s] is None else dk_all[s] + dk
            dv_all[s] = dv if dv_all[s] is None else dv_all[s] + dv
        dq_heads.append(dq)
    dq = jnp.where(low_lane, dq_heads[0], dq_heads[1]) * SCALE
    cosine, sine = cos_ref[...], sin_ref[...]
    dq_ref[...] = (dq * cosine - half_swap(dq) * sine).astype(BF16)
    dks_ref[...] = dk_all[0] * SCALE
    dvs_ref[...] = dv_all[0]
    for s in range(pieces):
        both = jnp.concatenate([dk_all[s + 1] * SCALE, dv_all[s + 1]], axis=1)
        at = slice(s * size, (s + 1) * size)

        @pl.when(prompt)
        def _(both=both, at=at):
            acc_ref[at, :] = both

        @pl.when(jnp.logical_not(prompt))
        def _(both=both, at=at):
            acc_ref[at, :] += both

    @pl.when(step == pl.num_programs(1) - 1)
    def _():
        wide = piece_refs[0].shape[1] // 2
        k_at = pl.ds(pl.multiple_of(pair * LANES, LANES), LANES)
        v_at = pl.ds(pl.multiple_of(wide + pair * LANES, LANES), LANES)
        for s in range(pieces):
            both = acc_ref[s * size : (s + 1) * size, :]
            piece_refs[s][:, k_at] = both[:, :LANES].astype(piece_refs[s].dtype)
            piece_refs[s][:, v_at] = both[:, LANES:].astype(piece_refs[s].dtype)


def merge_kernel(others, mine_ref, dk_ref, dv_ref, own_ref, *refs):
    got = refs[:others]
    cos_ref, sin_ref, dk_out, dv_out = refs[others:]
    width = dk_ref.shape[1]
    cosine, sine = cos_ref[...], sin_ref[...]

    def write(dk, dv):
        for at in range(0, width, LANES):
            part = dk[:, at : at + LANES]
            dk_out[:, at : at + LANES] = (part * cosine - half_swap(part) * sine).astype(BF16)
        dv_out[...] = dv.astype(BF16)

    mine = pl.program_id(0) == mine_ref[0]

    @pl.when(mine)
    def _():
        extra = own_ref[...]
        for ref in got:
            extra = extra + ref[...].astype(F32)
        write(dk_ref[...] + extra[:, :width], dv_ref[...] + extra[:, width:])

    @pl.when(jnp.logical_not(mine))
    def _():
        write(dk_ref[...], dv_ref[...])


def merge_keys(mine, dkey, dvalue, own, got, cosine, sine):
    rows, width = dkey.shape
    row = lambda i, mine: (i, 0)
    full = lambda i, mine: (0, 0)
    return pl.pallas_call(
        functools.partial(merge_kernel, len(got)),
        grid_spec=pltpu.PrefetchScalarGridSpec(
            num_scalar_prefetch=1,
            grid=(rows // CLEN,),
            in_specs=[pl.BlockSpec((CLEN, width), row)] * 2
            + [pl.BlockSpec((CLEN, 2 * width), full)] * (1 + len(got))
            + [pl.BlockSpec((CLEN, LANES), row)] * 2,
            out_specs=[pl.BlockSpec((CLEN, width), row)] * 2,
        ),
        out_shape=[jax.ShapeDtypeStruct((rows, width), BF16)] * 2,
        compiler_params=pltpu.CompilerParams(vmem_limit_bytes=VMEM_LIMIT),
        cost_estimate=cost(8 * rows * width, 16 * rows * width, 0),
        name="merge_keys",
    )(mine, dkey, dvalue, own, *got, cosine, sine)


def attention_specs(pieces, key_pairs):
    own = pl.BlockSpec((CLEN, LANES), lambda h, j, order, rank: (order[j], h))
    own_value = pl.BlockSpec((CLEN, LANES), lambda h, j, order, rank: (order[j], key_pairs + h))
    key = pl.BlockSpec((CLEN, LANES), lambda h, j, order, rank: (0, h))
    value = pl.BlockSpec((CLEN, LANES), lambda h, j, order, rank: (0, key_pairs + h))
    trig = pl.BlockSpec((CLEN, LANES), lambda h, j, order, rank: (order[j], 0))
    prompt = pl.BlockSpec((CLEN, 2 * key_pairs * LANES), lambda h, j, order, rank: (0, 0))
    return own, own_value, key, value, trig, prompt


def attention_forward(order, rank, query, kv, prompts):
    rows, width = query.shape
    pieces, pairs = len(prompts), width // LANES
    own, own_value, key, value, _, _ = attention_specs(pieces, pairs)
    scores = rows * (pieces + 1) * CLEN * (width // HEAD_DIM)
    return pl.pallas_call(
        functools.partial(forward_kernel, pieces),
        grid_spec=pltpu.PrefetchScalarGridSpec(
            num_scalar_prefetch=2,
            grid=(pairs, rows // CLEN),
            in_specs=[own, own, own_value] + [key] * pieces + [value] * pieces,
            out_specs=[own, own],
        ),
        out_shape=[jax.ShapeDtypeStruct((rows, width), BF16), jax.ShapeDtypeStruct((rows, width), F32)],
        compiler_params=pltpu.CompilerParams(vmem_limit_bytes=VMEM_LIMIT),
        cost_estimate=cost(
            16 * scores * HEAD_DIM, 16 * rows * width, scores
        ),
        name="attend",
    )(order, rank, query, kv, kv, *prompts, *prompts)


def attention_backward(order, rank, query, kv, mixed, lse, dmixed, cosine, sine, prompts):
    rows, width = query.shape
    pieces, pairs = len(prompts), width // LANES
    own, own_value, key, value, trig, prompt = attention_specs(pieces, pairs)
    scores = rows * (pieces + 1) * CLEN * (width // HEAD_DIM)
    return pl.pallas_call(
        functools.partial(backward_kernel, pieces),
        grid_spec=pltpu.PrefetchScalarGridSpec(
            num_scalar_prefetch=2,
            grid=(pairs, rows // CLEN),
            in_specs=[own, own, own_value, own, own, own] + [trig] * 2 + [key] * pieces + [value] * pieces,
            out_specs=[own, own, own] + [prompt] * pieces,
            scratch_shapes=[pltpu.VMEM((pieces * CLEN, 2 * LANES), F32)],
        ),
        out_shape=[
            jax.ShapeDtypeStruct((rows, width), BF16),
            jax.ShapeDtypeStruct((rows, width), F32),
            jax.ShapeDtypeStruct((rows, width), F32),
        ]
        + [jax.ShapeDtypeStruct((CLEN, 2 * width), BF16 if s else F32) for s in range(pieces)],
        compiler_params=pltpu.CompilerParams(vmem_limit_bytes=VMEM_LIMIT),
        cost_estimate=cost(
            40 * scores * HEAD_DIM, 32 * rows * width, scores
        ),
        name="attend_back",
    )(order, rank, query, kv, kv, mixed, lse, dmixed, cosine, sine, *prompts, *prompts)


def normalize(values):
    factor = lax.rsqrt(jnp.mean(values * values, axis=-1, keepdims=True) + EPS)
    return (values * factor, factor)


def rope_tables(where):
    half = HEAD_DIM // 2
    freqs = ROPE_BASE ** (-(jnp.arange(half).astype(F32) * 2.0) / HEAD_DIM)
    angles = where.astype(F32)[:, None] * freqs[None, :]
    cosine, sine = jnp.cos(angles), jnp.sin(angles)
    return (
        jnp.concatenate([cosine] * 4, axis=1),
        jnp.concatenate([-sine, sine, -sine, sine], axis=1),
    )


def body(
    tokens,
    attn_gain,
    query_weight,
    key_weight,
    value_weight,
    out_weight,
    ffn_gain,
    gate_weight,
    up_weight,
    down_weight,
    seq_ids,
    positions,
    out_grad,
):
    rows, width = tokens.shape
    head_width = query_weight.shape[1]
    own_rows, ffn_width = gate_weight.shape
    half_units = ffn_width // 2
    chunk = half_units // FFN_CHUNKS
    half = rows // 2
    dp_count = lax.axis_size("dp")
    ctx_count = lax.axis_size("hi") * 2
    tp_count = lax.axis_size("tp")
    dp_index = lax.axis_index("dp")
    parity = lax.axis_index("lo")
    ctx_index = lax.axis_index("hi") * 2 + parity
    tp_index = lax.axis_index("tp")
    bit = tp_index & 1
    bit_ref = bit.astype(jnp.int32)[None]

    def row_half(values, which=bit):
        return lax.dynamic_slice_in_dim(values, which * half, half)

    def assemble(mine, other):
        first = jnp.where(bit == 0, mine, other)
        last = jnp.where(bit == 0, other, mine)
        return jnp.concatenate([first, last], axis=0)

    slots = jnp.arange(dp_count * ctx_count, dtype=jnp.int32)

    def places_of(order_k):
        slot_k = jnp.array(order_k, jnp.int32)[slots % ctx_count]
        return (
            lax.rem(dp_index + slots // ctx_count, dp_count) * ctx_count + (ctx_index ^ slot_k)
        ).astype(jnp.int32)

    def slots_of(order_k):
        slot_of = jnp.array([order_k.index(k) for k in range(ctx_count)], jnp.int32)
        return slot_of[ctx_index ^ jnp.arange(ctx_count, dtype=jnp.int32)]

    attn_order, ffn_order = (0, 2, 1, 3), (0, 1, 2, 3)
    places, places_ffn = places_of(attn_order), places_of(ffn_order)
    slots_attn, slots_ffn = slots_of(attn_order), slots_of(ffn_order)
    owners = lax.rem(dp_index + jnp.arange(dp_count, dtype=jnp.int32), dp_count).astype(jnp.int32)
    near_rows = width // dp_count

    def over_dp(blocks):
        return blocks + [turn(x, "dp", -s) for s in range(1, dp_count) for x in blocks]

    kv_weight = jnp.concatenate([key_weight, value_weight], axis=1)
    kv_one, kv_two = swap(kv_weight, "lo"), swap(kv_weight, "hi")
    kv_three = swap(kv_two, "lo")
    kv_stack = over_dp([kv_weight, kv_two, kv_one, kv_three])
    qo_weight = after(jnp.concatenate([query_weight, out_weight], axis=1), kv_three)
    qo_two = swap(qo_weight, "hi")
    qo_even = jnp.concatenate([qo_weight, qo_two], axis=0)
    qo_odd = swap(qo_even, "lo")
    qo_stack = over_dp([qo_even, qo_odd])

    def ffn_columns(f, which):
        first = which * half_units + f * chunk
        return jnp.concatenate(
            [
                lax.dynamic_slice_in_dim(w, first, chunk, 1)
                for w in (gate_weight, up_weight, down_weight)
            ],
            axis=1,
        )

    def ffn_sends(f, *needed):
        keep, give = after((ffn_columns(f, parity), ffn_columns(f, 1 - parity)), *needed)
        near = jnp.concatenate([keep, swap(give, "lo")], axis=0)
        return near, swap(keep, "hi"), give

    def ffn_stack(near_blocks, far_blocks):
        return place_rows([x for both in zip(near_blocks, far_blocks) for x in both], places_ffn)

    def gather_dp(own):
        return [own] + [turn(own, "dp", -s) for s in range(1, dp_count)]

    group_seq = seq_ids[0].reshape(ctx_count, rows // CLEN, CLEN)[:, :, 0]
    group_pos = positions[0].reshape(ctx_count, rows // CLEN, CLEN)[:, :, 0]
    prompt_at = jnp.argmax(group_seq == 0, axis=1).astype(jnp.int32)
    prompt_rank = jnp.sum(jnp.where(group_seq == 0, group_pos, 0), axis=1).astype(jnp.int32)
    rank = prompt_rank[ctx_index ^ jnp.arange(ctx_count, dtype=jnp.int32)]
    mine = prompt_at[ctx_index]
    pieces = jnp.arange(rows // CLEN, dtype=jnp.int32)
    order = jnp.where(pieces == 0, mine, jnp.where(pieces <= mine, pieces - 1, pieces))
    own_pos = lax.dynamic_slice_in_dim(positions[0], ctx_index * rows, rows)
    cosine, sine = rope_tables(own_pos)

    gain_one = attn_gain[None].astype(F32)
    gain_two = ffn_gain[None].astype(F32)
    first_norm, first_scale = normalize(tokens.astype(F32))
    first = low(first_norm * gain_one)

    kv = project(
        [after(first, qo_two)], kv_stack, places, bit_ref, 0, 2 * head_width, cosine, sine, head_width
    )
    prompt_own = lax.dynamic_slice_in_dim(kv, mine * CLEN, CLEN)
    prompts = [prompt_own] + [swap(prompt_own, CTX, k) for k in range(1, ctx_count)]
    near_one, two_one, give_one = ffn_sends(0, kv_three)
    query = project(
        [after(first, two_one, near_one)],
        qo_stack,
        places,
        bit_ref,
        0,
        head_width,
        cosine,
        sine,
        head_width,
    )
    near_one = gather_dp(near_one)
    cotangent_half = row_half(out_grad)
    cotangent_far = swap(after(cotangent_half, *prompts[1:]), "lo")
    three_one = swap(after(give_one, kv_stack[-1]), CTX, 3)
    query = after(query, *near_one[1:], three_one)
    mixed, lse = attention_forward(order, rank, query, kv, prompts)
    near_two, two_two, give_two = ffn_sends(1, *prompts[1:])
    near_two = gather_dp(after(near_two, two_one, *qo_stack[2:]))
    mixed = after(mixed, two_two, *near_two[1:])
    three_two = swap(after(give_two, three_one), CTX, 3)
    far_one_blocks = gather_dp(jnp.concatenate([two_one, three_one], axis=0))
    far_two_blocks = gather_dp(jnp.concatenate([two_two, three_two], axis=0))
    ffn_weights = [ffn_stack(near_one, far_one_blocks), ffn_stack(near_two, far_two_blocks)]

    kept, given = project_back(
        [mixed], ((0, head_width),), [qo_stack], places, bit_ref
    )
    mixed_out = low(add(kept, after(swap(given, "tp"), three_two)))
    mixed_far = after(
        swap(mixed_out, "tp", 2), ffn_weights[0], cotangent_far
    )
    middle = row_half(tokens).astype(F32) + add(mixed_out, mixed_far)
    second_norm, second_scale = normalize(middle)
    second_half = low(second_norm * gain_two)

    cotangents = [
        [cotangent_half, row_half(out_grad, 1 - bit)],
        [cotangent_far, swap(cotangent_far, "tp")],
    ]
    second_far = swap(second_half, "lo")
    near = [second_half, after(swap(second_half, "tp"), *far_two_blocks[1:])]
    made = [[ffn(near, cotangents[0], [w]) for w in ffn_weights]]
    gate_spans = tuple((f, 0, f, 0, 2 * chunk) for f in range(FFN_CHUNKS))
    down_spans = tuple((f, 0, f, 2 * chunk, chunk) for f in range(FFN_CHUNKS))
    dsecond_near = ffn_back([m[1] for m in made[0]], ffn_weights, gate_spans)
    second_far = after(second_far, *dsecond_near)
    far = [second_far, swap(second_far, "tp")]
    made.append([ffn(far, cotangents[1], [w]) for w in ffn_weights])
    seconds = [near, far]
    hiddens = [[m[0] for m in side] for side in made]
    dpairs = [[m[1] for m in side] for side in made]

    def cores(part):
        return low(add(part[0], swap(part[1], "tp")))

    dsecond_far = ffn_back(dpairs[1], ffn_weights, gate_spans)
    dsecond_got, dsecond_half = swap(cores(dsecond_far), "lo"), cores(dsecond_near)

    lefts, left_cots = after(
        (seconds[0] + seconds[1], cotangents[0] + cotangents[1]), *dsecond_near, *dsecond_far
    )
    ffn_given, ffn_own = [], []
    for f in range(FFN_CHUNKS):

        def part(s, f=f):
            return ffn_grads(
                lefts,
                left_cots,
                [side[f] for side in hiddens],
                [side[f] for side in dpairs],
                owners,
                slots_ffn,
                s,
                near_rows,
                own_rows,
            )

        ffn_given.append([part(s) for s in range(1, dp_count)])
        ffn_own.append(part(0))
    pair_rows = 2 * own_rows

    def over_dp_rows(f, first, *needed):
        return [
            turn(after(x[first : first + pair_rows], *needed), "dp", s + 1)
            for s, x in enumerate(ffn_given[f])
        ]

    def total_rows(f, first, got):
        total = ffn_own[f][first : first + pair_rows]
        for x in got:
            total = add(total, x)
        return low(total)

    far_one = over_dp_rows(0, pair_rows)
    near_one_got = over_dp_rows(0, 0, *far_one)
    far_two = over_dp_rows(1, pair_rows, *near_one_got)
    near_two_got = over_dp_rows(1, 0, *near_one_got)
    dsecond_got = after(dsecond_got, *ffn_given[1], ffn_own[0], *far_one)
    dsecond = low(add(dsecond_half, dsecond_got))
    hi_one = swap(total_rows(0, pair_rows, far_one), "hi")
    hiddens_late = after(hiddens, dsecond)
    out_far = ffn_back(hiddens_late[1], ffn_weights, down_spans)
    out_near = ffn_back(hiddens_late[0], ffn_weights, down_spans)

    def ffn_deliver(near, hi_got, needed):
        pair = add(near, hi_got)
        kept = pair[:own_rows]
        got = after(swap(low(pair[own_rows:]), "lo"), needed).astype(F32)
        return (jnp.where(parity == 0, kept, got), jnp.where(parity == 0, got, kept))

    dsecond = add(dsecond, after(
        swap(dsecond, "tp", 2), *ffn_own, *out_far, *out_near, *near_one_got
    ))
    gain_two_grad = jnp.sum(dsecond * second_norm, axis=0)
    scaled_two = dsecond * gain_two
    dmiddle = cotangent_half.astype(F32) + second_scale * (
        scaled_two - second_norm * jnp.mean(scaled_two * second_norm, axis=-1, keepdims=True)
    )
    out_half, out_far_got = cores(out_near), swap(cores(out_far), "lo")
    dmiddle_low = [low(dmiddle), after(swap(low(dmiddle), "tp"), out_half)]
    dmixed = project(dmiddle_low, qo_stack, places, bit_ref, head_width, head_width, cosine, sine, 0)
    dquery_low, dkey_own, dvalue_own, dprompt_own, *dprompts = attention_backward(
        order, rank, query, kv, mixed, lse, dmixed, cosine, sine, prompts
    )
    got = [swap(piece, CTX, k + 1) for k, piece in enumerate(dprompts)]
    far_two = after(far_two, dquery_low)
    hi_two = swap(total_rows(1, pair_rows, far_two), "hi")
    dkey_low, dvalue_low = merge_keys(
        mine[None], dkey_own, dvalue_own, dprompt_own, got, cosine, sine
    )

    def attn_grads(pairs):
        parts = [
            attn_grads_block(pairs, bit_ref, owners, slots_attn, s, near_rows, own_rows)
            for s in range(dp_count)
        ]
        total = parts[0]
        for s in range(1, dp_count):
            total = add(total, turn(parts[s], "dp", s))
        total = low(total)
        pair = add(total[: 2 * own_rows], swap(total[2 * own_rows :], "lo"))
        return total, pair[:own_rows] + swap(low(pair[own_rows:]), "hi").astype(F32)

    _, early = attn_grads([(dmiddle_low, mixed), ([first], dquery_low)])
    late_total, late = attn_grads([([first], dkey_low), ([first], dvalue_low)])
    ffn_sums = [
        ffn_deliver(total_rows(0, 0, near_one_got), after(hi_one, dquery_low), dkey_low),
        ffn_deliver(
            total_rows(1, 0, after(near_two_got, dquery_low)),
            after(hi_two, late_total),
            late_total,
        ),
    ]

    kept, given = project_back(
        [dquery_low, dkey_low, dvalue_low],
        ((0, 0), (1, 0), (1, head_width)),
        [qo_stack, kv_stack],
        places,
        bit_ref,
    )
    norm_half, norm_other = row_half(first_norm), row_half(first_norm, 1 - bit)
    gain_one_grad = jnp.sum(kept.astype(F32) * norm_half, axis=0) + jnp.sum(
        given.astype(F32) * norm_other, axis=0
    )
    dfirst = after(low(add(kept, swap(given, "tp"))), gain_one_grad)
    dfirst = add(dfirst, swap(dfirst, "tp", 2))
    scaled_one = dfirst * gain_one
    dinputs = dmiddle + row_half(first_scale) * (
        scaled_one - norm_half * jnp.mean(scaled_one * norm_half, axis=-1, keepdims=True)
    )

    share = width // tp_count
    here = tp_index // 2
    gains = jnp.stack([gain_one_grad, jnp.where(here == 0, gain_two_grad, 0.0)])
    for axis in ("tp", "lo", "hi", "dp"):
        mask = 1
        while mask < lax.axis_size(axis):
            gains = gains + swap(gains, axis, mask)
            mask *= 2

    def wide_part(values, which):
        return lax.dynamic_slice_in_dim(values, which * 2 * share, 2 * share, 1)

    def deliver(wide):
        kept = lax.dynamic_slice_in_dim(wide, bit * share, share, 1)
        given = lax.dynamic_slice_in_dim(wide, (1 - bit) * share, share, 1)
        return assemble(kept, swap(given, "tp"))

    in_grad = deliver(after(low(wide_part(dinputs, here)), gains))

    ffn_out = low(add(out_half, after(out_far_got, dquery_low)))
    ffn_out = add(wide_part(ffn_out, here), swap(wide_part(ffn_out, 1 - here), "tp", 2))
    block_out = deliver(low(wide_part(middle, here) + ffn_out))

    part = width // (dp_count * ctx_count)
    gains = lax.dynamic_slice_in_dim(gains, (dp_index * ctx_count + ctx_index) * part, part, 1)

    ffn_final = [
        jnp.concatenate(
            [
                ffn_sums[f][side][:, i * chunk : (i + 1) * chunk]
                for side in range(2)
                for f in range(FFN_CHUNKS)
            ],
            axis=1,
        )
        for i in range(3)
    ]
    return (
        block_out,
        in_grad,
        gains[0],
        early[:, head_width:],
        late[:, :head_width],
        late[:, head_width:],
        early[:, :head_width],
        gains[1],
        ffn_final[0],
        ffn_final[1],
        ffn_final[2],
    )


def solution(mesh):
    dp, ctx, tp = (mesh.shape[name] for name in ("dp", "ctx", "tp"))
    split_mesh = Mesh(mesh.devices.reshape(dp, ctx // 2, 2, tp), ("dp", "hi", "lo", "tp"))
    every = ("dp",) + CTX
    split = P(every, "tp")
    rows = P(every, None)
    vector = P(every)
    return jax.shard_map(
        body,
        mesh=split_mesh,
        in_specs=(rows, P(), split, split, split, split, P(), split, split, split)
        + (P("dp", None), P("dp", None), rows),
        out_specs=(split, split, vector, split, split, split, split, vector, split, split, split),
        check_vma=False,
    )
```

```python
import functools
import math

import jax
import jax.numpy as jnp
from jax import lax
from jax.experimental import pallas as pl
from jax.experimental.pallas import tpu as pltpu
from jax.sharding import Mesh
from jax.sharding import PartitionSpec as P

HEAD_DIM = 64
CLEN = 256
LANES = 128
EPS = 1e-05
ROPE_BASE = 130000.0
MASKED = -1e30
FFN_CHUNKS = 2
COST_SCALE = 4
BF16 = jnp.bfloat16
F32 = jnp.float32
VMEM_LIMIT = 32 * 1024 * 1024
VMEM_WHOLE = 60 * 1024 * 1024
CTX = ("hi", "lo")


def swap(values, axis, mask=1):
    count = lax.axis_size(axis)
    return lax.ppermute(values, axis, [(i, i ^ mask) for i in range(count)])


def turn(values, axis, shift):
    count = lax.axis_size(axis)
    return lax.ppermute(values, axis, [(i, (i + shift) % count) for i in range(count)])


def add(left, right):
    return left.astype(F32) + right.astype(F32)


def low(values):
    return values.astype(BF16)


def after(values, *needed):
    return lax.optimization_barrier((values,) + needed)[0]


def cost(flops, data, transcendentals=0):
    return pl.CostEstimate(
        flops=flops // COST_SCALE,
        bytes_accessed=data // COST_SCALE,
        transcendentals=transcendentals // COST_SCALE,
    )


def dot(left, right, dims):
    return lax.dot_general(left, right, (dims, ((), ())), preferred_element_type=F32)


NN = ((1,), (0,))
NT = ((1,), (1,))
TN = ((0,), (0,))
VMEM = pl.BlockSpec(memory_space=pltpu.VMEM)
SMEM = pl.BlockSpec(memory_space=pltpu.SMEM)


def at_block(index, size):
    return pl.ds(pl.multiple_of(index * size, size), size)


def half_swap(values):
    lane = lax.broadcasted_iota(jnp.int32, values.shape, 1)
    ahead = pltpu.roll(values, LANES - 32, 1)
    behind = pltpu.roll(values, 32, 1)
    return jnp.where((lane & 63) < 32, ahead, behind)


def call(kernel, operands, out_shape, name, flops, data, scratch=(), smem=(), transcendentals=0):
    many = isinstance(out_shape, list)
    return pl.pallas_call(
        kernel,
        in_specs=[SMEM] * len(smem) + [VMEM] * len(operands),
        out_specs=[VMEM] * len(out_shape) if many else VMEM,
        out_shape=out_shape,
        scratch_shapes=list(scratch),
        compiler_params=pltpu.CompilerParams(vmem_limit_bytes=VMEM_LIMIT),
        cost_estimate=cost(flops, data, transcendentals),
        name=name,
    )(*smem, *operands)


def fill(whole, pieces, place_ref, unit, column, width):
    at = 0
    for piece in pieces:
        for row in range(0, piece.shape[0], unit):
            whole[at_block(place_ref[at], unit), :] = piece[
                row : row + unit, column : column + width
            ]
            at += 1


def project_kernel(parts, column, width, rope_width, bit_ref, place_ref, *refs):
    x_refs = refs[:parts]
    w_refs = refs[parts:-5]
    cos_ref, sin_ref, out_ref, x_all, w_all = refs[-5:]
    fill(w_all, w_refs, place_ref, w_all.shape[0] // place_ref.shape[0], column, width)
    if parts == 2:
        rows = x_refs[0].shape[0]
        x_all[at_block(bit_ref[0], rows), :] = x_refs[0][...]
        x_all[at_block(1 - bit_ref[0], rows), :] = x_refs[1][...]
        x_ref = x_all
    else:
        x_ref = x_refs[0]
    tile = min(width, 256)

    def columns(first, rope):
        def step(t, carry):
            at = pl.multiple_of(first + t * tile, tile)
            total = dot(x_ref[...], w_all[:, pl.ds(at, tile)], NN)
            for c in range(0, tile, LANES):
                part = total[:, c : c + LANES]
                if rope:
                    part = part * cos_ref[...] + half_swap(part) * sin_ref[...]
                out_ref[:, pl.ds(pl.multiple_of(at + c, LANES), LANES)] = part.astype(BF16)
            return carry

        return step

    if rope_width:
        lax.fori_loop(0, rope_width // tile, columns(0, True), 0)
    if rope_width < width:
        lax.fori_loop(0, (width - rope_width) // tile, columns(rope_width, False), 0)


def project(x_parts, stack, places, bit, column, width, cosine, sine, rope_width):
    rows = sum(x.shape[0] for x in x_parts)
    depth = x_parts[0].shape[1]
    return call(
        functools.partial(project_kernel, len(x_parts), column, width, rope_width),
        [*x_parts, *stack, cosine, sine],
        jax.ShapeDtypeStruct((rows, width), BF16),
        "project",
        2 * rows * depth * width,
        2 * (rows * depth + depth * width + rows * width),
        [
            pltpu.VMEM((rows if len(x_parts) == 2 else 16, depth), BF16),
            pltpu.VMEM((depth, width), BF16),
        ],
        [bit, places],
    )


def place_kernel(count, place_ref, *refs):
    out_ref = refs[-1]
    unit = out_ref.shape[0] // count
    at = 0
    for ref in refs[:-1]:
        for row in range(0, ref.shape[0], unit):
            out_ref[at_block(place_ref[at], unit), :] = ref[row : row + unit, :]
            at += 1


def place_rows(pieces, places):
    rows, width = sum(p.shape[0] for p in pieces), pieces[0].shape[1]
    return call(
        functools.partial(place_kernel, places.shape[0]),
        pieces,
        jax.ShapeDtypeStruct((rows, width), BF16),
        "place_rows",
        0,
        4 * rows * width,
        smem=[places],
    )


def ffn_kernel(chunks, *refs):
    x_refs, cot_refs = refs[:2], refs[2:4]
    w_refs = refs[4 : 4 + chunks]
    hidden_ref, dpair_ref = refs[4 + chunks :]
    rows = x_refs[0].shape[0]
    wide = w_refs[0].shape[1] // 3
    tile = min(wide, 256)
    for f, w_ref in enumerate(w_refs):

        def step(t, carry, f=f, w_ref=w_ref):
            for part in range(2):
                x, g = x_refs[part][...], cot_refs[part][...]
                gate = dot(x, w_ref[:, pl.ds(pl.multiple_of(t * tile, tile), tile)], NN)
                upward = dot(x, w_ref[:, pl.ds(pl.multiple_of(wide + t * tile, tile), tile)], NN)
                dhidden = dot(g, w_ref[:, pl.ds(pl.multiple_of(2 * wide + t * tile, tile), tile)], NN)
                sig = 1.0 / (1.0 + jnp.exp(-gate))
                silu = gate * sig
                at = slice(part * rows, (part + 1) * rows)
                hidden_ref[at, pl.ds(pl.multiple_of(f * wide + t * tile, tile), tile)] = (
                    silu * upward
                ).astype(BF16)
                dpair_ref[at, pl.ds(pl.multiple_of(2 * f * wide + t * tile, tile), tile)] = (
                    dhidden * upward * (sig + silu * (1.0 - sig))
                ).astype(BF16)
                dpair_ref[at, pl.ds(pl.multiple_of((2 * f + 1) * wide + t * tile, tile), tile)] = (
                    dhidden * silu
                ).astype(BF16)
            return carry

        lax.fori_loop(0, wide // tile, step, 0)


def ffn(seconds, cotangents, weights):
    rows = 2 * seconds[0].shape[0]
    width = seconds[0].shape[1]
    units = sum(w.shape[1] for w in weights) // 3
    return call(
        functools.partial(ffn_kernel, len(weights)),
        [*seconds, *cotangents, *weights],
        [jax.ShapeDtypeStruct((rows, units), BF16), jax.ShapeDtypeStruct((rows, 2 * units), BF16)],
        "ffn",
        6 * rows * width * units,
        2 * (2 * rows * width + 3 * width * units + 3 * rows * units),
        transcendentals=rows * units,
    )


def back_kernel(spans, *refs):
    count = 1 + max(span[2] for span in spans)
    lefts = refs[: 1 + max(span[0] for span in spans)]
    rights = refs[len(lefts) : len(lefts) + count]
    outs = refs[len(lefts) + count :]
    rows, width = outs[0].shape
    tile = 256

    def step(t, carry):
        for part, out_ref in enumerate(outs):
            total = None
            for left, l_at, right, r_at, wide in spans:
                term = dot(
                    lefts[left][part * rows : (part + 1) * rows, l_at : l_at + wide],
                    rights[right][at_block(t, tile), r_at : r_at + wide],
                    NT,
                )
                total = term if total is None else total + term
            out_ref[:, at_block(t, tile)] = total.astype(BF16)
        return carry

    lax.fori_loop(0, width // tile, step, 0)


def ffn_back(lefts, weights, spans):
    rows = lefts[0].shape[0]
    width = weights[0].shape[0]
    depth = sum(span[4] for span in spans)
    return call(
        functools.partial(back_kernel, spans),
        [*lefts, *weights],
        [jax.ShapeDtypeStruct((rows // 2, width), BF16)] * 2,
        "ffn_back",
        2 * rows * width * depth,
        2 * (rows * depth + width * depth + rows * width),
    )


def project_back_kernel(columns, counts, bit_ref, place_ref, *refs):
    lefts = refs[: len(columns)]
    at, stacks = len(columns), []
    for count in counts:
        stacks.append(refs[at : at + count])
        at += count
    outs, w_all = refs[at : at + 2], refs[at + 2]
    rows, width = outs[0].shape
    unit = width // place_ref.shape[0]
    wide = lefts[0].shape[1]
    for n, (which, column) in enumerate(columns):
        at = 0
        for piece in stacks[which]:
            for row in range(0, piece.shape[0], unit):
                w_all[at_block(place_ref[at], unit), n * wide : (n + 1) * wide] = piece[
                    row : row + unit, column : column + wide
                ]
                at += 1
    tile = 256

    def step(t, carry):
        for part, out_ref in enumerate(outs):
            which = bit_ref[0] if part == 0 else 1 - bit_ref[0]
            total = None
            for n, left in enumerate(lefts):
                term = dot(
                    left[at_block(which, rows), :],
                    w_all[at_block(t, tile), n * wide : (n + 1) * wide],
                    NT,
                )
                total = term if total is None else total + term
            out_ref[:, at_block(t, tile)] = total.astype(BF16)
        return carry

    lax.fori_loop(0, width // tile, step, 0)


def project_back(lefts, columns, stacks, places, bit):
    rows, wide = lefts[0].shape
    width = sum(piece.shape[0] for piece in stacks[0])
    depth = wide * len(lefts)
    return call(
        functools.partial(project_back_kernel, columns, tuple(len(s) for s in stacks)),
        [*lefts, *[piece for stack in stacks for piece in stack]],
        [jax.ShapeDtypeStruct((rows // 2, width), BF16)] * 2,
        "project_back",
        2 * rows * width * depth,
        2 * (rows * depth + width * depth + rows * width),
        [pltpu.VMEM((width, depth), BF16)],
        [bit, places],
    )


def store_blocks(out_ref, values, first, unit, slot_ref, column):
    wide = values.shape[1]
    for row in range(0, values.shape[0], unit):
        slot = slot_ref[(first + row) // unit]
        out_ref[at_block(slot, unit), column : column + wide] = values[row : row + unit]


def ffn_grads_kernel(tile, unit, dp_ref, slot_ref, *refs):
    del dp_ref
    x_refs, cot_refs = refs[:4], refs[4:8]
    hiddens, dpairs, out_ref = refs[8:10], refs[10:12], refs[12]
    rows = x_refs[0].shape[0]
    wide = hiddens[0].shape[1]

    def product(lefts, rights):
        total = None
        for n, left in enumerate(lefts):
            part = slice((n % 2) * rows, (n % 2 + 1) * rows)
            term = dot(left[...], rights[n // 2][part, :], TN)
            total = term if total is None else total + term
        return total.astype(BF16)

    first = pl.program_id(0) * tile
    store_blocks(out_ref, product(x_refs, dpairs), first, unit, slot_ref, 0)
    store_blocks(out_ref, product(cot_refs, hiddens), first, unit, slot_ref, 2 * wide)


def ffn_grads(seconds, cotangents, hiddens, dpairs, owners, slots, s, count, unit):
    half, wide = seconds[0].shape[0], hiddens[0].shape[1]
    rows = 4 * half
    tile = 256
    left = pl.BlockSpec((half, tile), lambda t, dp, slot: (0, dp[s] * (count // tile) + t))
    whole = lambda x: pl.BlockSpec(x.shape, lambda t, dp, slot: (0, 0))
    return pl.pallas_call(
        functools.partial(ffn_grads_kernel, tile, unit),
        grid_spec=pltpu.PrefetchScalarGridSpec(
            num_scalar_prefetch=2,
            grid=(count // tile,),
            in_specs=[left] * 8 + [whole(x) for x in (*hiddens, *dpairs)],
            out_specs=pl.BlockSpec((count, 3 * wide), lambda t, dp, slot: (0, 0)),
        ),
        out_shape=jax.ShapeDtypeStruct((count, 3 * wide), BF16),
        compiler_params=pltpu.CompilerParams(vmem_limit_bytes=VMEM_WHOLE),
        cost_estimate=cost(
            6 * rows * count * wide,
            2 * (2 * rows * count + 3 * rows * wide + 3 * count * wide),
        ),
        name="ffn_grads",
    )(owners, slots, *seconds, *cotangents, *hiddens, *dpairs)


def attn_grads_kernel(kinds, s, unit, bit_ref, dp_ref, slot_ref, *refs):
    at, pairs = 0, []
    for parts in kinds:
        pairs.append((refs[at : at + parts], refs[at + parts]))
        at += parts + 1
    out_ref = refs[at]
    count = out_ref.shape[0]
    tile = 256

    def step(t, carry):
        where = pl.ds(pl.multiple_of(dp_ref[s] * count + t * tile, tile), tile)
        column = 0
        for lefts, right in pairs:
            if len(lefts) == 1:
                total = dot(lefts[0][:, where], right[...], TN)
            else:
                rows = lefts[0].shape[0]
                total = dot(lefts[0][:, where], right[at_block(bit_ref[0], rows), :], TN) + dot(
                    lefts[1][:, where], right[at_block(1 - bit_ref[0], rows), :], TN
                )
            store_blocks(out_ref, total.astype(BF16), t * tile, unit, slot_ref, column)
            column += right.shape[1]
        return carry

    lax.fori_loop(0, count // tile, step, 0)


def attn_grads_block(pairs, bit, owners, slots, s, count, unit):
    kinds = tuple(len(lefts) for lefts, _ in pairs)
    width = sum(right.shape[1] for _, right in pairs)
    rows = pairs[0][1].shape[0]
    return call(
        functools.partial(attn_grads_kernel, kinds, s, unit),
        [x for lefts, right in pairs for x in (*lefts, right)],
        jax.ShapeDtypeStruct((count, width), BF16),
        "attn_grads",
        2 * rows * width * count,
        2 * (rows * count + rows * width + count * width),
        smem=[bit, owners, slots],
    )


SCALE = HEAD_DIM**-0.5
SCALE_LOG2 = SCALE * math.log2(math.e)


def forward_kernel(pieces, order_ref, rank_ref, q_ref, ks_ref, vs_ref, *refs):
    kp_refs, vp_refs = refs[:pieces], refs[pieces : 2 * pieces]
    o_ref, lse_ref = refs[2 * pieces :]
    q = q_ref[...]
    size = q.shape[0]
    prompt = pl.program_id(1) == 0
    low_lane = lax.broadcasted_iota(jnp.int32, q.shape, 1) < HEAD_DIM
    causal = lax.broadcasted_iota(jnp.int32, (size, size), 0) >= lax.broadcasted_iota(
        jnp.int32, (size, size), 1
    )
    outs = []
    for head in range(2):
        own = low_lane if head == 0 else jnp.logical_not(low_lane)
        qh = jnp.where(own, q, jnp.zeros_like(q))
        raw = [jnp.where(causal, dot(qh, ks_ref[...], NT), MASKED)]
        for s in range(pieces):
            hidden = jnp.logical_and(prompt, rank_ref[s] >= rank_ref[0])
            raw.append(dot(qh, kp_refs[s][...], NT) + jnp.where(hidden, MASKED, 0.0))
        top = raw[0]
        for r in raw[1:]:
            top = jnp.maximum(top, r)
        top = jnp.max(top, axis=-1, keepdims=True) * SCALE_LOG2
        sums, acc = None, None
        for s, r in enumerate(raw):
            e = jnp.exp2(r * SCALE_LOG2 - top)
            v = vs_ref if s == 0 else vp_refs[s - 1]
            term = dot(e.astype(BF16), v[...], NN)
            sums = e if sums is None else sums + e
            acc = term if acc is None else acc + term
        total = jnp.sum(sums, axis=-1, keepdims=True)
        outs.append((acc / total, top + jnp.log2(total)))
    o_ref[...] = jnp.where(low_lane, outs[0][0], outs[1][0]).astype(BF16)
    lse_ref[...] = jnp.where(low_lane, outs[0][1], outs[1][1])


def backward_kernel(
    pieces, order_ref, rank_ref, q_ref, ks_ref, vs_ref, o_ref, lse_ref, do_ref, cos_ref, sin_ref, *refs
):
    kp_refs, vp_refs = refs[:pieces], refs[pieces : 2 * pieces]
    dq_ref, dks_ref, dvs_ref = refs[2 * pieces : 2 * pieces + 3]
    piece_refs = refs[2 * pieces + 3 : 3 * pieces + 3]
    acc_ref = refs[-1]
    pair, step = pl.program_id(0), pl.program_id(1)
    prompt = step == 0
    q, do = q_ref[...], do_ref[...]
    size = q.shape[0]
    low_lane = lax.broadcasted_iota(jnp.int32, q.shape, 1) < HEAD_DIM
    causal = lax.broadcasted_iota(jnp.int32, (size, size), 0) <= lax.broadcasted_iota(
        jnp.int32, (size, size), 1
    )
    product = (do.astype(F32) * o_ref[...].astype(F32)).T
    lse = lse_ref[...].T
    dq_heads = [None, None]
    dk_all = [None] * (pieces + 1)
    dv_all = [None] * (pieces + 1)
    heads = []
    for head in range(2):
        own = low_lane if head == 0 else jnp.logical_not(low_lane)
        at = slice(head * HEAD_DIM, (head + 1) * HEAD_DIM)
        heads.append(
            (
                jnp.where(own, q, jnp.zeros_like(q)),
                jnp.where(own, do, jnp.zeros_like(do)),
                jnp.sum(product[at], axis=0, keepdims=True),
                lse[head * HEAD_DIM : head * HEAD_DIM + 1],
            )
        )
    for s in range(pieces + 1):
        k = (ks_ref if s == 0 else kp_refs[s - 1])[...]
        v = (vs_ref if s == 0 else vp_refs[s - 1])[...]
        k_turned = k.T
        for head, (qh, doh, delta, log_sum) in enumerate(heads):
            raw = dot(k, qh, NT)
            if s == 0:
                raw = jnp.where(causal, raw, MASKED)
            else:
                hidden = jnp.logical_and(prompt, rank_ref[s - 1] >= rank_ref[0])
                raw = raw + jnp.where(hidden, MASKED, 0.0)
            prob = jnp.exp2(raw * SCALE_LOG2 - log_sum)
            ds = (prob * (dot(v, doh, NT) - delta)).astype(BF16)
            term = dot(k_turned[head * HEAD_DIM : (head + 1) * HEAD_DIM], ds, NN)
            dq_heads[head] = term if dq_heads[head] is None else dq_heads[head] + term
            dk = dot(ds, qh, NN)
            dv = dot(prob.astype(BF16), doh, NN)
            dk_all[s] = dk if dk_all[s] is None else dk_all[s] + dk
            dv_all[s] = dv if dv_all[s] is None else dv_all[s] + dv
    dq = jnp.concatenate(dq_heads, axis=0).T * SCALE
    cosine, sine = cos_ref[...], sin_ref[...]
    dq_ref[...] = (dq * cosine - half_swap(dq) * sine).astype(BF16)
    dks_ref[...] = dk_all[0] * SCALE
    dvs_ref[...] = dv_all[0]
    for s in range(pieces):
        both = jnp.concatenate([dk_all[s + 1] * SCALE, dv_all[s + 1]], axis=1)
        at = slice(s * size, (s + 1) * size)

        @pl.when(prompt)
        def _(both=both, at=at):
            acc_ref[at, :] = both

        @pl.when(jnp.logical_not(prompt))
        def _(both=both, at=at):
            acc_ref[at, :] += both

    @pl.when(step == pl.num_programs(1) - 1)
    def _():
        wide = piece_refs[0].shape[1] // 2
        k_at = pl.ds(pl.multiple_of(pair * LANES, LANES), LANES)
        v_at = pl.ds(pl.multiple_of(wide + pair * LANES, LANES), LANES)
        for s in range(pieces):
            both = acc_ref[s * size : (s + 1) * size, :]
            piece_refs[s][:, k_at] = both[:, :LANES].astype(piece_refs[s].dtype)
            piece_refs[s][:, v_at] = both[:, LANES:].astype(piece_refs[s].dtype)


def merge_kernel(others, mine_ref, dk_ref, dv_ref, own_ref, *refs):
    got = refs[:others]
    cos_ref, sin_ref, dk_out, dv_out = refs[others:]
    width = dk_ref.shape[1]
    cosine, sine = cos_ref[...], sin_ref[...]

    def write(dk, dv):
        for at in range(0, width, LANES):
            part = dk[:, at : at + LANES]
            dk_out[:, at : at + LANES] = (part * cosine - half_swap(part) * sine).astype(BF16)
        dv_out[...] = dv.astype(BF16)

    mine = pl.program_id(0) == mine_ref[0]

    @pl.when(mine)
    def _():
        extra = own_ref[...]
        for ref in got:
            extra = extra + ref[...].astype(F32)
        write(dk_ref[...] + extra[:, :width], dv_ref[...] + extra[:, width:])

    @pl.when(jnp.logical_not(mine))
    def _():
        write(dk_ref[...], dv_ref[...])


def merge_keys(mine, dkey, dvalue, own, got, cosine, sine):
    rows, width = dkey.shape
    row = lambda i, mine: (i, 0)
    full = lambda i, mine: (0, 0)
    return pl.pallas_call(
        functools.partial(merge_kernel, len(got)),
        grid_spec=pltpu.PrefetchScalarGridSpec(
            num_scalar_prefetch=1,
            grid=(rows // CLEN,),
            in_specs=[pl.BlockSpec((CLEN, width), row)] * 2
            + [pl.BlockSpec((CLEN, 2 * width), full)] * (1 + len(got))
            + [pl.BlockSpec((CLEN, LANES), row)] * 2,
            out_specs=[pl.BlockSpec((CLEN, width), row)] * 2,
        ),
        out_shape=[jax.ShapeDtypeStruct((rows, width), BF16)] * 2,
        compiler_params=pltpu.CompilerParams(vmem_limit_bytes=VMEM_LIMIT),
        cost_estimate=cost(8 * rows * width, 16 * rows * width, 0),
        name="merge_keys",
    )(mine, dkey, dvalue, own, *got, cosine, sine)


def attention_specs(pieces, key_pairs):
    own = pl.BlockSpec((CLEN, LANES), lambda h, j, order, rank: (order[j], h))
    own_value = pl.BlockSpec((CLEN, LANES), lambda h, j, order, rank: (order[j], key_pairs + h))
    key = pl.BlockSpec((CLEN, LANES), lambda h, j, order, rank: (0, h))
    value = pl.BlockSpec((CLEN, LANES), lambda h, j, order, rank: (0, key_pairs + h))
    trig = pl.BlockSpec((CLEN, LANES), lambda h, j, order, rank: (order[j], 0))
    prompt = pl.BlockSpec((CLEN, 2 * key_pairs * LANES), lambda h, j, order, rank: (0, 0))
    return own, own_value, key, value, trig, prompt


def attention_forward(order, rank, query, kv, prompts):
    rows, width = query.shape
    pieces, pairs = len(prompts), width // LANES
    own, own_value, key, value, _, _ = attention_specs(pieces, pairs)
    scores = rows * (pieces + 1) * CLEN * (width // HEAD_DIM)
    return pl.pallas_call(
        functools.partial(forward_kernel, pieces),
        grid_spec=pltpu.PrefetchScalarGridSpec(
            num_scalar_prefetch=2,
            grid=(pairs, rows // CLEN),
            in_specs=[own, own, own_value] + [key] * pieces + [value] * pieces,
            out_specs=[own, own],
        ),
        out_shape=[jax.ShapeDtypeStruct((rows, width), BF16), jax.ShapeDtypeStruct((rows, width), F32)],
        compiler_params=pltpu.CompilerParams(vmem_limit_bytes=VMEM_LIMIT),
        cost_estimate=cost(
            16 * scores * HEAD_DIM, 16 * rows * width, scores
        ),
        name="attend",
    )(order, rank, query, kv, kv, *prompts, *prompts)


def attention_backward(order, rank, query, kv, mixed, lse, dmixed, cosine, sine, prompts):
    rows, width = query.shape
    pieces, pairs = len(prompts), width // LANES
    own, own_value, key, value, trig, prompt = attention_specs(pieces, pairs)
    scores = rows * (pieces + 1) * CLEN * (width // HEAD_DIM)
    return pl.pallas_call(
        functools.partial(backward_kernel, pieces),
        grid_spec=pltpu.PrefetchScalarGridSpec(
            num_scalar_prefetch=2,
            grid=(pairs, rows // CLEN),
            in_specs=[own, own, own_value, own, own, own] + [trig] * 2 + [key] * pieces + [value] * pieces,
            out_specs=[own, own, own] + [prompt] * pieces,
            scratch_shapes=[pltpu.VMEM((pieces * CLEN, 2 * LANES), F32)],
        ),
        out_shape=[
            jax.ShapeDtypeStruct((rows, width), BF16),
            jax.ShapeDtypeStruct((rows, width), F32),
            jax.ShapeDtypeStruct((rows, width), F32),
        ]
        + [jax.ShapeDtypeStruct((CLEN, 2 * width), BF16 if s else F32) for s in range(pieces)],
        compiler_params=pltpu.CompilerParams(vmem_limit_bytes=VMEM_LIMIT),
        cost_estimate=cost(
            40 * scores * HEAD_DIM, 32 * rows * width, scores
        ),
        name="attend_back",
    )(order, rank, query, kv, kv, mixed, lse, dmixed, cosine, sine, *prompts, *prompts)


def normalize(values):
    factor = lax.rsqrt(jnp.mean(values * values, axis=-1, keepdims=True) + EPS)
    return (values * factor, factor)


def rope_tables(where):
    half = HEAD_DIM // 2
    freqs = ROPE_BASE ** (-(jnp.arange(half).astype(F32) * 2.0) / HEAD_DIM)
    angles = where.astype(F32)[:, None] * freqs[None, :]
    cosine, sine = jnp.cos(angles), jnp.sin(angles)
    return (
        jnp.concatenate([cosine] * 4, axis=1),
        jnp.concatenate([-sine, sine, -sine, sine], axis=1),
    )


def body(
    tokens,
    attn_gain,
    query_weight,
    key_weight,
    value_weight,
    out_weight,
    ffn_gain,
    gate_weight,
    up_weight,
    down_weight,
    seq_ids,
    positions,
    out_grad,
):
    rows, width = tokens.shape
    head_width = query_weight.shape[1]
    own_rows, ffn_width = gate_weight.shape
    half_units = ffn_width // 2
    chunk = half_units // FFN_CHUNKS
    half = rows // 2
    dp_count = lax.axis_size("dp")
    ctx_count = lax.axis_size("hi") * 2
    tp_count = lax.axis_size("tp")
    dp_index = lax.axis_index("dp")
    parity = lax.axis_index("lo")
    ctx_index = lax.axis_index("hi") * 2 + parity
    tp_index = lax.axis_index("tp")
    bit = tp_index & 1
    bit_ref = bit.astype(jnp.int32)[None]

    def row_half(values, which=bit):
        return lax.dynamic_slice_in_dim(values, which * half, half)

    def assemble(mine, other):
        first = jnp.where(bit == 0, mine, other)
        last = jnp.where(bit == 0, other, mine)
        return jnp.concatenate([first, last], axis=0)

    slots = jnp.arange(dp_count * ctx_count, dtype=jnp.int32)

    def places_of(order_k):
        slot_k = jnp.array(order_k, jnp.int32)[slots % ctx_count]
        return (
            lax.rem(dp_index + slots // ctx_count, dp_count) * ctx_count + (ctx_index ^ slot_k)
        ).astype(jnp.int32)

    def slots_of(order_k):
        slot_of = jnp.array([order_k.index(k) for k in range(ctx_count)], jnp.int32)
        return slot_of[ctx_index ^ jnp.arange(ctx_count, dtype=jnp.int32)]

    attn_order, ffn_order = (0, 2, 1, 3), (0, 1, 2, 3)
    places, places_ffn = places_of(attn_order), places_of(ffn_order)
    slots_attn, slots_ffn = slots_of(attn_order), slots_of(ffn_order)
    owners = lax.rem(dp_index + jnp.arange(dp_count, dtype=jnp.int32), dp_count).astype(jnp.int32)
    near_rows = width // dp_count

    def over_dp(blocks):
        return blocks + [turn(x, "dp", -s) for s in range(1, dp_count) for x in blocks]

    kv_weight = jnp.concatenate([key_weight, value_weight], axis=1)
    kv_one, kv_two = swap(kv_weight, "lo"), swap(kv_weight, "hi")
    kv_three = swap(kv_two, "lo")
    kv_stack = over_dp([kv_weight, kv_two, kv_one, kv_three])
    qo_weight = after(jnp.concatenate([query_weight, out_weight], axis=1), kv_three)
    qo_two = swap(qo_weight, "hi")
    qo_even = jnp.concatenate([qo_weight, qo_two], axis=0)
    qo_odd = swap(qo_even, "lo")
    qo_stack = over_dp([qo_even, qo_odd])

    def ffn_columns(f, which):
        first = which * half_units + f * chunk
        return jnp.concatenate(
            [
                lax.dynamic_slice_in_dim(w, first, chunk, 1)
                for w in (gate_weight, up_weight, down_weight)
            ],
            axis=1,
        )

    def ffn_sends(f, *needed):
        keep, give = after((ffn_columns(f, parity), ffn_columns(f, 1 - parity)), *needed)
        near = jnp.concatenate([keep, swap(give, "lo")], axis=0)
        return near, swap(keep, "hi"), give

    def ffn_stack(near_blocks, far_blocks):
        return place_rows([x for both in zip(near_blocks, far_blocks) for x in both], places_ffn)

    def gather_dp(own):
        return [own] + [turn(own, "dp", -s) for s in range(1, dp_count)]

    group_seq = seq_ids[0].reshape(ctx_count, rows // CLEN, CLEN)[:, :, 0]
    group_pos = positions[0].reshape(ctx_count, rows // CLEN, CLEN)[:, :, 0]
    prompt_at = jnp.argmax(group_seq == 0, axis=1).astype(jnp.int32)
    prompt_rank = jnp.sum(jnp.where(group_seq == 0, group_pos, 0), axis=1).astype(jnp.int32)
    rank = prompt_rank[ctx_index ^ jnp.arange(ctx_count, dtype=jnp.int32)]
    mine = prompt_at[ctx_index]
    pieces = jnp.arange(rows // CLEN, dtype=jnp.int32)
    order = jnp.where(pieces == 0, mine, jnp.where(pieces <= mine, pieces - 1, pieces))
    own_pos = lax.dynamic_slice_in_dim(positions[0], ctx_index * rows, rows)
    cosine, sine = rope_tables(own_pos)

    gain_one = attn_gain[None].astype(F32)
    gain_two = ffn_gain[None].astype(F32)
    first_norm, first_scale = normalize(tokens.astype(F32))
    first = low(first_norm * gain_one)

    kv = project(
        [after(first, qo_two)], kv_stack, places, bit_ref, 0, 2 * head_width, cosine, sine, head_width
    )
    prompt_own = lax.dynamic_slice_in_dim(kv, mine * CLEN, CLEN)
    prompts = [prompt_own] + [swap(prompt_own, CTX, k) for k in range(1, ctx_count)]
    near_one, two_one, give_one = ffn_sends(0, kv_three)
    query = project(
        [after(first, two_one, near_one)],
        qo_stack,
        places,
        bit_ref,
        0,
        head_width,
        cosine,
        sine,
        head_width,
    )
    near_one = gather_dp(near_one)
    cotangent_half = row_half(out_grad)
    cotangent_far = swap(after(cotangent_half, *prompts[1:]), "lo")
    three_one = swap(after(give_one, kv_stack[-1]), CTX, 3)
    query = after(query, *near_one[1:], three_one)
    mixed, lse = attention_forward(order, rank, query, kv, prompts)
    near_two, two_two, give_two = ffn_sends(1, *prompts[1:])
    near_two = gather_dp(after(near_two, two_one, *qo_stack[2:]))
    mixed = after(mixed, two_two, *near_two[1:])
    three_two = swap(after(give_two, three_one), CTX, 3)
    far_one_blocks = gather_dp(jnp.concatenate([two_one, three_one], axis=0))
    far_two_blocks = gather_dp(jnp.concatenate([two_two, three_two], axis=0))
    ffn_weights = [ffn_stack(near_one, far_one_blocks), ffn_stack(near_two, far_two_blocks)]

    kept, given = project_back(
        [mixed], ((0, head_width),), [qo_stack], places, bit_ref
    )
    mixed_out = low(add(kept, after(swap(given, "tp"), three_two)))
    mixed_far = after(
        swap(mixed_out, "tp", 2), ffn_weights[0], cotangent_far
    )
    middle = row_half(tokens).astype(F32) + add(mixed_out, mixed_far)
    second_norm, second_scale = normalize(middle)
    second_half = low(second_norm * gain_two)

    cotangents = [
        [cotangent_half, row_half(out_grad, 1 - bit)],
        [cotangent_far, swap(cotangent_far, "tp")],
    ]
    second_far = swap(second_half, "lo")
    near = [second_half, after(swap(second_half, "tp"), *far_two_blocks[1:])]
    made = [[ffn(near, cotangents[0], [w]) for w in ffn_weights]]
    gate_spans = tuple((f, 0, f, 0, 2 * chunk) for f in range(FFN_CHUNKS))
    down_spans = tuple((f, 0, f, 2 * chunk, chunk) for f in range(FFN_CHUNKS))
    dsecond_near = ffn_back([m[1] for m in made[0]], ffn_weights, gate_spans)
    second_far = after(second_far, *dsecond_near)
    far = [second_far, swap(second_far, "tp")]
    made.append([ffn(far, cotangents[1], [w]) for w in ffn_weights])
    seconds = [near, far]
    hiddens = [[m[0] for m in side] for side in made]
    dpairs = [[m[1] for m in side] for side in made]

    def cores(part):
        return low(add(part[0], swap(part[1], "tp")))

    dsecond_far = ffn_back(dpairs[1], ffn_weights, gate_spans)
    dsecond_got, dsecond_half = swap(cores(dsecond_far), "lo"), cores(dsecond_near)

    lefts, left_cots = after(
        (seconds[0] + seconds[1], cotangents[0] + cotangents[1]), *dsecond_near, *dsecond_far
    )
    ffn_given, ffn_own = [], []
    for f in range(FFN_CHUNKS):

        def part(s, f=f):
            return ffn_grads(
                lefts,
                left_cots,
                [side[f] for side in hiddens],
                [side[f] for side in dpairs],
                owners,
                slots_ffn,
                s,
                near_rows,
                own_rows,
            )

        ffn_given.append([part(s) for s in range(1, dp_count)])
        ffn_own.append(part(0))
    pair_rows = 2 * own_rows

    def over_dp_rows(f, first, *needed):
        return [
            turn(after(x[first : first + pair_rows], *needed), "dp", s + 1)
            for s, x in enumerate(ffn_given[f])
        ]

    def total_rows(f, first, got):
        total = ffn_own[f][first : first + pair_rows]
        for x in got:
            total = add(total, x)
        return low(total)

    far_one = over_dp_rows(0, pair_rows)
    near_one_got = over_dp_rows(0, 0, *far_one)
    far_two = over_dp_rows(1, pair_rows, *near_one_got)
    near_two_got = over_dp_rows(1, 0, *near_one_got)
    dsecond_got = after(dsecond_got, *ffn_given[1], ffn_own[0], *far_one)
    dsecond = low(add(dsecond_half, dsecond_got))
    hi_one = swap(total_rows(0, pair_rows, far_one), "hi")
    hiddens_late = after(hiddens, dsecond)
    out_far = ffn_back(hiddens_late[1], ffn_weights, down_spans)
    out_near = ffn_back(hiddens_late[0], ffn_weights, down_spans)

    def ffn_deliver(near, hi_got, needed):
        pair = add(near, hi_got)
        kept = pair[:own_rows]
        got = after(swap(low(pair[own_rows:]), "lo"), needed).astype(F32)
        return (jnp.where(parity == 0, kept, got), jnp.where(parity == 0, got, kept))

    dsecond = add(dsecond, after(
        swap(dsecond, "tp", 2), *ffn_own, *out_far, *out_near, *near_one_got
    ))
    gain_two_grad = jnp.sum(dsecond * second_norm, axis=0)
    scaled_two = dsecond * gain_two
    dmiddle = cotangent_half.astype(F32) + second_scale * (
        scaled_two - second_norm * jnp.mean(scaled_two * second_norm, axis=-1, keepdims=True)
    )
    out_half, out_far_got = cores(out_near), swap(cores(out_far), "lo")
    dmiddle_low = [low(dmiddle), after(swap(low(dmiddle), "tp"), out_half)]
    dmixed = project(dmiddle_low, qo_stack, places, bit_ref, head_width, head_width, cosine, sine, 0)
    dquery_low, dkey_own, dvalue_own, dprompt_own, *dprompts = attention_backward(
        order, rank, query, kv, mixed, lse, dmixed, cosine, sine, prompts
    )
    got = [swap(piece, CTX, k + 1) for k, piece in enumerate(dprompts)]
    far_two = after(far_two, dquery_low)
    hi_two = swap(total_rows(1, pair_rows, far_two), "hi")
    dkey_low, dvalue_low = merge_keys(
        mine[None], dkey_own, dvalue_own, dprompt_own, got, cosine, sine
    )

    def attn_grads(pairs):
        parts = [
            attn_grads_block(pairs, bit_ref, owners, slots_attn, s, near_rows, own_rows)
            for s in range(dp_count)
        ]
        total = parts[0]
        for s in range(1, dp_count):
            total = add(total, turn(parts[s], "dp", s))
        total = low(total)
        pair = add(total[: 2 * own_rows], swap(total[2 * own_rows :], "lo"))
        return total, pair[:own_rows] + swap(low(pair[own_rows:]), "hi").astype(F32)

    _, early = attn_grads([(dmiddle_low, mixed), ([first], dquery_low)])
    late_total, late = attn_grads([([first], dkey_low), ([first], dvalue_low)])
    ffn_sums = [
        ffn_deliver(total_rows(0, 0, near_one_got), after(hi_one, dquery_low), dkey_low),
        ffn_deliver(
            total_rows(1, 0, after(near_two_got, dquery_low)),
            after(hi_two, late_total),
            late_total,
        ),
    ]

    kept, given = project_back(
        [dquery_low, dkey_low, dvalue_low],
        ((0, 0), (1, 0), (1, head_width)),
        [qo_stack, kv_stack],
        places,
        bit_ref,
    )
    norm_half, norm_other = row_half(first_norm), row_half(first_norm, 1 - bit)
    gain_one_grad = jnp.sum(kept.astype(F32) * norm_half, axis=0) + jnp.sum(
        given.astype(F32) * norm_other, axis=0
    )
    dfirst = after(low(add(kept, swap(given, "tp"))), gain_one_grad)
    dfirst = add(dfirst, swap(dfirst, "tp", 2))
    scaled_one = dfirst * gain_one
    dinputs = dmiddle + row_half(first_scale) * (
        scaled_one - norm_half * jnp.mean(scaled_one * norm_half, axis=-1, keepdims=True)
    )

    share = width // tp_count
    here = tp_index // 2
    gains = jnp.stack([gain_one_grad, jnp.where(here == 0, gain_two_grad, 0.0)])
    for axis in ("tp", "lo", "hi", "dp"):
        mask = 1
        while mask < lax.axis_size(axis):
            gains = gains + swap(gains, axis, mask)
            mask *= 2

    def wide_part(values, which):
        return lax.dynamic_slice_in_dim(values, which * 2 * share, 2 * share, 1)

    def deliver(wide):
        kept = lax.dynamic_slice_in_dim(wide, bit * share, share, 1)
        given = lax.dynamic_slice_in_dim(wide, (1 - bit) * share, share, 1)
        return assemble(kept, swap(given, "tp"))

    in_grad = deliver(after(low(wide_part(dinputs, here)), gains))

    ffn_out = low(add(out_half, after(out_far_got, dquery_low)))
    ffn_out = add(wide_part(ffn_out, here), swap(wide_part(ffn_out, 1 - here), "tp", 2))
    block_out = deliver(low(wide_part(middle, here) + ffn_out))

    part = width // (dp_count * ctx_count)
    gains = lax.dynamic_slice_in_dim(gains, (dp_index * ctx_count + ctx_index) * part, part, 1)

    ffn_final = [
        jnp.concatenate(
            [
                ffn_sums[f][side][:, i * chunk : (i + 1) * chunk]
                for side in range(2)
                for f in range(FFN_CHUNKS)
            ],
            axis=1,
        )
        for i in range(3)
    ]
    return (
        block_out,
        in_grad,
        gains[0],
        early[:, head_width:],
        late[:, :head_width],
        late[:, head_width:],
        early[:, :head_width],
        gains[1],
        ffn_final[0],
        ffn_final[1],
        ffn_final[2],
    )


def solution(mesh):
    dp, ctx, tp = (mesh.shape[name] for name in ("dp", "ctx", "tp"))
    split_mesh = Mesh(mesh.devices.reshape(dp, ctx // 2, 2, tp), ("dp", "hi", "lo", "tp"))
    every = ("dp",) + CTX
    split = P(every, "tp")
    rows = P(every, None)
    vector = P(every)
    return jax.shard_map(
        body,
        mesh=split_mesh,
        in_specs=(rows, P(), split, split, split, split, P(), split, split, split)
        + (P("dp", None), P("dp", None), rows),
        out_specs=(split, split, vector, split, split, split, split, vector, split, split, split),
        check_vma=False,
    )
```
